32 devices in a mesh: dp: 8 (over z, core), seq: 4 (over y, x).
Axes of the slice: x: 2, y: 2, z: 4, core: 2. Of those that a mesh axis runs over, the one named last changes fastest.
Arguments:
- tokens: bfloat16 [4096, 2048], P(('dp', 'seq')), may hold values from -6 to 6
- lengths: int32 [8, 1], P('dp'), may hold values from 512 to 512, as said below
- cotangent: bfloat16 [4096, 2048], P(('dp', 'seq')), may hold values from -6 to 6
- attn_norm_gain: bfloat16 [2048], replicated, may hold values from 0.25 to 1.75
- w_query: bfloat16 [2048, 2048], P('dp', 'seq'), may hold values from -0.125 to 0.125
- w_key: bfloat16 [2048, 2048], P('dp', 'seq'), may hold values from -0.125 to 0.125
- w_value: bfloat16 [2048, 2048], P('dp', 'seq'), may hold values from -0.125 to 0.125
- w_strength: bfloat16 [2048, 16], P('dp', 'seq'), may hold values from -0.125 to 0.125
- conv_weight: bfloat16 [3, 4, 2048], P(None, None, 'seq'), may hold values from -3 to 3
- head_gain: bfloat16 [128], replicated, may hold values from 0.25 to 1.75
- w_output: bfloat16 [2048, 2048], P('seq', 'dp'), may hold values from -0.125 to 0.125
- ffn_norm_gain: bfloat16 [2048], replicated, may hold values from 0.25 to 1.75
- w_gate: bfloat16 [2048, 5632], P('dp', 'seq'), may hold values from -0.125 to 0.125
- w_up: bfloat16 [2048, 5632], P('dp', 'seq'), may hold values from -0.125 to 0.125
- w_down: bfloat16 [5632, 2048], P('seq', 'dp'), may hold values from -0.15625 to 0.15625
Outputs:
- output: bfloat16 [4096, 2048], P(('dp', 'seq'))
- input_grad: float32 [4096, 2048], P(('dp', 'seq'))
- grad_attn_norm_gain: float32 [2048], replicated
- grad_w_query: float32 [2048, 2048], P('dp', 'seq')
- grad_w_key: float32 [2048, 2048], P('dp', 'seq')
- grad_w_value: float32 [2048, 2048], P('dp', 'seq')
- grad_w_strength: float32 [2048, 16], P('dp', 'seq')
- grad_conv_weight: float32 [3, 4, 2048], P(None, None, 'seq')
- grad_head_gain: float32 [128], replicated
- grad_w_output: float32 [2048, 2048], P('seq', 'dp')
- grad_ffn_norm_gain: float32 [2048], replicated
- grad_w_gate: float32 [2048, 5632], P('dp', 'seq')
- grad_w_up: float32 [2048, 5632], P('dp', 'seq')
- grad_w_down: float32 [5632, 2048], P('seq', 'dp')
The draws below stay inside these ranges and needn't reach their ends.
Inputs may be any that keep to these rules, and one draw needn't show every extreme that they name: Each length is a multiple of 64. In each group the lengths sum to 512 or less, the rest of the group's slots being padding; in every draw some group has no padding and holds a sequence of the greatest length, and some group has every sequence at the least length.
All inputs are finite; a program needn't handle non-finite values.
Results may differ from the reference program's by a relative error of at most 0.035.
Values may be sent and summed in bfloat16 or wider, within the bound.
No kernel may reach another device: no remote copies, remote signals or barrier semaphores. Data moves between devices by JAX's collectives and lax.ppermute only.
A program may use at most 128 MiB of HBM per device.

```python
import jax
import jax.numpy as jnp
from jax import lax

D = 2048
H = 16
DH = 128
FF = 5632
CONV = 4
SPAN = 64
GROUPS = 8
GROUP_TOK = 512
TOKENS = 4096
SEQ_MIN = 512
SLOTS = 1


def draw_lengths(key, part):
    blocks = GROUP_TOK // SPAN
    least = SEQ_MIN // SPAN
    spare = blocks - SLOTS * least
    first, second, third = jax.random.split(key, 3)
    targets = jax.random.randint(first, (GROUPS, spare), 0, SLOTS + 1)
    filled = jax.random.randint(second, (), 0, GROUPS)
    chosen = jax.random.randint(third, (), 0, SLOTS)
    shortest = (filled + 1) % GROUPS
    group_ids = jnp.arange(GROUPS)[:, None]
    targets = jnp.where(group_ids == filled, chosen, targets)
    targets = jnp.where(group_ids == shortest, SLOTS, targets)
    counts = jnp.sum((targets[:, :, None] == jnp.arange(SLOTS)[None, None, :]).astype(jnp.int32), axis=1)
    return ((least + counts) * SPAN).astype(jnp.int32)


def block_levels(stream_key, extent, cuts, low, high):
    level, own = 1.0, jax.random.fold_in(stream_key, 6)
    for axis_at, parts in cuts:
        draws = jnp.exp(jax.random.uniform(jax.random.fold_in(own, axis_at), (parts,), jnp.float32, low / len(cuts), high / len(cuts)))
        level = level * jnp.repeat(draws, extent[axis_at] // parts).reshape([-1 if axis == axis_at else 1 for axis in range(len(extent))])
    return level


def noise(key, shape, spread, limit, cuts=(), held_as=jnp.bfloat16):
    drawn = jax.random.normal(key, shape, jnp.float32) * spread
    if len(cuts) > 0:
        drawn = block_levels(key, shape, cuts, -0.22, 0.18) * drawn
    return jnp.clip(drawn, min=-limit, max=limit).astype(held_as)


def setup_inputs(seed: int = 0) -> dict:
    arg_keys = jax.random.split(jax.random.key(seed), 16)
    tokens = noise(arg_keys[0], (TOKENS, D), 1.0, 6.0, ((0, 32),))
    lengths = draw_lengths(jax.random.fold_in(arg_keys[15], 71), 0)
    cotangent = noise(arg_keys[2], (TOKENS, D), 1.0, 6.0, ((0, 32),))
    attn_norm_gain = jnp.clip(1.0 + 0.15 * jax.random.normal(arg_keys[3], (D,), jnp.float32), 0.25, 1.75).astype(jnp.bfloat16)
    w_query = noise(arg_keys[4], (D, D), D ** -0.5, 0.125, ((0, 8), (1, 4)))
    w_key = noise(arg_keys[5], (D, D), D ** -0.5, 0.125, ((0, 8), (1, 4)))
    w_value = noise(arg_keys[6], (D, D), D ** -0.5, 0.125, ((0, 8), (1, 4)))
    w_strength = noise(arg_keys[7], (D, H), D ** -0.5, 0.125, ((0, 8), (1, 4)))
    conv_weight = noise(arg_keys[8], (3, CONV, D), CONV ** -0.5, 3.0, ((2, 4),))
    head_gain = jnp.clip(1.0 + 0.15 * jax.random.normal(arg_keys[9], (DH,), jnp.float32), 0.25, 1.75).astype(jnp.bfloat16)
    w_output = noise(arg_keys[10], (D, D), D ** -0.5, 0.125, ((0, 4), (1, 8)))
    ffn_norm_gain = jnp.clip(1.0 + 0.15 * jax.random.normal(arg_keys[11], (D,), jnp.float32), 0.25, 1.75).astype(jnp.bfloat16)
    w_gate = noise(arg_keys[12], (D, FF), D ** -0.5, 0.125, ((0, 8), (1, 4)))
    w_up = noise(arg_keys[13], (D, FF), D ** -0.5, 0.125, ((0, 8), (1, 4)))
    w_down = noise(arg_keys[14], (FF, D), (FF // 4) ** -0.5, 0.15625, ((0, 4), (1, 8)))
    return {"tokens": tokens, "lengths": lengths, "cotangent": cotangent, "attn_norm_gain": attn_norm_gain, "w_query": w_query, "w_key": w_key, "w_value": w_value, "w_strength": w_strength, "conv_weight": conv_weight, "head_gain": head_gain, "w_output": w_output, "ffn_norm_gain": ffn_norm_gain, "w_gate": w_gate, "w_up": w_up, "w_down": w_down}


epsilon = 1e-06
highest = lax.Precision.HIGHEST

@jax.custom_vjp
def low(v):
    return lax.optimization_barrier(v.astype(jnp.bfloat16)).astype(jnp.float32)

@jax.custom_vjp
def low_back(v):
    return v

def low_keep(v):
    return (low(v), None)

def low_pass(kept, grad):
    return (grad,)

def back_keep(v):
    return (v, None)

def back_low(kept, grad):
    return (low(grad),)
low.defvjp(low_keep, low_pass)
low_back.defvjp(back_keep, back_low)

def send(value):
    return low(low_back(value))

def rms_scale(value, gain):
    return value * lax.rsqrt(lax.optimization_barrier(jnp.mean(value * value, axis=-1, keepdims=True)) + epsilon) * gain

def segment_tables(lengths_row, group_tok):
    lengths_row = lengths_row.astype(jnp.int32)
    offsets = (jnp.cumsum(lengths_row) - lengths_row).astype(jnp.int32)
    total = jnp.sum(lengths_row).astype(jnp.int32)
    starts = jnp.concatenate([offsets, total[None]]).astype(jnp.int32)
    places = jnp.arange(group_tok, dtype=jnp.int32)
    seg_start = lax.optimization_barrier(jnp.max(jnp.where(starts[None, :] <= places[:, None], starts[None, :], 0), axis=1)).astype(jnp.int32)
    valid = jnp.stack([places - lag >= seg_start for lag in range(CONV)]).astype(jnp.float32)
    block_first = jnp.arange(group_tok // SPAN, dtype=jnp.int32) * SPAN
    reset = jnp.any(block_first[:, None] == starts[None, :], axis=1).astype(jnp.float32)
    live = (places < total).astype(jnp.float32)
    return (valid, reset, live)

def short_conv(values, weight, valid):
    total = weight[0] * values
    for lag in range(1, CONV):
        moved = jnp.concatenate([jnp.zeros((lag, values.shape[1]), jnp.float32), values[:-lag]], axis=0)
        total = total + weight[lag] * moved * valid[lag][:, None]
    return jax.nn.silu(total)

def unit_rows(values, heads):
    shaped = values.reshape(values.shape[0], heads, DH)
    return shaped * lax.rsqrt(lax.optimization_barrier(jnp.sum(shaped * shaped, axis=-1, keepdims=True)) + epsilon)

def delta_block(state, pieces):
    query, key, value, strength, restart = pieces
    state = state * (1.0 - restart)
    inner = jnp.einsum('hid,hjd->hij', key, key, precision=highest)
    lower = jnp.tril(inner * strength[:, :, None], -1)
    system = jnp.eye(SPAN, dtype=jnp.float32)[None] + lower
    right = jnp.concatenate([strength[:, :, None] * key, strength[:, :, None] * value], axis=-1)
    solved = jax.scipy.linalg.solve_triangular(system, right, lower=True, unit_diagonal=True)
    wide = solved[..., :DH]
    plain = solved[..., DH:]
    fresh = plain - jnp.einsum('hcd,hde->hce', wide, state, precision=highest)
    scores = jnp.tril(jnp.einsum('hid,hjd->hij', query, key, precision=highest))
    output = jnp.einsum('hcd,hde->hce', query, state, precision=highest) + jnp.einsum('hij,hje->hie', scores, fresh, precision=highest)
    state = state + jnp.einsum('hcd,hce->hde', key, fresh, precision=highest)
    return (state, output)

def mixer(query, key, value, strength, conv_part, valid, reset):
    width = query.shape[1]
    heads = width // DH
    length = query.shape[0]
    query = unit_rows(short_conv(query, conv_part[0], valid), heads)
    key = unit_rows(short_conv(key, conv_part[1], valid), heads)
    value = short_conv(value, conv_part[2], valid).reshape(length, heads, DH)
    blocks = length // SPAN

    def blockify(values):
        return values.reshape(blocks, SPAN, heads, DH).transpose(0, 2, 1, 3)
    gates = strength.reshape(blocks, SPAN, heads).transpose(0, 2, 1)
    initial = jnp.zeros((heads, DH, DH), jnp.float32)
    final_state, outputs = lax.scan(jax.checkpoint(delta_block), initial, (blockify(query), blockify(key), blockify(value), gates, reset))
    return outputs.transpose(0, 2, 1, 3).reshape(length, width)

def layer(x_rows, params, valid, reset):
    gain_one, w_query, w_key, w_value, w_strength, conv_weight, head_gain, w_output, gain_two, w_gate, w_up, w_down = params
    length = x_rows.shape[0]
    hidden = low(rms_scale(x_rows, gain_one))
    query = send(jnp.dot(hidden, w_query, precision=highest))
    key = send(jnp.dot(hidden, w_key, precision=highest))
    value = send(jnp.dot(hidden, w_value, precision=highest))
    logit = low_back(jnp.dot(hidden, w_strength, precision=highest))
    strength = send(jax.nn.sigmoid(logit))
    mixed = send(mixer(query, key, value, strength, conv_weight, valid, reset))
    normed = low(rms_scale(mixed.reshape(length, H, DH), head_gain).reshape(length, D))
    resid = x_rows + low_back(jnp.dot(normed, w_output, precision=highest))
    second = low(rms_scale(resid, gain_two))
    gate = low_back(jnp.dot(second, w_gate, precision=highest))
    upper = low_back(jnp.dot(second, w_up, precision=highest))
    act = low(jax.nn.silu(gate) * upper)
    return resid + low_back(jnp.dot(act, w_down, precision=highest))

def add_pair(first, second):
    return first + second

def reference(tokens, lengths, cotangent, attn_norm_gain, w_query, w_key, w_value, w_strength, conv_weight, head_gain, w_output, ffn_norm_gain, w_gate, w_up, w_down):
    weights = tuple((item.astype(jnp.float32) for item in (attn_norm_gain, w_query, w_key, w_value, w_strength, conv_weight, head_gain, w_output, ffn_norm_gain, w_gate, w_up, w_down)))
    grouped_x = tokens.reshape(GROUPS, GROUP_TOK, D)
    grouped_c = cotangent.reshape(GROUPS, GROUP_TOK, D)

    def one_group(totals, items):
        rows_x, rows_c, row_len = items
        valid, reset, live = segment_tables(row_len, GROUP_TOK)

        def forward(x_rows, params):
            return layer(x_rows, params, valid, reset)
        result, pullback = jax.vjp(forward, rows_x.astype(jnp.float32), weights)
        out_rows = (result * live[:, None]).astype(jnp.bfloat16)
        x_grad, w_grads = pullback(rows_c.astype(jnp.float32) * live[:, None])
        totals = jax.tree.map(add_pair, totals, w_grads)
        return (totals, (out_rows, x_grad))
    zeros = jax.tree.map(jnp.zeros_like, weights)
    totals, (out_rows, x_grads) = lax.scan(one_group, zeros, (grouped_x, grouped_c, lengths))
    return (out_rows.reshape(TOKENS, D), x_grads.reshape(TOKENS, D), totals[0], totals[1], totals[2], totals[3], totals[4], totals[5], totals[6], totals[7], totals[8], totals[9], totals[10], totals[11])
```

```python
import functools

import jax
import jax.numpy as jnp
from jax import lax
from jax.experimental import pallas as pl
from jax.experimental.pallas import tpu as pltpu
from jax.sharding import PartitionSpec as P

DH = 128
CONV = 4
SPAN = 64
HALO = 8
epsilon = 1e-06
f32 = jnp.float32
bf16 = jnp.bfloat16

NN = (((1,), (0,)), ((), ()))
NT = (((1,), (1,)), ((), ()))
TN = (((0,), (0,)), ((), ()))


def mm(left, right, dims=NN):
    return lax.dot_general(left.astype(bf16), right.astype(bf16), dims, preferred_element_type=f32)


def mm3(left, right, dims=NN):
    lh = left.astype(bf16)
    ll = (left - lh.astype(f32)).astype(bf16)
    rh = right.astype(bf16)
    rl = (right - rh.astype(f32)).astype(bf16)
    out = lax.dot_general(ll, rh, dims, preferred_element_type=f32)
    out = out + lax.dot_general(lh, rl, dims, preferred_element_type=f32)
    return out + lax.dot_general(lh, rh, dims, preferred_element_type=f32)


def tri_masks(rows):
    r = lax.broadcasted_iota(jnp.int32, (rows, rows), 0)
    c = lax.broadcasted_iota(jnp.int32, (rows, rows), 1)
    same = (r // SPAN) == (c // SPAN)
    return r, c, same


def unit_lower_inverse(lower, r, c):
    eye = (r == c).astype(f32)
    half = 1
    inverse = eye
    while half < SPAN:
        pair = ((r // (2 * half)) == (c // (2 * half))) & ((r // half) != (c // half))
        corner = jnp.where(pair, lower, 0.0)
        if half == 1:
            inverse = eye - corner
        else:
            inverse = inverse - mm(mm(inverse, corner), inverse)
        half *= 2
    resid = eye - inverse - mm3(lower, inverse)
    return inverse + mm(inverse, resid)


def rolled(block, halo_before, lag):
    if lag == 0:
        return block
    whole = jnp.concatenate([halo_before, block], axis=0)
    return pltpu.roll(whole, lag, 0)[HALO:]


def rolled_back(block, halo_after, lag):
    if lag == 0:
        return block
    whole = jnp.concatenate([block, halo_after], axis=0)
    return pltpu.roll(whole, whole.shape[0] - lag, 0)[: block.shape[0]]


def sigmoid(v):
    return 1.0 / (1.0 + jnp.exp(-v))


def row_start(place_ref, c, per):
    chunk = lax.div(c, per)
    return pl.multiple_of(((chunk ^ place_ref[0]) * per + lax.rem(c, per)) * SPAN, SPAN)


def conv_block(x_ref, conv_ref, start, before, keep, part, head, width):
    cols = pl.ds(part * width + head * DH, DH)
    block = x_ref[pl.ds(start, SPAN), cols].astype(f32)
    halo = x_ref[pl.ds(before, 16), cols].astype(f32)[16 - HALO :] * keep
    shifted = [rolled(block, halo, lag) for lag in range(CONV)]
    taps = [conv_ref[pl.ds(part * CONV + lag, 1), pl.ds(head * DH, DH)] for lag in range(CONV)]
    total = taps[0] * shifted[0]
    for lag in range(1, CONV):
        total = total + taps[lag] * shifted[lag]
    return total, shifted, taps


def strengths(logit_ref, start, heads):
    block = sigmoid(logit_ref[pl.ds(start, SPAN), :]).astype(bf16).astype(f32)
    return jnp.concatenate([block[:, h : h + 1] for h in range(heads)], axis=0)


def fwd_kernel(per, reset_ref, place_ref, x_ref, logit_ref, conv_ref, gain_ref, normed_ref, mixed_ref, t_ref, s_ref, n_ref, q_s, k_s, u_s, w_s, p_s, state):
    length = x_ref.shape[0]
    width = x_ref.shape[1] // 3
    heads = width // DH
    blocks = length // SPAN
    rows = heads * SPAN
    r, c_, same = tri_masks(rows)
    strict = same & (r > c_)
    incl = same & (r >= c_)

    def local(c, carry):
        keep = 1.0 - reset_ref[c]
        start = row_start(place_ref, c, per)
        before = pl.multiple_of(row_start(place_ref, jnp.maximum(c - 1, 0), per) + (SPAN - 16), 16)
        parts = []
        for part in range(3):
            pieces = []
            for h in range(heads):
                z, _, _ = conv_block(x_ref, conv_ref, start, before, keep, part, h, width)
                pieces.append(z)
            z = jnp.concatenate(pieces, axis=0)
            parts.append(z * sigmoid(z))
        q, k, v = parts
        q = q * lax.rsqrt(jnp.sum(q * q, axis=-1, keepdims=True) + epsilon)
        k = k * lax.rsqrt(jnp.sum(k * k, axis=-1, keepdims=True) + epsilon)
        b = strengths(logit_ref, start, heads)
        gram = mm3(k, k, NT)
        lower = jnp.where(strict, gram * b, 0.0)
        inverse = unit_lower_inverse(lower, r, c_)
        p_s[c] = jnp.where(incl, mm(q, k, NT), 0.0).astype(bf16)
        t_ref[c] = inverse.astype(bf16)
        solved = mm(inverse, jnp.concatenate([b * k, b * v], axis=1))
        w_s[c] = solved[:, :DH].astype(bf16)
        u_s[c] = solved[:, DH:]
        q_s[c] = q.astype(bf16)
        k_s[c] = k.astype(bf16)
        return carry

    lax.fori_loop(0, blocks, local, 0)
    state[...] = jnp.zeros_like(state)
    gain = gain_ref[...]

    def scan(c, carry):
        keep = 1.0 - reset_ref[c]
        start = row_start(place_ref, c, per)
        news = []
        reads = []
        for h in range(heads):
            s = state[pl.ds(h * DH, DH), :] * keep
            low = s.astype(bf16)
            s_ref[c, pl.ds(h * DH, DH), :] = low
            both = jnp.concatenate([w_s[c, pl.ds(h * SPAN, SPAN), :], q_s[c, pl.ds(h * SPAN, SPAN), :]], axis=0)
            got = mm(both, low)
            fresh = u_s[c, pl.ds(h * SPAN, SPAN), :] - got[:SPAN]
            state[pl.ds(h * DH, DH), :] = s + mm(k_s[c, pl.ds(h * SPAN, SPAN), :], fresh, TN)
            news.append(fresh)
            reads.append(got[SPAN:])
        fresh = jnp.concatenate(news, axis=0).astype(bf16)
        n_ref[c] = fresh
        out = jnp.concatenate(reads, axis=0) + mm(p_s[c], fresh)
        mixed = out.astype(bf16)
        wide = mixed.astype(f32)
        normed = (wide * lax.rsqrt(jnp.mean(wide * wide, axis=-1, keepdims=True) + epsilon) * gain).astype(bf16)
        for h in range(heads):
            cols = pl.ds(h * DH, DH)
            mixed_ref[pl.ds(start, SPAN), cols] = mixed[h * SPAN : (h + 1) * SPAN]
            normed_ref[pl.ds(start, SPAN), cols] = normed[h * SPAN : (h + 1) * SPAN]
        return carry

    lax.fori_loop(0, blocks, scan, 0)


def delta_forward(per, reset, place, x, logit, conv, gain):
    length = x.shape[0]
    width = x.shape[1] // 3
    heads = width // DH
    blocks = length // SPAN
    rows = heads * SPAN
    shape = jax.ShapeDtypeStruct
    vmem = pl.BlockSpec(memory_space=pltpu.VMEM)
    smem = pl.BlockSpec(memory_space=pltpu.SMEM)
    return pl.pallas_call(
        functools.partial(fwd_kernel, per),
        out_shape=(
            shape((length, width), bf16),
            shape((length, width), bf16),
            shape((blocks, rows, rows), bf16),
            shape((blocks, heads * DH, DH), bf16),
            shape((blocks, rows, DH), bf16),
        ),
        in_specs=[smem, smem] + [vmem] * 4,
        out_specs=(vmem,) * 5,
        scratch_shapes=[
            pltpu.VMEM((blocks, rows, DH), bf16),
            pltpu.VMEM((blocks, rows, DH), bf16),
            pltpu.VMEM((blocks, rows, DH), f32),
            pltpu.VMEM((blocks, rows, DH), bf16),
            pltpu.VMEM((blocks, rows, rows), bf16),
            pltpu.VMEM((heads * DH, DH), f32),
        ],
        name="delta_forward",
    )(reset, place, x, logit, conv, gain)


def bwd_kernel(per, reset_ref, place_ref, x_ref, logit_ref, conv_ref, gain_ref, mixed_ref, dnorm_ref, t_ref, s_ref, n_ref, dx_ref, dlogit_ref, dconv_ref, dgain_ref,
               q_s, k_s, v_s, iq_s, ik_s, do_s, g_s, kt_s, ds_s, dstate):
    length = x_ref.shape[0]
    width = x_ref.shape[1] // 3
    heads = width // DH
    blocks = length // SPAN
    rows = heads * SPAN
    r, c_, same = tri_masks(rows)
    strict = same & (r > c_)
    incl = same & (r >= c_)
    gain = gain_ref[...]

    def stack(ref, start):
        return jnp.concatenate([ref[pl.ds(start, SPAN), pl.ds(h * DH, DH)] for h in range(heads)], axis=0)

    def local(c, total):
        keep = 1.0 - reset_ref[c]
        start = row_start(place_ref, c, per)
        before = pl.multiple_of(row_start(place_ref, jnp.maximum(c - 1, 0), per) + (SPAN - 16), 16)
        parts = []
        for part in range(3):
            pieces = []
            for h in range(heads):
                z, _, _ = conv_block(x_ref, conv_ref, start, before, keep, part, h, width)
                pieces.append(z)
            z = jnp.concatenate(pieces, axis=0)
            parts.append(z * sigmoid(z))
        q, k, v = parts
        iq = lax.rsqrt(jnp.sum(q * q, axis=-1, keepdims=True) + epsilon)
        ik = lax.rsqrt(jnp.sum(k * k, axis=-1, keepdims=True) + epsilon)
        q = q * iq
        k = k * ik
        q_s[c] = q
        k_s[c] = k
        v_s[c] = v
        iq_s[c] = jnp.broadcast_to(iq, (rows, DH))
        ik_s[c] = jnp.broadcast_to(ik, (rows, DH))
        mixed = stack(mixed_ref, start).astype(f32)
        dnorm = stack(dnorm_ref, start)
        inv = lax.rsqrt(jnp.mean(mixed * mixed, axis=-1, keepdims=True) + epsilon)
        u = mixed * inv
        total = total + jnp.sum(dnorm * u, axis=0, keepdims=True)
        dg = dnorm * gain
        do = ((dg - u * jnp.mean(dg * u, axis=-1, keepdims=True)) * inv).astype(bf16)
        do_s[c] = do
        p = jnp.where(incl, mm(q, k, NT), 0.0)
        t = t_ref[c]
        pre = mm(p, do, TN)
        got = mm(t, jnp.concatenate([pre, k], axis=1), TN)
        g_s[c] = got[:, :DH]
        kt_s[c] = got[:, DH:].astype(bf16)
        return total

    dgain_ref[...] = lax.fori_loop(0, blocks, local, jnp.zeros((1, DH), f32))
    dstate[...] = jnp.zeros_like(dstate)

    def scan(i, carry):
        c = blocks - 1 - i
        keep = 1.0 - reset_ref[c]
        start = row_start(place_ref, c, per)
        b = strengths(logit_ref, start, heads)
        k = k_s[c]
        bk = (b * k).astype(bf16)
        for h in range(heads):
            hr = pl.ds(h * SPAN, SPAN)
            ds = dstate[pl.ds(h * DH, DH), :]
            low = ds.astype(bf16)
            ds_s[c, pl.ds(h * DH, DH), :] = low
            g = g_s[c, hr, :] + mm(kt_s[c, hr, :], low)
            g_s[c, hr, :] = g
            ql = q_s[c, hr, :].astype(bf16)
            both = jnp.concatenate([ql, bk[h * SPAN : (h + 1) * SPAN]], axis=0)
            other = jnp.concatenate([do_s[c, hr, :], (-g).astype(bf16)], axis=0)
            dstate[pl.ds(h * DH, DH), :] = (ds + mm(both, other, TN)) * keep
        return carry

    lax.fori_loop(0, blocks, scan, 0)
    dconv_ref[...] = jnp.zeros_like(dconv_ref)
    lane = lax.broadcasted_iota(jnp.int32, (SPAN, heads), 1)

    def last(i, carry):
        c = blocks - 1 - i
        keep = 1.0 - reset_ref[c]
        start = row_start(place_ref, c, per)
        before = pl.multiple_of(row_start(place_ref, jnp.maximum(c - 1, 0), per) + (SPAN - 16), 16)
        b = strengths(logit_ref, start, heads)
        q, k, v = q_s[c], k_s[c], v_s[c]
        g, n, do = g_s[c], n_ref[c], do_s[c]
        gl = g.astype(bf16)
        both = jnp.concatenate([do, gl], axis=0)
        outer = mm(both, n, NT)
        dp = jnp.where(incl, outer[:rows], 0.0).astype(bf16)
        da = jnp.where(strict, -outer[rows:], 0.0).astype(bf16)
        down = mm(jnp.concatenate([dp, da], axis=0), k)
        up = mm(jnp.concatenate([dp, da], axis=0), jnp.concatenate([q, b * k], axis=0), TN)
        sides = []
        nds = []
        for h in range(heads):
            s = s_ref[c, pl.ds(h * DH, DH), :]
            hr = slice(h * SPAN, (h + 1) * SPAN)
            sides.append(mm(jnp.concatenate([do[hr], gl[hr]], axis=0), s, NT))
            nds.append(mm(n[hr], ds_s[c, pl.ds(h * DH, DH), :], NT))
        dos = jnp.concatenate([x[:SPAN] for x in sides], axis=0)
        gs = jnp.concatenate([x[SPAN:] for x in sides], axis=0)
        dq = dos + down[:rows]
        y = down[rows:] - gs
        dk = up + jnp.concatenate(nds, axis=0) + b * y
        dv = b * g
        db = jnp.sum(k * y + v * g, axis=-1, keepdims=True)
        dq = (dq - q * jnp.sum(q * dq, axis=-1, keepdims=True)) * iq_s[c]
        dk = (dk - k * jnp.sum(k * dk, axis=-1, keepdims=True)) * ik_s[c]
        row = jnp.zeros((SPAN, heads), f32)
        for h in range(heads):
            row = jnp.where(lane == h, db[h * SPAN : (h + 1) * SPAN], row)
        sg = sigmoid(logit_ref[pl.ds(start, SPAN), :])
        dlogit_ref[pl.ds(start, SPAN), :] = (row.astype(bf16).astype(f32) * sg * (1.0 - sg)).astype(bf16)
        new_carry = []
        for part, grad in enumerate((dq, dk, dv)):
            for h in range(heads):
                z, shifted, taps = conv_block(x_ref, conv_ref, start, before, keep, part, h, width)
                sz = sigmoid(z)
                dz = grad[h * SPAN : (h + 1) * SPAN] * (sz * (1.0 + z * (1.0 - sz)))
                after = carry[part * heads + h]
                total = taps[0] * dz
                for lag in range(1, CONV):
                    total = total + taps[lag] * rolled_back(dz, after, lag)
                dx_ref[pl.ds(start, SPAN), pl.ds(part * width + h * DH, DH)] = total.astype(bf16)
                for lag in range(CONV):
                    at = pl.ds(part * CONV + lag, 1), pl.ds(h * DH, DH)
                    dconv_ref[at] = dconv_ref[at] + jnp.sum(dz * shifted[lag], axis=0, keepdims=True)
                new_carry.append(dz[:HALO] * keep)
        return tuple(new_carry)

    zero = jnp.zeros((HALO, DH), f32)
    lax.fori_loop(0, blocks, last, (zero,) * (3 * heads))


def delta_backward(per, reset, place, x, logit, conv, gain, mixed, dnorm, t, s, n):
    length = x.shape[0]
    width = x.shape[1] // 3
    heads = width // DH
    blocks = length // SPAN
    rows = heads * SPAN
    shape = jax.ShapeDtypeStruct
    vmem = pl.BlockSpec(memory_space=pltpu.VMEM)
    smem = pl.BlockSpec(memory_space=pltpu.SMEM)
    return pl.pallas_call(
        functools.partial(bwd_kernel, per),
        out_shape=(
            shape((length, 3 * width), bf16),
            shape((length, heads), bf16),
            shape((3 * CONV, width), f32),
            shape((1, DH), f32),
        ),
        in_specs=[smem, smem] + [vmem] * 9,
        out_specs=(vmem,) * 4,
        scratch_shapes=[pltpu.VMEM((blocks, rows, DH), f32)] * 5
        + [
            pltpu.VMEM((blocks, rows, DH), bf16),
            pltpu.VMEM((blocks, rows, DH), f32),
            pltpu.VMEM((blocks, rows, DH), bf16),
            pltpu.VMEM((blocks, heads * DH, DH), bf16),
            pltpu.VMEM((heads * DH, DH), f32),
        ],
        name="delta_backward",
    )(reset, place, x, logit, conv, gain, mixed, dnorm, t, s, n)


def rms_scale(value, gain):
    return value * lax.rsqrt(jnp.mean(value * value, axis=-1, keepdims=True) + epsilon) * gain


def segment_tables(lengths_row, group_tok):
    offsets = jnp.cumsum(lengths_row) - lengths_row
    total = jnp.sum(lengths_row)
    starts = jnp.concatenate([offsets, total[None]])
    block_first = jnp.arange(group_tok // SPAN, dtype=jnp.int32) * SPAN
    reset = jnp.any(block_first[:, None] == starts[None, :], axis=1).astype(f32)
    live = (jnp.arange(group_tok, dtype=jnp.int32) < total).astype(f32)
    return reset, live


def swap(values, axis, mask):
    size = lax.axis_size(axis)
    return lax.ppermute(values, axis, [(i, i ^ mask) for i in range(size)])


def group_rows(values):
    size = lax.axis_size("seq")
    return jnp.concatenate([values] + [swap(values, "seq", k) for k in range(1, size)], axis=0)


def dot(left, right, dims, kind=f32):
    return lax.dot_general(left, right, dims, preferred_element_type=f32).astype(kind)


def row_sum(left, right, dims, local):
    size = lax.axis_size("seq")
    others = dot(left[local:], right, dims, bf16)
    sent = [
        swap(others[(k - 1) * local : k * local], "seq", k) for k in range(1, size)
    ]
    total = dot(left[:local], right, dims)
    for piece in sent:
        total = total + piece.astype(f32)
    return total


def doubled(values, axis):
    size = lax.axis_size(axis)
    mask = 1
    while mask < size:
        values = values + swap(values, axis, mask)
        mask *= 2
    return values


def gathered(values):
    return lax.all_gather(values, "dp", axis=0, tiled=True)


def scattered(values):
    return lax.psum_scatter(values, "dp", scatter_dimension=0, tiled=True)


def shards(
    tokens,
    lengths,
    cotangent,
    attn_norm_gain,
    w_query,
    w_key,
    w_value,
    w_strength,
    conv_weight,
    head_gain,
    w_output,
    ffn_norm_gain,
    w_gate,
    w_up,
    w_down,
):
    local = tokens.shape[0]
    model = tokens.shape[1]
    seq_parts = lax.axis_size("seq")
    seq_place = lax.axis_index("seq")
    dp_parts = lax.axis_size("dp")
    dp_place = lax.axis_index("dp")
    group_tok = local * seq_parts
    width = w_query.shape[1]
    heads = w_strength.shape[1]
    hidden_units = w_gate.shape[1]
    depth = w_query.shape[0]
    per = local // SPAN

    wide_qkv = gathered(jnp.concatenate([w_query, w_key, w_value], axis=1))
    second_set = gathered(jnp.concatenate([w_output.T, w_gate, w_up], axis=1))
    wide_out = second_set[:, :width]
    wide_gu = second_set[:, width:]
    wide_down = gathered(w_down.T)

    strength = w_strength.T
    strengths_all = strength
    mask = 1
    while mask < dp_parts:
        other = swap(strengths_all, "dp", mask)
        low = (dp_place & mask) == 0
        first = jnp.where(low, strengths_all, other)
        last = jnp.where(low, other, strengths_all)
        strengths_all = jnp.concatenate([first, last], axis=1)
        mask *= 2

    reset, live = segment_tables(lengths[0], group_tok)
    own_live = lax.dynamic_slice_in_dim(live, seq_place * local, local)
    place = jnp.full((1,), seq_place, jnp.int32)
    taps = conv_weight.astype(f32).reshape(3 * CONV, width)
    gain_h = head_gain.astype(f32)[None]
    x_float = tokens.astype(f32)
    hidden_float, first_pull = jax.vjp(rms_scale, x_float, attn_norm_gain.astype(f32))
    d_final = cotangent.astype(f32) * own_live[:, None]
    hidden = group_rows(hidden_float.astype(bf16))
    d_ffo = group_rows(d_final.astype(bf16))

    x_mix = dot(hidden, wide_qkv, NN, bf16)
    logit = dot(hidden, strengths_all, NT)
    normed, mixed, kept_t, kept_s, kept_n = delta_forward(per, reset, place, x_mix, logit, taps, gain_h)
    resid = x_float + row_sum(normed, wide_out, NT, local)
    second_float, second_pull = jax.vjp(rms_scale, resid, ffn_norm_gain.astype(f32))
    second = group_rows(second_float.astype(bf16))
    gate_up = dot(second, wide_gu, NN)
    gate = gate_up[:, :hidden_units]
    upper = gate_up[:, hidden_units:]
    sg = jax.nn.sigmoid(gate)
    act = (gate * sg * upper).astype(bf16)
    grad_down = scattered(dot(d_ffo, act, TN, bf16)).astype(f32).T
    d_act = dot(d_ffo, wide_down, NN)
    d_gate = (d_act * upper * (sg * (1.0 + gate * (1.0 - sg)))).astype(bf16)
    d_up = (d_act * gate * sg).astype(bf16)
    d_gu = jnp.concatenate([d_gate, d_up], axis=1)
    d_second = row_sum(d_gu, wide_gu, NT, local)
    grad_gu = scattered(dot(second, d_gu, TN, bf16)).astype(f32)
    final = resid + row_sum(act, wide_down, NT, local)
    output = (final * own_live[:, None]).astype(bf16)
    d_resid_norm, grad_gain_two = second_pull(d_second)
    d_resid = d_final + d_resid_norm
    d_branch = group_rows(d_resid.astype(bf16))
    d_normed = dot(d_branch, wide_out, NN)
    grad_out = scattered(dot(d_branch, normed, TN, bf16)).astype(f32).T
    d_mix, d_logit, d_taps, grad_head = delta_backward(
        per, reset, place, x_mix, logit, taps, gain_h, mixed, d_normed, kept_t, kept_s, kept_n
    )
    grad_qkv = scattered(dot(hidden, d_mix, TN, bf16)).astype(f32)
    grad_strength = dot(d_logit, hidden, TN)
    others = dot(d_mix[local:], wide_qkv, NT) + dot(d_logit[local:], strengths_all, NN)
    others = others.astype(bf16)
    sent = [swap(others[(k - 1) * local : k * local], "seq", k) for k in range(1, seq_parts)]
    d_hidden = dot(d_mix[:local], wide_qkv, NT) + dot(d_logit[:local], strengths_all, NN)
    for piece in sent:
        d_hidden = d_hidden + piece.astype(f32)
    d_x_norm, grad_gain_one = first_pull(d_hidden)
    input_grad = d_resid + d_x_norm

    early = doubled(
        jnp.concatenate([d_taps.reshape(-1), grad_strength.reshape(-1)]).reshape(-1, DH), "dp"
    ).reshape(-1)
    conv_grad = early[: 3 * CONV * width].reshape(3, CONV, width)
    strength_sum = early[3 * CONV * width :].reshape(heads, model)
    strength_grad = lax.dynamic_slice_in_dim(strength_sum, dp_place * depth, depth, 1).T
    gains = jnp.concatenate([grad_gain_one, grad_gain_two, grad_head[0]]).reshape(-1, DH)
    gains = doubled(doubled(gains, "dp"), "seq").reshape(-1)
    return (
        output,
        input_grad,
        gains[:model],
        grad_qkv[:, :width],
        grad_qkv[:, width : 2 * width],
        grad_qkv[:, 2 * width :],
        strength_grad,
        conv_grad,
        gains[2 * model :],
        grad_out,
        gains[model : 2 * model],
        grad_gu[:, :hidden_units],
        grad_gu[:, hidden_units:],
        grad_down,
    )


def solution(mesh):
    placed = (
        P(("dp", "seq"), None),
        P("dp", None),
        P(("dp", "seq"), None),
        P(),
        P("dp", "seq"),
        P("dp", "seq"),
        P("dp", "seq"),
        P("dp", "seq"),
        P(None, None, "seq"),
        P(),
        P("seq", "dp"),
        P(),
        P("dp", "seq"),
        P("dp", "seq"),
        P("seq", "dp"),
    )
    return jax.shard_map(
        shards,
        mesh=mesh,
        in_specs=placed,
        out_specs=(
            P(("dp", "seq"), None),
            P(("dp", "seq"), None),
            P(),
            P("dp", "seq"),
            P("dp", "seq"),
            P("dp", "seq"),
            P("dp", "seq"),
            P(None, None, "seq"),
            P(),
            P("seq", "dp"),
            P(),
            P("dp", "seq"),
            P("dp", "seq"),
            P("seq", "dp"),
        ),
        check_vma=False,
    )
```

```python
import functools

import jax
import jax.numpy as jnp
from jax import lax
from jax.experimental import pallas as pl
from jax.experimental.pallas import tpu as pltpu
from jax.sharding import PartitionSpec as P

DH = 128
CONV = 4
SPAN = 64
HALO = 8
epsilon = 1e-06
f32 = jnp.float32
bf16 = jnp.bfloat16

NN = (((1,), (0,)), ((), ()))
NT = (((1,), (1,)), ((), ()))
TN = (((0,), (0,)), ((), ()))


def mm(left, right, dims=NN):
    return lax.dot_general(left.astype(bf16), right.astype(bf16), dims, preferred_element_type=f32)


def mm3(left, right, dims=NN):
    lh = left.astype(bf16)
    ll = (left - lh.astype(f32)).astype(bf16)
    rh = right.astype(bf16)
    rl = (right - rh.astype(f32)).astype(bf16)
    out = lax.dot_general(ll, rh, dims, preferred_element_type=f32)
    out = out + lax.dot_general(lh, rl, dims, preferred_element_type=f32)
    return out + lax.dot_general(lh, rh, dims, preferred_element_type=f32)


def tri_masks(rows):
    r = lax.broadcasted_iota(jnp.int32, (rows, rows), 0)
    c = lax.broadcasted_iota(jnp.int32, (rows, rows), 1)
    same = (r // SPAN) == (c // SPAN)
    return r, c, same


def unit_lower_inverse(lower, r, c):
    eye = (r == c).astype(f32)
    half = 1
    inverse = eye
    while half < SPAN:
        pair = ((r // (2 * half)) == (c // (2 * half))) & ((r // half) != (c // half))
        corner = jnp.where(pair, lower, 0.0)
        if half == 1:
            inverse = eye - corner
        else:
            inverse = inverse - mm(mm(inverse, corner), inverse)
        half *= 2
    resid = eye - inverse - mm3(lower, inverse)
    return inverse + mm(inverse, resid)


def rolled(block, halo_before, lag):
    if lag == 0:
        return block
    whole = jnp.concatenate([halo_before, block], axis=0)
    return pltpu.roll(whole, lag, 0)[HALO:]


def rolled_back(block, halo_after, lag):
    if lag == 0:
        return block
    whole = jnp.concatenate([block, halo_after], axis=0)
    return pltpu.roll(whole, whole.shape[0] - lag, 0)[: block.shape[0]]


def sigmoid(v):
    return 1.0 / (1.0 + jnp.exp(-v))


def row_start(place_ref, c, per):
    chunk = lax.div(c, per)
    return pl.multiple_of(((chunk ^ place_ref[0]) * per + lax.rem(c, per)) * SPAN, SPAN)


def conv_block(x_ref, conv_ref, start, before, keep, part, head, width):
    cols = pl.ds(part * width + head * DH, DH)
    block = x_ref[pl.ds(start, SPAN), cols].astype(f32)
    halo = x_ref[pl.ds(before, 16), cols].astype(f32)[16 - HALO :] * keep
    shifted = [rolled(block, halo, lag) for lag in range(CONV)]
    taps = [conv_ref[pl.ds(part * CONV + lag, 1), pl.ds(head * DH, DH)] for lag in range(CONV)]
    total = taps[0] * shifted[0]
    for lag in range(1, CONV):
        total = total + taps[lag] * shifted[lag]
    return total, shifted, taps


def strengths(logit_refs, start, heads):
    columns = []
    for logit_ref in logit_refs:
        block = sigmoid(logit_ref[pl.ds(start, SPAN), :]).astype(bf16).astype(f32)
        columns += [block[:, h : h + 1] for h in range(heads)]
    return jnp.concatenate(columns, axis=0)


def fwd_kernel(per, groups, reset_ref, place_ref, conv_ref, gain_ref, *refs):
    x_refs, logit_refs = refs[:groups], refs[groups : 2 * groups]
    normed_refs, mixed_refs = refs[2 * groups : 3 * groups], refs[3 * groups : 4 * groups]
    t_ref, s_ref, n_ref, q_s, k_s, u_s, w_s, p_s, state = refs[4 * groups :]
    length = x_refs[0].shape[0]
    width = x_refs[0].shape[1] // 3
    heads = width // DH
    blocks = length // SPAN
    pairs = [(g, h) for g in range(groups) for h in range(heads)]
    rows = len(pairs) * SPAN
    r, c_, same = tri_masks(rows)
    strict = same & (r > c_)
    incl = same & (r >= c_)

    def local(c, carry):
        start = row_start(place_ref, c, per)
        before = pl.multiple_of(row_start(place_ref, jnp.maximum(c - 1, 0), per) + (SPAN - 16), 16)
        parts = []
        for part in range(3):
            pieces = []
            for g, h in pairs:
                keep = 1.0 - reset_ref[g * blocks + c]
                z, _, _ = conv_block(x_refs[g], conv_ref, start, before, keep, part, h, width)
                pieces.append(z)
            z = jnp.concatenate(pieces, axis=0)
            parts.append(z * sigmoid(z))
        q, k, v = parts
        q = q * lax.rsqrt(jnp.sum(q * q, axis=-1, keepdims=True) + epsilon)
        k = k * lax.rsqrt(jnp.sum(k * k, axis=-1, keepdims=True) + epsilon)
        b = strengths(logit_refs, start, heads)
        gram = mm3(k, k, NT)
        lower = jnp.where(strict, gram * b, 0.0)
        inverse = unit_lower_inverse(lower, r, c_)
        p_s[c] = jnp.where(incl, mm(q, k, NT), 0.0).astype(bf16)
        t_ref[c] = inverse.astype(bf16)
        solved = mm(inverse, jnp.concatenate([b * k, b * v], axis=1))
        w_s[c] = solved[:, :DH].astype(bf16)
        u_s[c] = solved[:, DH:]
        q_s[c] = q.astype(bf16)
        k_s[c] = k.astype(bf16)
        return carry

    lax.fori_loop(0, blocks, local, 0)
    state[...] = jnp.zeros_like(state)
    gain = gain_ref[...]

    def scan(c, carry):
        start = row_start(place_ref, c, per)
        news = []
        reads = []
        for at, (g, h) in enumerate(pairs):
            keep = 1.0 - reset_ref[g * blocks + c]
            here = pl.ds(at * SPAN, SPAN)
            s = state[pl.ds(at * DH, DH), :] * keep
            low = s.astype(bf16)
            s_ref[c, pl.ds(at * DH, DH), :] = low
            both = jnp.concatenate([w_s[c, here, :], q_s[c, here, :]], axis=0)
            got = mm(both, low)
            fresh = u_s[c, here, :] - got[:SPAN]
            state[pl.ds(at * DH, DH), :] = s + mm(k_s[c, here, :], fresh, TN)
            news.append(fresh)
            reads.append(got[SPAN:])
        fresh = jnp.concatenate(news, axis=0).astype(bf16)
        n_ref[c] = fresh
        out = jnp.concatenate(reads, axis=0) + mm(p_s[c], fresh)
        mixed = out.astype(bf16)
        wide = mixed.astype(f32)
        normed = (wide * lax.rsqrt(jnp.mean(wide * wide, axis=-1, keepdims=True) + epsilon) * gain).astype(bf16)
        for at, (g, h) in enumerate(pairs):
            cols = pl.ds(h * DH, DH)
            mixed_refs[g][pl.ds(start, SPAN), cols] = mixed[at * SPAN : (at + 1) * SPAN]
            normed_refs[g][pl.ds(start, SPAN), cols] = normed[at * SPAN : (at + 1) * SPAN]
        return carry

    lax.fori_loop(0, blocks, scan, 0)


def delta_forward(per, reset, place, xs, logits, conv, gain):
    groups = len(xs)
    length = xs[0].shape[0]
    width = xs[0].shape[1] // 3
    heads = groups * (width // DH)
    blocks = length // SPAN
    rows = heads * SPAN
    shape = jax.ShapeDtypeStruct
    vmem = pl.BlockSpec(memory_space=pltpu.VMEM)
    smem = pl.BlockSpec(memory_space=pltpu.SMEM)
    out = pl.pallas_call(
        functools.partial(fwd_kernel, per, groups),
        out_shape=(shape((length, width), bf16),) * (2 * groups)
        + (
            shape((blocks, rows, rows), bf16),
            shape((blocks, heads * DH, DH), bf16),
            shape((blocks, rows, DH), bf16),
        ),
        in_specs=[smem, smem] + [vmem] * (2 + 2 * groups),
        out_specs=(vmem,) * (2 * groups + 3),
        scratch_shapes=[
            pltpu.VMEM((blocks, rows, DH), bf16),
            pltpu.VMEM((blocks, rows, DH), bf16),
            pltpu.VMEM((blocks, rows, DH), f32),
            pltpu.VMEM((blocks, rows, DH), bf16),
            pltpu.VMEM((blocks, rows, rows), bf16),
            pltpu.VMEM((heads * DH, DH), f32),
        ],
        name="delta_forward",
    )(reset, place, conv, gain, *xs, *logits)
    return out[:groups], out[groups : 2 * groups], out[2 * groups :]


def bwd_kernel(per, groups, reset_ref, place_ref, conv_ref, gain_ref, *refs):
    x_refs, logit_refs = refs[:groups], refs[groups : 2 * groups]
    mixed_refs, dnorm_refs = refs[2 * groups : 3 * groups], refs[3 * groups : 4 * groups]
    t_ref, s_ref, n_ref = refs[4 * groups : 4 * groups + 3]
    dx_refs = refs[4 * groups + 3 : 5 * groups + 3]
    dconv_ref, dgain_ref, q_s, k_s, v_s, iq_s, ik_s, do_s, g_s, kt_s, ds_s, dstate = refs[5 * groups + 3 :]
    length = x_refs[0].shape[0]
    width = x_refs[0].shape[1] // 3
    heads = width // DH
    blocks = length // SPAN
    pairs = [(g, h) for g in range(groups) for h in range(heads)]
    rows = len(pairs) * SPAN
    r, c_, same = tri_masks(rows)
    strict = same & (r > c_)
    incl = same & (r >= c_)
    gain = gain_ref[...]

    def stack(some, start):
        return jnp.concatenate([some[g][pl.ds(start, SPAN), pl.ds(h * DH, DH)] for g, h in pairs], axis=0)

    def local(c, total):
        start = row_start(place_ref, c, per)
        before = pl.multiple_of(row_start(place_ref, jnp.maximum(c - 1, 0), per) + (SPAN - 16), 16)
        parts = []
        for part in range(3):
            pieces = []
            for g, h in pairs:
                keep = 1.0 - reset_ref[g * blocks + c]
                z, _, _ = conv_block(x_refs[g], conv_ref, start, before, keep, part, h, width)
                pieces.append(z)
            z = jnp.concatenate(pieces, axis=0)
            parts.append(z * sigmoid(z))
        q, k, v = parts
        iq = lax.rsqrt(jnp.sum(q * q, axis=-1, keepdims=True) + epsilon)
        ik = lax.rsqrt(jnp.sum(k * k, axis=-1, keepdims=True) + epsilon)
        q = q * iq
        k = k * ik
        q_s[c] = q
        k_s[c] = k
        v_s[c] = v
        iq_s[c] = jnp.broadcast_to(iq, (rows, DH))
        ik_s[c] = jnp.broadcast_to(ik, (rows, DH))
        mixed = stack(mixed_refs, start).astype(f32)
        dnorm = stack(dnorm_refs, start)
        inv = lax.rsqrt(jnp.mean(mixed * mixed, axis=-1, keepdims=True) + epsilon)
        u = mixed * inv
        total = total + jnp.sum(dnorm * u, axis=0, keepdims=True)
        dg = dnorm * gain
        do = ((dg - u * jnp.mean(dg * u, axis=-1, keepdims=True)) * inv).astype(bf16)
        do_s[c] = do
        p = jnp.where(incl, mm(q, k, NT), 0.0)
        t = t_ref[c]
        pre = mm(p, do, TN)
        got = mm(t, jnp.concatenate([pre, k], axis=1), TN)
        g_s[c] = got[:, :DH]
        kt_s[c] = got[:, DH:].astype(bf16)
        return total

    dgain_ref[...] = lax.fori_loop(0, blocks, local, jnp.zeros((1, DH), f32))
    dstate[...] = jnp.zeros_like(dstate)

    def scan(i, carry):
        c = blocks - 1 - i
        start = row_start(place_ref, c, per)
        b = strengths(logit_refs, start, heads)
        k = k_s[c]
        bk = (b * k).astype(bf16)
        for at, (g_, h) in enumerate(pairs):
            keep = 1.0 - reset_ref[g_ * blocks + c]
            hr = pl.ds(at * SPAN, SPAN)
            ds = dstate[pl.ds(at * DH, DH), :]
            low = ds.astype(bf16)
            ds_s[c, pl.ds(at * DH, DH), :] = low
            g = g_s[c, hr, :] + mm(kt_s[c, hr, :], low)
            g_s[c, hr, :] = g
            ql = q_s[c, hr, :].astype(bf16)
            both = jnp.concatenate([ql, bk[at * SPAN : (at + 1) * SPAN]], axis=0)
            other = jnp.concatenate([do_s[c, hr, :], (-g).astype(bf16)], axis=0)
            dstate[pl.ds(at * DH, DH), :] = (ds + mm(both, other, TN)) * keep
        return carry

    lax.fori_loop(0, blocks, scan, 0)
    dconv_ref[...] = jnp.zeros_like(dconv_ref)
    extra = dx_refs[0].shape[1] - 3 * width
    lane = lax.broadcasted_iota(jnp.int32, (SPAN, extra), 1)

    def last(i, carry):
        c = blocks - 1 - i
        start = row_start(place_ref, c, per)
        before = pl.multiple_of(row_start(place_ref, jnp.maximum(c - 1, 0), per) + (SPAN - 16), 16)
        b = strengths(logit_refs, start, heads)
        q, k, v = q_s[c], k_s[c], v_s[c]
        g, n, do = g_s[c], n_ref[c], do_s[c]
        gl = g.astype(bf16)
        both = jnp.concatenate([do, gl], axis=0)
        outer = mm(both, n, NT)
        dp = jnp.where(incl, outer[:rows], 0.0).astype(bf16)
        da = jnp.where(strict, -outer[rows:], 0.0).astype(bf16)
        down = mm(jnp.concatenate([dp, da], axis=0), k)
        up = mm(jnp.concatenate([dp, da], axis=0), jnp.concatenate([q, b * k], axis=0), TN)
        sides = []
        nds = []
        for at in range(len(pairs)):
            s = s_ref[c, pl.ds(at * DH, DH), :]
            hr = slice(at * SPAN, (at + 1) * SPAN)
            sides.append(mm(jnp.concatenate([do[hr], gl[hr]], axis=0), s, NT))
            nds.append(mm(n[hr], ds_s[c, pl.ds(at * DH, DH), :], NT))
        dos = jnp.concatenate([x[:SPAN] for x in sides], axis=0)
        gs = jnp.concatenate([x[SPAN:] for x in sides], axis=0)
        dq = dos + down[:rows]
        y = down[rows:] - gs
        dk = up + jnp.concatenate(nds, axis=0) + b * y
        dv = b * g
        db = jnp.sum(k * y + v * g, axis=-1, keepdims=True)
        dq = (dq - q * jnp.sum(q * dq, axis=-1, keepdims=True)) * iq_s[c]
        dk = (dk - k * jnp.sum(k * dk, axis=-1, keepdims=True)) * ik_s[c]
        for g_ in range(groups):
            row = jnp.zeros((SPAN, extra), f32)
            for h in range(heads):
                at = g_ * heads + h
                row = jnp.where(lane == h, db[at * SPAN : (at + 1) * SPAN], row)
            sg = sigmoid(logit_refs[g_][pl.ds(start, SPAN), :])
            dl = (row.astype(bf16).astype(f32) * sg * (1.0 - sg)).astype(bf16)
            dx_refs[g_][pl.ds(start, SPAN), pl.ds(3 * width, extra)] = dl
        new_carry = []
        for part, grad in enumerate((dq, dk, dv)):
            for at, (g_, h) in enumerate(pairs):
                keep = 1.0 - reset_ref[g_ * blocks + c]
                z, shifted, taps = conv_block(x_refs[g_], conv_ref, start, before, keep, part, h, width)
                sz = sigmoid(z)
                dz = grad[at * SPAN : (at + 1) * SPAN] * (sz * (1.0 + z * (1.0 - sz)))
                rest = carry[part * len(pairs) + at]
                total = taps[0] * dz
                for lag in range(1, CONV):
                    total = total + taps[lag] * rolled_back(dz, rest, lag)
                dx_refs[g_][pl.ds(start, SPAN), pl.ds(part * width + h * DH, DH)] = total.astype(bf16)
                for lag in range(CONV):
                    spot = pl.ds(part * CONV + lag, 1), pl.ds(h * DH, DH)
                    dconv_ref[spot] = dconv_ref[spot] + jnp.sum(dz * shifted[lag], axis=0, keepdims=True)
                new_carry.append(dz[:HALO] * keep)
        return tuple(new_carry)

    zero = jnp.zeros((HALO, DH), f32)
    lax.fori_loop(0, blocks, last, (zero,) * (3 * len(pairs)))


def delta_backward(per, reset, place, xs, logits, conv, gain, mixeds, dnorms, kept):
    groups = len(xs)
    length = xs[0].shape[0]
    width = xs[0].shape[1] // 3
    extra = logits[0].shape[1]
    heads = groups * (width // DH)
    blocks = length // SPAN
    rows = heads * SPAN
    shape = jax.ShapeDtypeStruct
    vmem = pl.BlockSpec(memory_space=pltpu.VMEM)
    smem = pl.BlockSpec(memory_space=pltpu.SMEM)
    out = pl.pallas_call(
        functools.partial(bwd_kernel, per, groups),
        out_shape=(shape((length, 3 * width + extra), bf16),) * groups
        + (shape((3 * CONV, width), f32), shape((1, DH), f32)),
        in_specs=[smem, smem] + [vmem] * (2 + 4 * groups + 3),
        out_specs=(vmem,) * (groups + 2),
        scratch_shapes=[pltpu.VMEM((blocks, rows, DH), f32)] * 5
        + [
            pltpu.VMEM((blocks, rows, DH), bf16),
            pltpu.VMEM((blocks, rows, DH), f32),
            pltpu.VMEM((blocks, rows, DH), bf16),
            pltpu.VMEM((blocks, heads * DH, DH), bf16),
            pltpu.VMEM((heads * DH, DH), f32),
        ],
        name="delta_backward",
    )(reset, place, conv, gain, *xs, *logits, *mixeds, *dnorms, *kept)
    return out[:groups], out[groups], out[groups + 1]


def slot_of(block, core, parts):
    return ((block & 1) ^ core) * (parts // 2) + block // 2


def put_columns(values, out_ref, core, parts):
    depth = values.shape[1] // parts
    for block in range(parts):
        start = pl.multiple_of(slot_of(block, core, parts) * depth, depth)
        out_ref[:, pl.ds(start, depth)] = values[:, block * depth : (block + 1) * depth]


def column_sum(pieces, core, parts):
    depth = pieces[0].shape[1] // parts
    blocks = []
    for block in range(parts):
        start = pl.multiple_of(slot_of(block, core, parts) * depth, depth)
        total = pieces[0][:, pl.ds(start, depth)].astype(f32)
        for piece in pieces[1:]:
            total = total + piece[:, pl.ds(start, depth)].astype(f32)
        blocks.append(total)
    return jnp.concatenate(blocks, axis=1)


def on_core(kernel, name, shapes, core, *arrays):
    vmem = pl.BlockSpec(memory_space=pltpu.VMEM)
    smem = pl.BlockSpec(memory_space=pltpu.SMEM)
    return pl.pallas_call(
        kernel,
        out_shape=shapes,
        in_specs=[smem] + [vmem] * len(arrays),
        out_specs=(vmem,) * len(shapes),
        name=name,
    )(core, *arrays)


def first_kernel(parts, core_ref, x_ref, gain_ref, cot_ref, live_ref, hidden_ref, d_ffo_ref):
    x = x_ref[...].astype(f32)
    scale = lax.rsqrt(jnp.mean(x * x, axis=-1, keepdims=True) + epsilon)
    put_columns((x * scale * gain_ref[...]).astype(bf16), hidden_ref, core_ref[0], parts)
    put_columns((cot_ref[...].astype(f32) * live_ref[...]).astype(bf16), d_ffo_ref, core_ref[0], parts)


def middle_kernel(parts, core_ref, x_ref, gain_ref, *refs):
    pieces, (resid_ref, second_ref) = refs[:-2], refs[-2:]
    resid = x_ref[...].astype(f32) + column_sum(pieces, core_ref[0], parts)
    resid_ref[...] = resid
    scale = lax.rsqrt(jnp.mean(resid * resid, axis=-1, keepdims=True) + epsilon)
    put_columns((resid * scale * gain_ref[...]).astype(bf16), second_ref, core_ref[0], parts)


def norm_back(base, gain, grad):
    scale = lax.rsqrt(jnp.mean(base * base, axis=-1, keepdims=True) + epsilon)
    unit = base * scale
    d_unit = grad * gain
    d_base = (d_unit - unit * jnp.mean(d_unit * unit, axis=-1, keepdims=True)) * scale
    return d_base, jnp.sum(grad * unit, axis=0, keepdims=True)


def back_kernel(parts, core_ref, resid_ref, gain_ref, cot_ref, live_ref, *refs):
    pieces, (d_resid_ref, d_branch_ref, d_gain_ref) = refs[:-3], refs[-3:]
    d_norm, d_gain_ref[...] = norm_back(resid_ref[...], gain_ref[...], column_sum(pieces, core_ref[0], parts))
    d_resid = cot_ref[...].astype(f32) * live_ref[...] + d_norm
    d_resid_ref[...] = d_resid
    put_columns(d_resid.astype(bf16), d_branch_ref, core_ref[0], parts)


def last_kernel(parts, core_ref, x_ref, gain_ref, d_resid_ref, *refs):
    pieces, (grad_ref, d_gain_ref) = refs[:-2], refs[-2:]
    d_norm, d_gain_ref[...] = norm_back(
        x_ref[...].astype(f32), gain_ref[...], column_sum(pieces, core_ref[0], parts)
    )
    grad_ref[...] = d_resid_ref[...] + d_norm


def finish_kernel(parts, core_ref, resid_ref, live_ref, *refs):
    pieces, out_ref = refs[:-1], refs[-1]
    out_ref[...] = ((resid_ref[...] + column_sum(pieces, core_ref[0], parts)) * live_ref[...]).astype(bf16)


def row_copies(pieces, whole, sems):
    rows = pieces[0].shape[0]
    return [
        pltpu.make_async_copy(piece, whole.at[pl.ds(j * rows, rows), :], sems.at[j])
        for j, piece in enumerate(pieces)
    ]


def weight_copies(packs, whole, sems, lines, first, units):
    depth = packs[0].shape[1]
    stride = packs[0].shape[0] // lines
    copies = []
    for side, pack in enumerate(packs):
        for k in range(lines):
            start = (side * lines + k) * depth
            copies.append(
                pltpu.make_async_copy(
                    pack.at[pl.ds(k * stride + first, units), :],
                    whole.at[:, pl.ds(start, depth)],
                    sems.at[side * lines + k],
                )
            )
    return copies


def started(copies):
    for copy in copies:
        copy.start()
    return copies


def waited(copies):
    for copy in copies:
        copy.wait()


def mix_kernel(lines, count, width, near, far, *refs):
    pieces, (rows_ref, x_ref, logit_ref, buf, row_sems, sems) = refs[:count], refs[count:]
    copies = started(row_copies(pieces, rows_ref, row_sems))
    copies += started(weight_copies((near, far), buf, sems, lines, 0, buf.shape[0]))
    waited(copies)
    out = lax.dot_general(rows_ref[...], buf[...], NT, preferred_element_type=f32)
    x_ref[...] = out[:, :width].astype(bf16)
    logit_ref[...] = out[:, width:]


def mix_product(lines, pieces, packs, width, extra):
    vmem = pl.BlockSpec(memory_space=pltpu.VMEM)
    smem = pl.BlockSpec(memory_space=pltpu.SMEM)
    hbm = pl.BlockSpec(memory_space=pl.ANY)
    tokens = pieces[0].shape[0] * len(pieces)
    model = pieces[0].shape[1]
    shape = jax.ShapeDtypeStruct
    return pl.pallas_call(
        functools.partial(mix_kernel, lines, len(pieces), width),
        out_shape=(shape((tokens, model), bf16), shape((tokens, width), bf16), shape((tokens, extra), f32)),
        in_specs=[hbm] * (2 + len(pieces)),
        out_specs=(vmem,) * 3,
        scratch_shapes=[
            pltpu.VMEM((width + extra, model), bf16),
            pltpu.SemaphoreType.DMA((len(pieces),)),
            pltpu.SemaphoreType.DMA((2 * lines,)),
        ],
        cost_estimate=pl.CostEstimate(
            flops=2 * tokens * model * (width + extra), bytes_accessed=2 * model * (2 * tokens + width), transcendentals=0
        ),
        name="mix_product",
    )(*packs, *pieces)


def branch_kernel(lines, count, first, near, far, *refs):
    pieces, (rows_ref, out_ref, buf, row_sems, sems) = refs[:count], refs[count:]
    copies = started(row_copies(pieces, rows_ref, row_sems))
    copies += started(weight_copies((near, far), buf, sems, lines, first, buf.shape[0]))
    waited(copies)
    out_ref[...] = lax.dot_general(rows_ref[...], buf[...], NT, preferred_element_type=f32)


def branch_back(lines, pieces, packs, first, units):
    vmem = pl.BlockSpec(memory_space=pltpu.VMEM)
    smem = pl.BlockSpec(memory_space=pltpu.SMEM)
    hbm = pl.BlockSpec(memory_space=pl.ANY)
    tokens = pieces[0].shape[0] * len(pieces)
    model = pieces[0].shape[1]
    shape = jax.ShapeDtypeStruct
    return pl.pallas_call(
        functools.partial(branch_kernel, lines, len(pieces), first),
        out_shape=(shape((tokens, model), bf16), shape((tokens, units), f32)),
        in_specs=[hbm] * (2 + len(pieces)),
        out_specs=(vmem,) * 2,
        scratch_shapes=[
            pltpu.VMEM((units, model), bf16),
            pltpu.SemaphoreType.DMA((len(pieces),)),
            pltpu.SemaphoreType.DMA((2 * lines,)),
        ],
        cost_estimate=pl.CostEstimate(
            flops=2 * tokens * model * units, bytes_accessed=2 * model * (2 * tokens + units), transcendentals=0
        ),
        name="branch_back",
    )(*packs, *pieces)


def ffn_kernel(lines, count, half, seq_ref, near, far, cots, *refs):
    seconds = refs[:count]
    s_ref, f_ref, act_ref, dgate_ref, dup_ref = refs[count : count + 5]
    chunk_refs, (bufs, row_sems, sems) = refs[count + 5 : 2 * count + 5], refs[2 * count + 5 :]
    rows = seconds[0].shape[0]
    units = act_ref.shape[1]
    first = started(row_copies(seconds, s_ref, row_sems.at[0]))
    weights = []
    for j in range(3):
        weights.append(
            started(weight_copies((near, far), bufs.at[j], sems.at[j], lines, j * units, units))
        )
    later = []
    for j in range(count):
        start = pl.multiple_of(((seq_ref[0] ^ j) * 2 + half) * rows, rows)
        later.append(
            pltpu.make_async_copy(
                cots.at[pl.ds(start, rows), :], f_ref.at[pl.ds(j * rows, rows), :], row_sems.at[1, j]
            )
        )
    started(later)
    waited(first + weights[0])
    gate = lax.dot_general(s_ref[...], bufs[0], NT, preferred_element_type=f32)
    waited(weights[1])
    upper = lax.dot_general(s_ref[...], bufs[1], NT, preferred_element_type=f32)
    sg = sigmoid(gate)
    soft = gate * sg
    act_ref[...] = (soft * upper).astype(bf16)
    slope = upper * (sg * (1.0 + gate * (1.0 - sg)))
    waited(later + weights[2])
    d_act = lax.dot_general(f_ref[...], bufs[2], NT, preferred_element_type=f32)
    d_gate = (d_act * slope).astype(bf16)
    d_up = (d_act * soft).astype(bf16)
    dgate_ref[...] = d_gate
    dup_ref[...] = d_up
    tile = s_ref.shape[1] // 4
    for t in range(4):
        cols = slice(t * tile, (t + 1) * tile)
        out = lax.dot_general(d_gate, bufs[0, :, cols], NN, preferred_element_type=f32)
        out = out + lax.dot_general(d_up, bufs[1, :, cols], NN, preferred_element_type=f32)
        for j, chunk in enumerate(chunk_refs):
            chunk[:, cols] = out[j * rows : (j + 1) * rows].astype(bf16)


def ffn_part(lines, half, seq, seconds, cots, packs):
    vmem = pl.BlockSpec(memory_space=pltpu.VMEM)
    smem = pl.BlockSpec(memory_space=pltpu.SMEM)
    hbm = pl.BlockSpec(memory_space=pl.ANY)
    count = len(seconds)
    tokens = seconds[0].shape[0] * count
    model = seconds[0].shape[1]
    units = packs[0].shape[0] // (3 * lines)
    shape = jax.ShapeDtypeStruct
    return pl.pallas_call(
        functools.partial(ffn_kernel, lines, count, half),
        out_shape=(shape((tokens, model), bf16),) * 2
        + (shape((tokens, units), bf16),) * 3
        + (shape((tokens // count, model), bf16),) * count,
        in_specs=[smem] + [hbm] * (3 + count),
        out_specs=(vmem,) * (5 + count),
        scratch_shapes=[
            pltpu.VMEM((3, units, model), bf16),
            pltpu.SemaphoreType.DMA((2, count)),
            pltpu.SemaphoreType.DMA((3, 2 * lines)),
        ],
        cost_estimate=pl.CostEstimate(
            flops=10 * tokens * units * model, bytes_accessed=6 * units * model + 8 * tokens * model, transcendentals=tokens * units
        ),
        name="ffn_part",
    )(seq, *packs, cots, *seconds)


def product_kernel(halves, spans, steps, fold, stride, count, *refs):
    terms = len(spans)
    lefts = refs[: halves * terms]
    near_ref, far_ref = refs[halves * terms : halves * terms + 2]
    outs = refs[halves * terms + 2 :]
    step = pl.program_id(0)
    rows = outs[0].shape[0]
    depth = near_ref.shape[1]

    def run(pack):
        for half in range(halves):
            for k in range(fold):
                total = None
                for left, (first, units) in zip(lefts[half * terms : (half + 1) * terms], spans):
                    at = k * stride + first
                    part = lax.dot_general(left[...], pack[at : at + units, :], NN, preferred_element_type=f32)
                    total = part if total is None else total + part
                for j in range(count):
                    outs[half * count + j][:, k * depth : (k + 1) * depth] = total[j * rows : (j + 1) * rows].astype(bf16)

    @pl.when(step < steps)
    def _():
        run(near_ref)

    @pl.when(step >= steps)
    def _():
        run(far_ref)


def team_product(lines, lefts, spans, packs, count):
    halves = len(lefts)
    flat = [left for half in lefts for left in half]
    tokens = flat[0].shape[0]
    fold = 2
    stride = packs[0].shape[0] // lines
    depth = packs[0].shape[1]
    steps = lines // fold
    rows = tokens // count
    units = sum(n for _, n in spans)
    out = pl.pallas_call(
        functools.partial(product_kernel, halves, spans, steps, fold, stride, count),
        grid=(2 * steps,),
        in_specs=[pl.BlockSpec(left.shape, lambda t: (0, 0)) for left in flat]
        + [
            pl.BlockSpec((fold * stride, depth), lambda t: (jnp.minimum(t, steps - 1), 0)),
            pl.BlockSpec((fold * stride, depth), lambda t: (jnp.maximum(t - steps, 0), 0)),
        ],
        out_specs=[pl.BlockSpec((rows, fold * depth), lambda t: (0, t))] * (count * halves),
        out_shape=[jax.ShapeDtypeStruct((rows, 2 * lines * depth), bf16)] * (count * halves),
        cost_estimate=pl.CostEstimate(
            flops=4 * halves * tokens * units * lines * depth,
            bytes_accessed=4 * stride * lines * depth + 4 * halves * tokens * lines * depth,
            transcendentals=0,
        ),
        name="team_product",
    )(*flat, *packs)
    return [out[half * count : (half + 1) * count] for half in range(halves)]


def finish_product_kernel(halves, first, units, steps, fold, stride, count, seq_ref, *refs):
    lefts = refs[:halves]
    near_ref, far_ref, out_ref = refs[halves:]
    step = pl.program_id(0)
    rows = lefts[0].shape[0] // count
    depth = near_ref.shape[1]

    def run(pack):
        for half, left in enumerate(lefts):
            for k in range(fold):
                at = k * stride + first
                total = lax.dot_general(left[...], pack[at : at + units, :], NN, preferred_element_type=f32)
                for j in range(count):
                    start = pl.multiple_of(((seq_ref[0] ^ j) * halves + half) * rows, rows)
                    out_ref[pl.ds(start, rows), k * depth : (k + 1) * depth] = total[j * rows : (j + 1) * rows].astype(bf16)

    @pl.when(step < steps)
    def _():
        run(near_ref)

    @pl.when(step >= steps)
    def _():
        run(far_ref)


def finish_product(lines, seq, lefts, span, packs, count):
    first, units = span
    tokens = lefts[0].shape[0]
    fold = 2
    stride = packs[0].shape[0] // lines
    depth = packs[0].shape[1]
    steps = lines // fold
    whole = tokens * len(lefts)
    grid_spec = pltpu.PrefetchScalarGridSpec(
        num_scalar_prefetch=1,
        grid=(2 * steps,),
        in_specs=[pl.BlockSpec(left.shape, lambda t, s: (0, 0)) for left in lefts]
        + [
            pl.BlockSpec((fold * stride, depth), lambda t, s: (jnp.minimum(t, steps - 1), 0)),
            pl.BlockSpec((fold * stride, depth), lambda t, s: (jnp.maximum(t - steps, 0), 0)),
        ],
        out_specs=pl.BlockSpec((whole, fold * depth), lambda t, s: (0, t)),
    )
    return pl.pallas_call(
        functools.partial(finish_product_kernel, len(lefts), first, units, steps, fold, stride, count),
        grid_spec=grid_spec,
        out_shape=jax.ShapeDtypeStruct((whole, 2 * lines * depth), bf16),
        cost_estimate=pl.CostEstimate(
            flops=4 * whole * units * lines * depth,
            bytes_accessed=4 * stride * lines * depth + 4 * whole * lines * depth,
            transcendentals=0,
        ),
        name="finish_product",
    )(seq, *lefts, *packs)


def cut_kernel(lines, count, *refs):
    kept, got, out_ref = refs[:count], refs[count : 2 * count], refs[2 * count]
    depth = out_ref.shape[1]
    stride = out_ref.shape[0] // lines
    first = 0
    for left, right in zip(kept, got):
        rows = left.shape[0]
        for k in range(lines):
            cols = slice(k * depth, (k + 1) * depth)
            out_ref[k * stride + first : k * stride + first + rows, :] = (
                left[:, cols].astype(f32) + right[:, cols].astype(f32)
            ).astype(bf16)
        first += rows


def line_cut(lines, kept, got):
    vmem = pl.BlockSpec(memory_space=pltpu.VMEM)
    rows = sum(left.shape[0] for left in kept)
    return pl.pallas_call(
        functools.partial(cut_kernel, lines, len(kept)),
        out_shape=jax.ShapeDtypeStruct((lines * rows, kept[0].shape[1] // lines), bf16),
        in_specs=[vmem] * (2 * len(kept)),
        out_specs=vmem,
        name="line_cut",
    )(*kept, *got)


def rms_scale(value, gain):
    return value * lax.rsqrt(jnp.mean(value * value, axis=-1, keepdims=True) + epsilon) * gain


def segment_tables(lengths_row, group_tok):
    offsets = jnp.cumsum(lengths_row) - lengths_row
    total = jnp.sum(lengths_row)
    starts = jnp.concatenate([offsets, total[None]])
    block_first = jnp.arange(group_tok // SPAN, dtype=jnp.int32) * SPAN
    reset = jnp.any(block_first[:, None] == starts[None, :], axis=1).astype(f32)
    live = (jnp.arange(group_tok, dtype=jnp.int32) < total).astype(f32)
    return reset, live


def swap(values, axis, mask):
    size = lax.axis_size(axis)
    return lax.ppermute(values, axis, [(i, i ^ mask) for i in range(size)])


def dot(left, right, dims, kind=f32):
    return lax.dot_general(left, right, dims, preferred_element_type=f32).astype(kind)


def after(values, *others):
    return lax.optimization_barrier((values, *others))[0]


def added(first, second):
    return (first.astype(f32) + second.astype(f32)).astype(bf16)


def seq_pieces(values):
    return [values] + [swap(values, "seq", k) for k in range(1, lax.axis_size("seq"))]


def seq_relayed(values, upward):
    pieces = [values]
    for k in range(1, lax.axis_size("seq")):
        hop = 1 << (k.bit_length() - 1) if upward else k & -k
        pieces.append(swap(pieces[k ^ hop], "seq", hop))
    return pieces


def twin_rows(values):
    return swap(values, "dp", 2)


def returned(chunks):
    return [chunks[0]] + [swap(chunks[j], "seq", j) for j in range(1, len(chunks))]


def summed(pieces):
    total = pieces[0].astype(f32)
    for piece in pieces[1:]:
        total = total + piece.astype(f32)
    return total


def halves_of(arrays, half):
    picked = []
    for array in arrays:
        rows = array.shape[0] // 2
        picked.append(array[half * rows : (half + 1) * rows])
    return jnp.concatenate(picked, axis=0)


def line_exchange(values):
    dp_parts = lax.axis_size("dp")
    groups = [list(range(c, dp_parts, 2)) for c in (0, 1)]
    return lax.all_to_all(values, "dp", 0, 0, tiled=True, axis_index_groups=groups)


def line_pack(arrays, lines, *others):
    both = jnp.concatenate([halves_of(arrays, 0), halves_of(arrays, 1)], axis=0)
    return line_exchange(after(jnp.concatenate([both] * (lines // 2), axis=0), *others))


def line_total(pieces, lines, spans):
    rows = pieces.shape[0] // lines
    split = [pieces[k * rows : (k + 1) * rows] for k in range(lines)]
    low = summed(split[0::2])
    high = summed(split[1::2])
    return [
        jnp.concatenate([low[first : first + n], high[first : first + n]], axis=0) for first, n in spans
    ]


def doubled(values, axis):
    size = lax.axis_size(axis)
    mask = 1
    while mask < size:
        values = values + swap(values, axis, mask)
        mask *= 2
    return values


def all_sum(values):
    seq_parts, dp_parts = lax.axis_size("seq"), lax.axis_size("dp")
    values = summed([values] + [swap(values, "seq", k) for k in range(1, seq_parts)])
    values = summed([values] + [swap(values, "dp", k) for k in range(2, dp_parts, 2)])
    return values + swap(values, "dp", 1)


def shards(
    tokens,
    lengths,
    cotangent,
    attn_norm_gain,
    w_query,
    w_key,
    w_value,
    w_strength,
    conv_weight,
    head_gain,
    w_output,
    ffn_norm_gain,
    w_gate,
    w_up,
    w_down,
):
    local, model = tokens.shape
    seq_parts = lax.axis_size("seq")
    seq_place = lax.axis_index("seq")
    dp_parts = lax.axis_size("dp")
    dp_place = lax.axis_index("dp")
    lines = dp_parts // 2
    group_tok = local * seq_parts
    full_width = w_query.shape[1]
    full_heads = w_strength.shape[1]
    width = full_width // 2
    heads = full_heads // 2
    extra = 16
    units = w_gate.shape[1] // 2
    side = model // 2
    per = local // SPAN
    odd = dp_place >> 1 & 1

    def scalar(value):
        return jnp.full((1,), value, jnp.int32)

    def twin(values):
        return swap(values, "dp", 1)

    core = scalar(dp_place & 1)
    place = scalar(seq_place)
    rows_f32 = jax.ShapeDtypeStruct((local, model), f32)
    rows_b16 = jax.ShapeDtypeStruct((local, model), bf16)
    gain_f32 = jax.ShapeDtypeStruct((1, model), f32)

    reset_own, live = segment_tables(lengths[0], group_tok)
    live_col = lax.dynamic_slice_in_dim(live, seq_place * local, local)[:, None]
    taps = lax.dynamic_slice_in_dim(conv_weight.astype(f32).reshape(3 * CONV, full_width), odd * width, width, 1)
    gain_h = head_gain.astype(f32)[None]
    gain_one = attn_norm_gain.astype(f32)[None]
    gain_two = ffn_norm_gain.astype(f32)[None]

    hidden_own, d_ffo_own = on_core(
        functools.partial(first_kernel, dp_parts), "first_norm", (rows_b16,) * 2, core, tokens, gain_one, cotangent, live_col
    )
    hidden_twin = twin_rows(hidden_own)
    reset_twin = twin_rows(reset_own)
    pad = jnp.zeros((extra - heads, w_strength.shape[0]), bf16)
    strength_t = w_strength.T
    strength_rows = jnp.concatenate([strength_t[:heads], pad, strength_t[heads:], pad], axis=0)
    mix_in = line_pack(
        (w_query.T, w_key.T, w_value.T, strength_rows, w_output), lines, hidden_twin, reset_twin
    )
    near_hidden = seq_relayed(hidden_own, True)
    far_hidden = seq_relayed(hidden_twin, False)
    reset = jnp.concatenate([reset_own, reset_twin])
    mix_near = after(mix_in, tuple(near_hidden), tuple(far_hidden))
    mix_packs = (mix_near, twin(mix_near))
    o_first = 3 * width + extra

    d_ffo_twin = twin_rows(after(d_ffo_own, mix_packs[1]))
    hidden_0, x_0, logit_0 = mix_product(lines, near_hidden, mix_packs, 3 * width, extra)
    late_cot = after(jnp.concatenate([d_ffo_own, d_ffo_twin], axis=0), x_0)
    ffn_in = line_pack((w_gate.T, w_up.T, w_down), lines, late_cot)
    cots_all = lax.all_gather(late_cot, "seq", axis=0, tiled=True)
    hidden_1, x_1, logit_1 = mix_product(lines, after(tuple(far_hidden), late_cot), mix_packs, 3 * width, extra)
    normed, mixed, kept = delta_forward(per, reset, place, (x_0, x_1), (logit_0, logit_1), taps, gain_h)
    o_span = ((o_first, width),)
    far_chunks, near_chunks = team_product(lines, ((normed[1],), (normed[0],)), o_span, mix_packs, seq_parts)
    far_sum = summed(returned(far_chunks)).astype(bf16)
    near_got = returned(near_chunks)
    resid, second_own = on_core(
        functools.partial(middle_kernel, dp_parts),
        "middle_norm",
        (rows_f32, rows_b16),
        core,
        tokens,
        gain_two,
        *near_got,
        twin_rows(far_sum),
    )
    second_twin = twin_rows(second_own)
    near_second = seq_pieces(second_own)
    far_second = seq_pieces(second_twin)
    ffn_near = after(ffn_in, second_own)
    ffn_packs = (ffn_near, twin(ffn_near))
    s_0, f_0, act_0, d_gate_0, d_up_0, *near_chunks = ffn_part(lines, 0, place, near_second, cots_all, ffn_packs)
    near_got = returned(near_chunks)
    far_second = after(tuple(far_second), near_chunks[0])
    s_1, f_1, act_1, d_gate_1, d_up_1, *far_chunks = ffn_part(lines, 1, place, far_second, cots_all, ffn_packs)
    acts, d_gates, d_ups, far_chunks = lax.optimization_barrier(
        ((act_0, act_1), (d_gate_0, d_gate_1), (d_up_0, d_up_1), tuple(far_chunks), tuple(near_got))
    )[:4]
    far_got = returned(far_chunks)

    def kept_sum(lefts, rights):
        def product(first, kind):
            return (
                dot(lefts[0], rights[0][:, first : first + side], TN)
                + dot(lefts[1], rights[1][:, first : first + side], TN)
            ).astype(kind)

        return product(0, bf16), product(side, bf16)

    seconds, cots = (s_0, s_1), (f_0, f_1)
    gate_kept, gate_sent = kept_sum(d_gates, seconds)
    up_kept, up_sent = kept_sum(d_ups, seconds)
    down_kept, down_sent = kept_sum(acts, cots)
    far_got = after(tuple(far_got), gate_sent, up_sent, down_sent)
    far_sum = summed(far_got).astype(bf16)
    back = twin_rows(far_sum)
    ffn_cut = line_cut(
        lines, (gate_kept, up_kept, down_kept), after((twin(gate_sent), twin(up_sent), twin(down_sent)), far_sum)
    )
    back = after(back, ffn_cut)
    d_resid, d_branch_own, grad_gain_two = on_core(
        functools.partial(back_kernel, dp_parts),
        "middle_back",
        (rows_f32, rows_b16, gain_f32),
        core,
        resid,
        gain_two,
        cotangent,
        live_col,
        *near_got,
        back,
    )
    d_branch_twin = twin_rows(d_branch_own)
    near_branch = seq_pieces(d_branch_own)
    far_branch = seq_pieces(d_branch_twin)
    ffn_back = line_exchange(after(ffn_cut, d_branch_twin))
    final = finish_product(
        lines, place, after((act_0, act_1), d_branch_own), (2 * units, units), ffn_packs, seq_parts
    )
    far_branch = after(tuple(far_branch), final)
    near_branch = after(tuple(near_branch), far_branch)
    b_0, d_normed_0 = branch_back(lines, near_branch, mix_packs, o_first, width)
    b_1, d_normed_1 = branch_back(lines, far_branch, mix_packs, o_first, width)
    final_sums = lax.psum_scatter(after(final, d_normed_0, d_normed_1), "seq", scatter_dimension=0, tiled=True)
    (d_x_0, d_x_1), d_taps, grad_head = delta_backward(
        per,
        reset,
        place,
        (x_0, x_1),
        (logit_0, logit_1),
        taps,
        gain_h,
        mixed,
        (d_normed_0, d_normed_1),
        kept,
    )
    x_kept, x_sent = kept_sum((d_x_0, d_x_1), (hidden_0, hidden_1))
    x_got = twin(x_sent)
    o_kept, o_sent = kept_sum(normed, after((b_0, b_1), x_sent))
    o_got = twin(o_sent)
    d_x_0, d_x_1 = lax.optimization_barrier((d_x_0, d_x_1, x_sent, x_kept, o_sent, o_kept))[:2]
    x_span = ((0, 3 * width + extra),)
    far_chunks, near_chunks = team_product(lines, ((d_x_1,), (d_x_0,)), x_span, mix_packs, seq_parts)
    far_got = returned(far_chunks)
    near_got = returned(near_chunks)
    grad_gate, grad_up, grad_down = line_total(
        ffn_back, lines, ((0, units), (units, units), (2 * units, units))
    )
    mix_cut = line_cut(lines, (x_kept, o_kept), after((x_got, o_got), near_chunks[0], grad_gate, grad_up, grad_down))
    mix_back = line_exchange(mix_cut)
    mix_spans = (
        (0, width),
        (width, width),
        (2 * width, width),
        (3 * width, heads),
        (o_first, width),
    )
    grad_query, grad_key, grad_value, grad_strength, grad_out = line_total(mix_back, lines, mix_spans)
    far_sum = summed(after(tuple(far_got), mix_cut, tuple(near_got))).astype(bf16)
    back = twin_rows(far_sum)
    final_twin = twin_rows(after(final_sums, far_sum)[local:])
    output = on_core(
        functools.partial(finish_kernel, dp_parts),
        "finish_rows",
        (rows_b16,),
        core,
        resid,
        live_col,
        final_sums[:local],
        final_twin,
    )[0]
    back = after(back, grad_query)
    input_grad, grad_gain_one = on_core(
        functools.partial(last_kernel, dp_parts),
        "last_norm",
        (rows_f32, gain_f32),
        core,
        tokens,
        gain_one,
        d_resid,
        *near_got,
        back,
    )
    early = jnp.zeros((3 * CONV, model), f32)
    early = lax.dynamic_update_slice_in_dim(early, d_taps, seq_place * full_width + odd * width, 1)
    gains = jnp.concatenate([grad_gain_one, grad_gain_two, early], axis=0).reshape(-1, DH)
    gains = all_sum(after(jnp.concatenate([gains, grad_head], axis=0), final_twin))
    wide = gains[:-1].reshape(-1, model)
    conv_grad = lax.dynamic_slice_in_dim(wide[2:], seq_place * full_width, full_width, 1)
    conv_grad = conv_grad.reshape(3, CONV, full_width)
    return (
        output,
        input_grad,
        wide[0],
        grad_query.T,
        grad_key.T,
        grad_value.T,
        grad_strength.T,
        conv_grad,
        gains[-1],
        grad_out,
        wide[1],
        grad_gate.T,
        grad_up.T,
        grad_down,
    )


def solution(mesh):
    placed = (
        P(("dp", "seq"), None),
        P("dp", None),
        P(("dp", "seq"), None),
        P(),
        P("dp", "seq"),
        P("dp", "seq"),
        P("dp", "seq"),
        P("dp", "seq"),
        P(None, None, "seq"),
        P(),
        P("seq", "dp"),
        P(),
        P("dp", "seq"),
        P("dp", "seq"),
        P("seq", "dp"),
    )
    return jax.shard_map(
        shards,
        mesh=mesh,
        in_specs=placed,
        out_specs=(
            P(("dp", "seq"), None),
            P(("dp", "seq"), None),
            P(),
            P("dp", "seq"),
            P("dp", "seq"),
            P("dp", "seq"),
            P("dp", "seq"),
            P(None, None, "seq"),
            P(),
            P("seq", "dp"),
            P(),
            P("dp", "seq"),
            P("dp", "seq"),
            P("seq", "dp"),
        ),
        check_vma=False,
    )
```

```python
import functools

import jax
import jax.numpy as jnp
from jax import lax
from jax.experimental import pallas as pl
from jax.experimental.pallas import tpu as pltpu
from jax.sharding import PartitionSpec as P

DH = 128
CONV = 4
SPAN = 64
HALO = 8
epsilon = 1e-06
f32 = jnp.float32
bf16 = jnp.bfloat16

NN = (((1,), (0,)), ((), ()))
NT = (((1,), (1,)), ((), ()))
TN = (((0,), (0,)), ((), ()))


def mm(left, right, dims=NN):
    return lax.dot_general(left.astype(bf16), right.astype(bf16), dims, preferred_element_type=f32)


def mm3(left, right, dims=NN):
    lh = left.astype(bf16)
    ll = (left - lh.astype(f32)).astype(bf16)
    rh = right.astype(bf16)
    rl = (right - rh.astype(f32)).astype(bf16)
    out = lax.dot_general(ll, rh, dims, preferred_element_type=f32)
    out = out + lax.dot_general(lh, rl, dims, preferred_element_type=f32)
    return out + lax.dot_general(lh, rh, dims, preferred_element_type=f32)


def tri_masks(rows):
    r = lax.broadcasted_iota(jnp.int32, (rows, rows), 0)
    c = lax.broadcasted_iota(jnp.int32, (rows, rows), 1)
    same = (r // SPAN) == (c // SPAN)
    return r, c, same


def unit_lower_inverse(lower, r, c):
    eye = (r == c).astype(f32)
    half = 1
    inverse = eye
    while half < SPAN:
        pair = ((r // (2 * half)) == (c // (2 * half))) & ((r // half) != (c // half))
        corner = jnp.where(pair, lower, 0.0)
        if half == 1:
            inverse = eye - corner
        else:
            inverse = inverse - mm(mm(inverse, corner), inverse)
        half *= 2
    resid = eye - inverse - mm3(lower, inverse)
    return inverse + mm(inverse, resid)


def rolled(block, halo_before, lag):
    if lag == 0:
        return block
    whole = jnp.concatenate([halo_before, block], axis=0)
    return pltpu.roll(whole, lag, 0)[HALO:]


def rolled_back(block, halo_after, lag):
    if lag == 0:
        return block
    whole = jnp.concatenate([block, halo_after], axis=0)
    return pltpu.roll(whole, whole.shape[0] - lag, 0)[: block.shape[0]]


def sigmoid(v):
    return 1.0 / (1.0 + jnp.exp(-v))


def row_start(place_ref, c, per):
    chunk = lax.div(c, per)
    return pl.multiple_of(((chunk ^ place_ref[0]) * per + lax.rem(c, per)) * SPAN, SPAN)


def conv_block(x_ref, conv_ref, start, before, keep, part, head, width):
    cols = pl.ds(part * width + head * DH, DH)
    block = x_ref[pl.ds(start, SPAN), cols].astype(f32)
    halo = x_ref[pl.ds(before, 16), cols].astype(f32)[16 - HALO :] * keep
    shifted = [rolled(block, halo, lag) for lag in range(CONV)]
    taps = [conv_ref[pl.ds(part * CONV + lag, 1), pl.ds(head * DH, DH)] for lag in range(CONV)]
    total = taps[0] * shifted[0]
    for lag in range(1, CONV):
        total = total + taps[lag] * shifted[lag]
    return total, shifted, taps


def strengths(logit_refs, start, heads):
    columns = []
    for logit_ref in logit_refs:
        block = sigmoid(logit_ref[pl.ds(start, SPAN), :]).astype(bf16).astype(f32)
        columns += [block[:, h : h + 1] for h in range(heads)]
    return jnp.concatenate(columns, axis=0)


def fwd_kernel(per, groups, reset_ref, place_ref, conv_ref, gain_ref, *refs):
    x_refs, logit_refs = refs[:groups], refs[groups : 2 * groups]
    normed_refs, mixed_refs = refs[2 * groups : 3 * groups], refs[3 * groups : 4 * groups]
    t_ref, s_ref, n_ref, q_s, k_s, u_s, w_s, p_s, state = refs[4 * groups :]
    length = x_refs[0].shape[0]
    width = x_refs[0].shape[1] // 3
    heads = width // DH
    blocks = length // SPAN
    pairs = [(g, h) for g in range(groups) for h in range(heads)]
    rows = len(pairs) * SPAN
    r, c_, same = tri_masks(rows)
    strict = same & (r > c_)
    incl = same & (r >= c_)

    def local_pair(i, carry):
        return local(2 * i + 1, local(2 * i, carry))

    def local(c, carry):
        start = row_start(place_ref, c, per)
        before = pl.multiple_of(row_start(place_ref, jnp.maximum(c - 1, 0), per) + (SPAN - 16), 16)
        parts = []
        for part in range(3):
            pieces = []
            for g, h in pairs:
                keep = 1.0 - reset_ref[g * blocks + c]
                z, _, _ = conv_block(x_refs[g], conv_ref, start, before, keep, part, h, width)
                pieces.append(z)
            z = jnp.concatenate(pieces, axis=0)
            parts.append(z * sigmoid(z))
        q, k, v = parts
        q = q * lax.rsqrt(jnp.sum(q * q, axis=-1, keepdims=True) + epsilon)
        k = k * lax.rsqrt(jnp.sum(k * k, axis=-1, keepdims=True) + epsilon)
        b = strengths(logit_refs, start, heads)
        gram = mm3(k, k, NT)
        lower = jnp.where(strict, gram * b, 0.0)
        inverse = unit_lower_inverse(lower, r, c_)
        p_s[c] = jnp.where(incl, mm(q, k, NT), 0.0).astype(bf16)
        t_ref[c] = inverse.astype(bf16)
        solved = mm(inverse, jnp.concatenate([b * k, b * v], axis=1))
        w_s[c] = solved[:, :DH].astype(bf16)
        u_s[c] = solved[:, DH:]
        q_s[c] = q.astype(bf16)
        k_s[c] = k.astype(bf16)
        return carry

    lax.fori_loop(0, blocks // 2, local_pair, 0)
    state[...] = jnp.zeros_like(state)
    gain = gain_ref[...]

    def scan(c, carry):
        start = row_start(place_ref, c, per)
        news = []
        reads = []
        for at, (g, h) in enumerate(pairs):
            keep = 1.0 - reset_ref[g * blocks + c]
            here = pl.ds(at * SPAN, SPAN)
            s = state[pl.ds(at * DH, DH), :] * keep
            low = s.astype(bf16)
            s_ref[c, pl.ds(at * DH, DH), :] = low
            both = jnp.concatenate([w_s[c, here, :], q_s[c, here, :]], axis=0)
            got = mm(both, low)
            fresh = u_s[c, here, :] - got[:SPAN]
            state[pl.ds(at * DH, DH), :] = s + mm(k_s[c, here, :], fresh, TN)
            news.append(fresh)
            reads.append(got[SPAN:])
        fresh = jnp.concatenate(news, axis=0).astype(bf16)
        n_ref[c] = fresh
        out = jnp.concatenate(reads, axis=0) + mm(p_s[c], fresh)
        mixed = out.astype(bf16)
        wide = mixed.astype(f32)
        normed = (wide * lax.rsqrt(jnp.mean(wide * wide, axis=-1, keepdims=True) + epsilon) * gain).astype(bf16)
        for at, (g, h) in enumerate(pairs):
            cols = pl.ds(h * DH, DH)
            mixed_refs[g][pl.ds(start, SPAN), cols] = mixed[at * SPAN : (at + 1) * SPAN]
            normed_refs[g][pl.ds(start, SPAN), cols] = normed[at * SPAN : (at + 1) * SPAN]
        return carry

    lax.fori_loop(0, blocks, scan, 0)


def delta_forward(per, reset, place, xs, logits, conv, gain):
    groups = len(xs)
    length = xs[0].shape[0]
    width = xs[0].shape[1] // 3
    heads = groups * (width // DH)
    blocks = length // SPAN
    rows = heads * SPAN
    shape = jax.ShapeDtypeStruct
    vmem = pl.BlockSpec(memory_space=pltpu.VMEM)
    smem = pl.BlockSpec(memory_space=pltpu.SMEM)
    out = pl.pallas_call(
        functools.partial(fwd_kernel, per, groups),
        out_shape=(shape((length, width), bf16),) * (2 * groups)
        + (
            shape((blocks, rows, rows), bf16),
            shape((blocks, heads * DH, DH), bf16),
            shape((blocks, rows, DH), bf16),
        ),
        in_specs=[smem, smem] + [vmem] * (2 + 2 * groups),
        out_specs=(vmem,) * (2 * groups + 3),
        scratch_shapes=[
            pltpu.VMEM((blocks, rows, DH), bf16),
            pltpu.VMEM((blocks, rows, DH), bf16),
            pltpu.VMEM((blocks, rows, DH), f32),
            pltpu.VMEM((blocks, rows, DH), bf16),
            pltpu.VMEM((blocks, rows, rows), bf16),
            pltpu.VMEM((heads * DH, DH), f32),
        ],
        name="delta_forward",
    )(reset, place, conv, gain, *xs, *logits)
    return out[:groups], out[groups : 2 * groups], out[2 * groups :]


def bwd_kernel(per, groups, reset_ref, place_ref, conv_ref, gain_ref, *refs):
    x_refs, logit_refs = refs[:groups], refs[groups : 2 * groups]
    mixed_refs, dnorm_refs = refs[2 * groups : 3 * groups], refs[3 * groups : 4 * groups]
    t_ref, s_ref, n_ref = refs[4 * groups : 4 * groups + 3]
    dx_refs = refs[4 * groups + 3 : 5 * groups + 3]
    dconv_ref, dgain_ref, q_s, k_s, v_s, iq_s, ik_s, do_s, g_s, kt_s, ds_s, dstate = refs[5 * groups + 3 :]
    length = x_refs[0].shape[0]
    width = x_refs[0].shape[1] // 3
    heads = width // DH
    blocks = length // SPAN
    pairs = [(g, h) for g in range(groups) for h in range(heads)]
    rows = len(pairs) * SPAN
    r, c_, same = tri_masks(rows)
    strict = same & (r > c_)
    incl = same & (r >= c_)
    gain = gain_ref[...]

    def stack(some, start):
        return jnp.concatenate([some[g][pl.ds(start, SPAN), pl.ds(h * DH, DH)] for g, h in pairs], axis=0)

    def local_pair(i, total):
        return local(2 * i + 1, local(2 * i, total))

    def local(c, total):
        start = row_start(place_ref, c, per)
        before = pl.multiple_of(row_start(place_ref, jnp.maximum(c - 1, 0), per) + (SPAN - 16), 16)
        parts = []
        for part in range(3):
            pieces = []
            for g, h in pairs:
                keep = 1.0 - reset_ref[g * blocks + c]
                z, _, _ = conv_block(x_refs[g], conv_ref, start, before, keep, part, h, width)
                pieces.append(z)
            z = jnp.concatenate(pieces, axis=0)
            parts.append(z * sigmoid(z))
        q, k, v = parts
        iq = lax.rsqrt(jnp.sum(q * q, axis=-1, keepdims=True) + epsilon)
        ik = lax.rsqrt(jnp.sum(k * k, axis=-1, keepdims=True) + epsilon)
        q = q * iq
        k = k * ik
        q_s[c] = q
        k_s[c] = k
        v_s[c] = v
        iq_s[c] = jnp.broadcast_to(iq, (rows, DH))
        ik_s[c] = jnp.broadcast_to(ik, (rows, DH))
        mixed = stack(mixed_refs, start).astype(f32)
        dnorm = stack(dnorm_refs, start)
        inv = lax.rsqrt(jnp.mean(mixed * mixed, axis=-1, keepdims=True) + epsilon)
        u = mixed * inv
        total = total + jnp.sum(dnorm * u, axis=0, keepdims=True)
        dg = dnorm * gain
        do = ((dg - u * jnp.mean(dg * u, axis=-1, keepdims=True)) * inv).astype(bf16)
        do_s[c] = do
        p = jnp.where(incl, mm(q, k, NT), 0.0)
        t = t_ref[c]
        pre = mm(p, do, TN)
        got = mm(t, jnp.concatenate([pre, k], axis=1), TN)
        g_s[c] = got[:, :DH]
        kt_s[c] = got[:, DH:].astype(bf16)
        return total

    dgain_ref[...] = lax.fori_loop(0, blocks // 2, local_pair, jnp.zeros((1, DH), f32))
    dstate[...] = jnp.zeros_like(dstate)

    def scan(i, carry):
        c = blocks - 1 - i
        start = row_start(place_ref, c, per)
        b = strengths(logit_refs, start, heads)
        k = k_s[c]
        bk = (b * k).astype(bf16)
        for at, (g_, h) in enumerate(pairs):
            keep = 1.0 - reset_ref[g_ * blocks + c]
            hr = pl.ds(at * SPAN, SPAN)
            ds = dstate[pl.ds(at * DH, DH), :]
            low = ds.astype(bf16)
            ds_s[c, pl.ds(at * DH, DH), :] = low
            g = g_s[c, hr, :] + mm(kt_s[c, hr, :], low)
            g_s[c, hr, :] = g
            ql = q_s[c, hr, :].astype(bf16)
            both = jnp.concatenate([ql, bk[at * SPAN : (at + 1) * SPAN]], axis=0)
            other = jnp.concatenate([do_s[c, hr, :], (-g).astype(bf16)], axis=0)
            dstate[pl.ds(at * DH, DH), :] = (ds + mm(both, other, TN)) * keep
        return carry

    lax.fori_loop(0, blocks, scan, 0)
    dconv_ref[...] = jnp.zeros_like(dconv_ref)
    extra = dx_refs[0].shape[1] - 3 * width
    lane = lax.broadcasted_iota(jnp.int32, (SPAN, extra), 1)

    def last(i, carry):
        c = blocks - 1 - i
        start = row_start(place_ref, c, per)
        before = pl.multiple_of(row_start(place_ref, jnp.maximum(c - 1, 0), per) + (SPAN - 16), 16)
        b = strengths(logit_refs, start, heads)
        q, k, v = q_s[c], k_s[c], v_s[c]
        g, n, do = g_s[c], n_ref[c], do_s[c]
        gl = g.astype(bf16)
        both = jnp.concatenate([do, gl], axis=0)
        outer = mm(both, n, NT)
        dp = jnp.where(incl, outer[:rows], 0.0).astype(bf16)
        da = jnp.where(strict, -outer[rows:], 0.0).astype(bf16)
        down = mm(jnp.concatenate([dp, da], axis=0), k)
        up = mm(jnp.concatenate([dp, da], axis=0), jnp.concatenate([q, b * k], axis=0), TN)
        sides = []
        nds = []
        for at in range(len(pairs)):
            s = s_ref[c, pl.ds(at * DH, DH), :]
            hr = slice(at * SPAN, (at + 1) * SPAN)
            sides.append(mm(jnp.concatenate([do[hr], gl[hr]], axis=0), s, NT))
            nds.append(mm(n[hr], ds_s[c, pl.ds(at * DH, DH), :], NT))
        dos = jnp.concatenate([x[:SPAN] for x in sides], axis=0)
        gs = jnp.concatenate([x[SPAN:] for x in sides], axis=0)
        dq = dos + down[:rows]
        y = down[rows:] - gs
        dk = up + jnp.concatenate(nds, axis=0) + b * y
        dv = b * g
        db = jnp.sum(k * y + v * g, axis=-1, keepdims=True)
        dq = (dq - q * jnp.sum(q * dq, axis=-1, keepdims=True)) * iq_s[c]
        dk = (dk - k * jnp.sum(k * dk, axis=-1, keepdims=True)) * ik_s[c]
        for g_ in range(groups):
            row = jnp.zeros((SPAN, extra), f32)
            for h in range(heads):
                at = g_ * heads + h
                row = jnp.where(lane == h, db[at * SPAN : (at + 1) * SPAN], row)
            sg = sigmoid(logit_refs[g_][pl.ds(start, SPAN), :])
            dl = (row.astype(bf16).astype(f32) * sg * (1.0 - sg)).astype(bf16)
            dx_refs[g_][pl.ds(start, SPAN), pl.ds(3 * width, extra)] = dl
        new_carry = []
        for part, grad in enumerate((dq, dk, dv)):
            for at, (g_, h) in enumerate(pairs):
                keep = 1.0 - reset_ref[g_ * blocks + c]
                z, shifted, taps = conv_block(x_refs[g_], conv_ref, start, before, keep, part, h, width)
                sz = sigmoid(z)
                dz = grad[at * SPAN : (at + 1) * SPAN] * (sz * (1.0 + z * (1.0 - sz)))
                rest = carry[part * len(pairs) + at]
                total = taps[0] * dz
                for lag in range(1, CONV):
                    total = total + taps[lag] * rolled_back(dz, rest, lag)
                dx_refs[g_][pl.ds(start, SPAN), pl.ds(part * width + h * DH, DH)] = total.astype(bf16)
                for lag in range(CONV):
                    spot = pl.ds(part * CONV + lag, 1), pl.ds(h * DH, DH)
                    dconv_ref[spot] = dconv_ref[spot] + jnp.sum(dz * shifted[lag], axis=0, keepdims=True)
                new_carry.append(dz[:HALO] * keep)
        return tuple(new_carry)

    zero = jnp.zeros((HALO, DH), f32)
    lax.fori_loop(0, blocks, last, (zero,) * (3 * len(pairs)))


def delta_backward(per, reset, place, xs, logits, conv, gain, mixeds, dnorms, kept):
    groups = len(xs)
    length = xs[0].shape[0]
    width = xs[0].shape[1] // 3
    extra = logits[0].shape[1]
    heads = groups * (width // DH)
    blocks = length // SPAN
    rows = heads * SPAN
    shape = jax.ShapeDtypeStruct
    vmem = pl.BlockSpec(memory_space=pltpu.VMEM)
    smem = pl.BlockSpec(memory_space=pltpu.SMEM)
    out = pl.pallas_call(
        functools.partial(bwd_kernel, per, groups),
        out_shape=(shape((length, 3 * width + extra), bf16),) * groups
        + (shape((3 * CONV, width), f32), shape((1, DH), f32)),
        in_specs=[smem, smem] + [vmem] * (2 + 4 * groups + 3),
        out_specs=(vmem,) * (groups + 2),
        scratch_shapes=[pltpu.VMEM((blocks, rows, DH), f32)] * 5
        + [
            pltpu.VMEM((blocks, rows, DH), bf16),
            pltpu.VMEM((blocks, rows, DH), f32),
            pltpu.VMEM((blocks, rows, DH), bf16),
            pltpu.VMEM((blocks, heads * DH, DH), bf16),
            pltpu.VMEM((heads * DH, DH), f32),
        ],
        name="delta_backward",
    )(reset, place, conv, gain, *xs, *logits, *mixeds, *dnorms, *kept)
    return out[:groups], out[groups], out[groups + 1]


def slot_of(block, core, parts):
    return ((block & 1) ^ core) * (parts // 2) + block // 2


def put_columns(values, out_ref, core, parts):
    depth = values.shape[1] // parts
    for block in range(parts):
        start = pl.multiple_of(slot_of(block, core, parts) * depth, depth)
        out_ref[:, pl.ds(start, depth)] = values[:, block * depth : (block + 1) * depth]


def column_sum(pieces, core, parts):
    depth = pieces[0].shape[1] // parts
    blocks = []
    for block in range(parts):
        start = pl.multiple_of(slot_of(block, core, parts) * depth, depth)
        total = pieces[0][:, pl.ds(start, depth)].astype(f32)
        for piece in pieces[1:]:
            total = total + piece[:, pl.ds(start, depth)].astype(f32)
        blocks.append(total)
    return jnp.concatenate(blocks, axis=1)


def on_core(kernel, name, shapes, core, *arrays):
    vmem = pl.BlockSpec(memory_space=pltpu.VMEM)
    smem = pl.BlockSpec(memory_space=pltpu.SMEM)
    return pl.pallas_call(
        kernel,
        out_shape=shapes,
        in_specs=[smem] + [vmem] * len(arrays),
        out_specs=(vmem,) * len(shapes),
        name=name,
    )(core, *arrays)


def first_kernel(parts, core_ref, gain_ref, x_ref, y_ref, hidden_ref, twin_ref):
    for rows_ref, out_ref in ((x_ref, hidden_ref), (y_ref, twin_ref)):
        x = rows_ref[...].astype(f32)
        scale = lax.rsqrt(jnp.mean(x * x, axis=-1, keepdims=True) + epsilon)
        put_columns((x * scale * gain_ref[...]).astype(bf16), out_ref, core_ref[0], parts)


def cot_kernel(parts, core_ref, x_ref, live_ref, y_ref, live_twin_ref, out_ref):
    rows = x_ref.shape[0]
    put_columns((x_ref[...].astype(f32) * live_ref[...]).astype(bf16), out_ref.at[:rows], core_ref[0], parts)
    put_columns((y_ref[...].astype(f32) * live_twin_ref[...]).astype(bf16), out_ref.at[rows:], core_ref[0], parts)


def middle_kernel(parts, core_ref, x_ref, gain_ref, *refs):
    pieces, (resid_ref, second_ref) = refs[:-2], refs[-2:]
    resid = x_ref[...].astype(f32) + column_sum(pieces, core_ref[0], parts)
    resid_ref[...] = resid
    scale = lax.rsqrt(jnp.mean(resid * resid, axis=-1, keepdims=True) + epsilon)
    put_columns((resid * scale * gain_ref[...]).astype(bf16), second_ref, core_ref[0], parts)


def norm_back(base, gain, grad):
    scale = lax.rsqrt(jnp.mean(base * base, axis=-1, keepdims=True) + epsilon)
    unit = base * scale
    d_unit = grad * gain
    d_base = (d_unit - unit * jnp.mean(d_unit * unit, axis=-1, keepdims=True)) * scale
    return d_base, jnp.sum(grad * unit, axis=0, keepdims=True)


def back_kernel(parts, core_ref, resid_ref, gain_ref, cot_ref, live_ref, *refs):
    pieces, (d_resid_ref, d_branch_ref, d_gain_ref) = refs[:-3], refs[-3:]
    d_norm, d_gain_ref[...] = norm_back(resid_ref[...], gain_ref[...], column_sum(pieces, core_ref[0], parts))
    d_resid = cot_ref[...].astype(f32) * live_ref[...] + d_norm
    d_resid_ref[...] = d_resid
    put_columns(d_resid.astype(bf16), d_branch_ref, core_ref[0], parts)


def last_kernel(parts, core_ref, x_ref, gain_ref, d_resid_ref, *refs):
    pieces, grad_ref = refs[:-1], refs[-1]
    d_norm, _ = norm_back(
        x_ref[...].astype(f32), gain_ref[...], column_sum(pieces, core_ref[0], parts)
    )
    grad_ref[...] = d_resid_ref[...] + d_norm


def finish_kernel(parts, core_ref, resid_ref, live_ref, *refs):
    pieces, out_ref = refs[:-1], refs[-1]
    out_ref[...] = ((resid_ref[...] + column_sum(pieces, core_ref[0], parts)) * live_ref[...]).astype(bf16)


def row_copies(pieces, whole, sems):
    rows = pieces[0].shape[0]
    return [
        pltpu.make_async_copy(piece, whole.at[pl.ds(j * rows, rows), :], sems.at[j])
        for j, piece in enumerate(pieces)
    ]


def weight_copies(packs, whole, sems, lines, first, units):
    depth = packs[0].shape[1]
    stride = packs[0].shape[0] // lines
    copies = []
    for side, pack in enumerate(packs):
        for k in range(lines):
            start = (side * lines + k) * depth
            copies.append(
                pltpu.make_async_copy(
                    pack.at[pl.ds(k * stride + first, units), :],
                    whole.at[:, pl.ds(start, depth)],
                    sems.at[side * lines + k],
                )
            )
    return copies


def started(copies):
    for copy in copies:
        copy.start()
    return copies


def waited(copies):
    for copy in copies:
        copy.wait()


def mix_kernel(lines, count, width, near, far, *refs):
    pieces, (rows_ref, x_ref, logit_ref, buf, row_sems, sems) = refs[:count], refs[count:]
    copies = started(row_copies(pieces, rows_ref, row_sems))
    copies += started(weight_copies((near, far), buf, sems, lines, 0, buf.shape[0]))
    waited(copies)
    out = lax.dot_general(rows_ref[...], buf[...], NT, preferred_element_type=f32)
    x_ref[...] = out[:, :width].astype(bf16)
    logit_ref[...] = out[:, width:]


def mix_product(lines, pieces, packs, width, extra):
    vmem = pl.BlockSpec(memory_space=pltpu.VMEM)
    smem = pl.BlockSpec(memory_space=pltpu.SMEM)
    hbm = pl.BlockSpec(memory_space=pl.ANY)
    tokens = pieces[0].shape[0] * len(pieces)
    model = pieces[0].shape[1]
    shape = jax.ShapeDtypeStruct
    return pl.pallas_call(
        functools.partial(mix_kernel, lines, len(pieces), width),
        out_shape=(shape((tokens, model), bf16), shape((tokens, width), bf16), shape((tokens, extra), f32)),
        in_specs=[hbm] * (2 + len(pieces)),
        out_specs=(vmem,) * 3,
        scratch_shapes=[
            pltpu.VMEM((width + extra, model), bf16),
            pltpu.SemaphoreType.DMA((len(pieces),)),
            pltpu.SemaphoreType.DMA((2 * lines,)),
        ],
        cost_estimate=pl.CostEstimate(
            flops=2 * tokens * model * (width + extra), bytes_accessed=2 * model * (2 * tokens + width), transcendentals=0
        ),
        name="mix_product",
    )(*packs, *pieces)


def branch_kernel(lines, count, first, near, far, *refs):
    pieces, (rows_ref, out_ref, buf, row_sems, sems) = refs[:count], refs[count:]
    copies = started(row_copies(pieces, rows_ref, row_sems))
    copies += started(weight_copies((near, far), buf, sems, lines, first, buf.shape[0]))
    waited(copies)
    out_ref[...] = lax.dot_general(rows_ref[...], buf[...], NT, preferred_element_type=f32)


def branch_back(lines, pieces, packs, first, units):
    vmem = pl.BlockSpec(memory_space=pltpu.VMEM)
    smem = pl.BlockSpec(memory_space=pltpu.SMEM)
    hbm = pl.BlockSpec(memory_space=pl.ANY)
    tokens = pieces[0].shape[0] * len(pieces)
    model = pieces[0].shape[1]
    shape = jax.ShapeDtypeStruct
    return pl.pallas_call(
        functools.partial(branch_kernel, lines, len(pieces), first),
        out_shape=(shape((tokens, model), bf16), shape((tokens, units), f32)),
        in_specs=[hbm] * (2 + len(pieces)),
        out_specs=(vmem,) * 2,
        scratch_shapes=[
            pltpu.VMEM((units, model), bf16),
            pltpu.SemaphoreType.DMA((len(pieces),)),
            pltpu.SemaphoreType.DMA((2 * lines,)),
        ],
        cost_estimate=pl.CostEstimate(
            flops=2 * tokens * model * units, bytes_accessed=2 * model * (2 * tokens + units), transcendentals=0
        ),
        name="branch_back",
    )(*packs, *pieces)


def ffn_kernel(lines, count, half, seq_ref, near, far, cots, *refs):
    seconds = refs[:count]
    s_ref, f_ref, act_ref, dgate_ref, dup_ref = refs[count : count + 5]
    chunk_refs, (bufs, row_sems, sems) = refs[count + 5 : 2 * count + 5], refs[2 * count + 5 :]
    rows = seconds[0].shape[0]
    units = act_ref.shape[1]
    first = started(row_copies(seconds, s_ref, row_sems.at[0]))
    weights = []
    for j in range(3):
        weights.append(
            started(weight_copies((near, far), bufs.at[j], sems.at[j], lines, j * units, units))
        )
    later = []
    for j in range(count):
        start = pl.multiple_of(((seq_ref[0] ^ j) * 2 + half) * rows, rows)
        later.append(
            pltpu.make_async_copy(
                cots.at[pl.ds(start, rows), :], f_ref.at[pl.ds(j * rows, rows), :], row_sems.at[1, j]
            )
        )
    started(later)
    waited(first + weights[0])
    gate = lax.dot_general(s_ref[...], bufs[0], NT, preferred_element_type=f32)
    waited(weights[1])
    upper = lax.dot_general(s_ref[...], bufs[1], NT, preferred_element_type=f32)
    sg = sigmoid(gate)
    soft = gate * sg
    act_ref[...] = (soft * upper).astype(bf16)
    slope = upper * (sg * (1.0 + gate * (1.0 - sg)))
    waited(later + weights[2])
    d_act = lax.dot_general(f_ref[...], bufs[2], NT, preferred_element_type=f32)
    d_gate = (d_act * slope).astype(bf16)
    d_up = (d_act * soft).astype(bf16)
    dgate_ref[...] = d_gate
    dup_ref[...] = d_up
    tile = s_ref.shape[1] // 4
    for t in range(4):
        cols = slice(t * tile, (t + 1) * tile)
        out = lax.dot_general(d_gate, bufs[0, :, cols], NN, preferred_element_type=f32)
        out = out + lax.dot_general(d_up, bufs[1, :, cols], NN, preferred_element_type=f32)
        for j, chunk in enumerate(chunk_refs):
            chunk[:, cols] = out[j * rows : (j + 1) * rows].astype(bf16)


def ffn_part(lines, half, seq, seconds, cots, packs):
    vmem = pl.BlockSpec(memory_space=pltpu.VMEM)
    smem = pl.BlockSpec(memory_space=pltpu.SMEM)
    hbm = pl.BlockSpec(memory_space=pl.ANY)
    count = len(seconds)
    tokens = seconds[0].shape[0] * count
    model = seconds[0].shape[1]
    units = packs[0].shape[0] // (3 * lines)
    shape = jax.ShapeDtypeStruct
    return pl.pallas_call(
        functools.partial(ffn_kernel, lines, count, half),
        out_shape=(shape((tokens, model), bf16),) * 2
        + (shape((tokens, units), bf16),) * 3
        + (shape((tokens // count, model), bf16),) * count,
        in_specs=[smem] + [hbm] * (3 + count),
        out_specs=(vmem,) * (5 + count),
        scratch_shapes=[
            pltpu.VMEM((3, units, model), bf16),
            pltpu.SemaphoreType.DMA((2, count)),
            pltpu.SemaphoreType.DMA((3, 2 * lines)),
        ],
        cost_estimate=pl.CostEstimate(
            flops=10 * tokens * units * model, bytes_accessed=6 * units * model + 8 * tokens * model, transcendentals=tokens * units
        ),
        name="ffn_part",
    )(seq, *packs, cots, *seconds)


def product_kernel(halves, spans, steps, fold, stride, count, gains, *refs):
    terms = len(spans)
    lefts = refs[: halves * terms]
    near_ref, far_ref = refs[halves * terms : halves * terms + 2]
    unit_refs = refs[halves * terms + 2 : halves * terms + 2 + gains]
    outs = refs[halves * terms + 2 + gains :]
    step = pl.program_id(0)
    rows = outs[0].shape[0]
    depth = near_ref.shape[1]

    def run(pack):
        if gains:
            outs[-1][...] = jnp.zeros_like(outs[-1])
        for half in range(halves):
            for k in range(fold):
                total = None
                for left, (first, units) in zip(lefts[half * terms : (half + 1) * terms], spans):
                    at = k * stride + first
                    part = lax.dot_general(left[...], pack[at : at + units, :], NN, preferred_element_type=f32)
                    total = part if total is None else total + part
                cols = slice(k * depth, (k + 1) * depth)
                if gains:
                    unit = unit_refs[half][:, cols].astype(f32)
                    outs[-1][:, cols] = outs[-1][:, cols] + jnp.sum(total * unit, axis=0, keepdims=True)
                for j in range(count):
                    outs[half * count + j][:, cols] = total[j * rows : (j + 1) * rows].astype(bf16)

    @pl.when(step < steps)
    def _():
        run(near_ref)

    @pl.when(step >= steps)
    def _():
        run(far_ref)


def team_product(lines, lefts, spans, packs, count, units=()):
    halves = len(lefts)
    flat = [left for half in lefts for left in half]
    tokens = flat[0].shape[0]
    fold = 2
    stride = packs[0].shape[0] // lines
    depth = packs[0].shape[1]
    steps = lines // fold
    rows = tokens // count
    inner = sum(n for _, n in spans)
    tile = pl.BlockSpec((tokens, fold * depth), lambda t: (0, t))
    total = pl.BlockSpec((1, fold * depth), lambda t: (0, t))
    out = pl.pallas_call(
        functools.partial(product_kernel, halves, spans, steps, fold, stride, count, len(units)),
        grid=(2 * steps,),
        in_specs=[pl.BlockSpec(left.shape, lambda t: (0, 0)) for left in flat]
        + [
            pl.BlockSpec((fold * stride, depth), lambda t: (jnp.minimum(t, steps - 1), 0)),
            pl.BlockSpec((fold * stride, depth), lambda t: (jnp.maximum(t - steps, 0), 0)),
        ]
        + [tile] * len(units),
        out_specs=[pl.BlockSpec((rows, fold * depth), lambda t: (0, t))] * (count * halves)
        + [total] * (len(units) > 0),
        out_shape=[jax.ShapeDtypeStruct((rows, 2 * lines * depth), bf16)] * (count * halves)
        + [jax.ShapeDtypeStruct((1, 2 * lines * depth), f32)] * (len(units) > 0),
        cost_estimate=pl.CostEstimate(
            flops=4 * halves * tokens * inner * lines * depth,
            bytes_accessed=4 * stride * lines * depth + 4 * halves * tokens * lines * depth,
            transcendentals=0,
        ),
        name="team_product",
    )(*flat, *packs, *units)
    return [out[half * count : (half + 1) * count] for half in range(halves)] + list(out[halves * count :])


def finish_product_kernel(halves, first, units, steps, fold, stride, count, seq_ref, *refs):
    lefts = refs[:halves]
    near_ref, far_ref, out_ref = refs[halves:]
    step = pl.program_id(0)
    rows = lefts[0].shape[0] // count
    depth = near_ref.shape[1]

    def run(pack):
        for half, left in enumerate(lefts):
            for k in range(fold):
                at = k * stride + first
                total = lax.dot_general(left[...], pack[at : at + units, :], NN, preferred_element_type=f32)
                for j in range(count):
                    start = pl.multiple_of(((seq_ref[0] ^ j) * halves + half) * rows, rows)
                    out_ref[pl.ds(start, rows), k * depth : (k + 1) * depth] = total[j * rows : (j + 1) * rows].astype(bf16)

    @pl.when(step < steps)
    def _():
        run(near_ref)

    @pl.when(step >= steps)
    def _():
        run(far_ref)


def finish_product(lines, seq, lefts, span, packs, count):
    first, units = span
    tokens = lefts[0].shape[0]
    fold = 2
    stride = packs[0].shape[0] // lines
    depth = packs[0].shape[1]
    steps = lines // fold
    whole = tokens * len(lefts)
    grid_spec = pltpu.PrefetchScalarGridSpec(
        num_scalar_prefetch=1,
        grid=(2 * steps,),
        in_specs=[pl.BlockSpec(left.shape, lambda t, s: (0, 0)) for left in lefts]
        + [
            pl.BlockSpec((fold * stride, depth), lambda t, s: (jnp.minimum(t, steps - 1), 0)),
            pl.BlockSpec((fold * stride, depth), lambda t, s: (jnp.maximum(t - steps, 0), 0)),
        ],
        out_specs=pl.BlockSpec((whole, fold * depth), lambda t, s: (0, t)),
    )
    return pl.pallas_call(
        functools.partial(finish_product_kernel, len(lefts), first, units, steps, fold, stride, count),
        grid_spec=grid_spec,
        out_shape=jax.ShapeDtypeStruct((whole, 2 * lines * depth), bf16),
        cost_estimate=pl.CostEstimate(
            flops=4 * whole * units * lines * depth,
            bytes_accessed=4 * stride * lines * depth + 4 * whole * lines * depth,
            transcendentals=0,
        ),
        name="finish_product",
    )(seq, *lefts, *packs)


def cut_kernel(lines, count, *refs):
    kept, got, out_ref = refs[:count], refs[count : 2 * count], refs[2 * count]
    depth = out_ref.shape[1]
    stride = out_ref.shape[0] // lines
    first = 0
    for left, right in zip(kept, got):
        rows = left.shape[0]
        for k in range(lines):
            cols = slice(k * depth, (k + 1) * depth)
            out_ref[k * stride + first : k * stride + first + rows, :] = (
                left[:, cols].astype(f32) + right[:, cols].astype(f32)
            ).astype(bf16)
        first += rows


def line_cut(lines, kept, got):
    vmem = pl.BlockSpec(memory_space=pltpu.VMEM)
    rows = sum(left.shape[0] for left in kept)
    return pl.pallas_call(
        functools.partial(cut_kernel, lines, len(kept)),
        out_shape=jax.ShapeDtypeStruct((lines * rows, kept[0].shape[1] // lines), bf16),
        in_specs=[vmem] * (2 * len(kept)),
        out_specs=vmem,
        name="line_cut",
    )(*kept, *got)


def rms_scale(value, gain):
    return value * lax.rsqrt(jnp.mean(value * value, axis=-1, keepdims=True) + epsilon) * gain


def segment_tables(lengths_row, group_tok):
    offsets = jnp.cumsum(lengths_row) - lengths_row
    total = jnp.sum(lengths_row)
    starts = jnp.concatenate([offsets, total[None]])
    block_first = jnp.arange(group_tok // SPAN, dtype=jnp.int32) * SPAN
    reset = jnp.any(block_first[:, None] == starts[None, :], axis=1).astype(f32)
    live = (jnp.arange(group_tok, dtype=jnp.int32) < total).astype(f32)
    return reset, live


def swap(values, axis, mask):
    size = lax.axis_size(axis)
    return lax.ppermute(values, axis, [(i, i ^ mask) for i in range(size)])


def dot(left, right, dims, kind=f32):
    return lax.dot_general(left, right, dims, preferred_element_type=f32).astype(kind)


def after(values, *others):
    return lax.optimization_barrier((values, *others))[0]


def added(first, second):
    return (first.astype(f32) + second.astype(f32)).astype(bf16)


def seq_pieces(values):
    return [values] + [swap(values, "seq", k) for k in range(1, lax.axis_size("seq"))]


def seq_relayed(values, upward):
    pieces = [values]
    for k in range(1, lax.axis_size("seq")):
        hop = 1 << (k.bit_length() - 1) if upward else k & -k
        pieces.append(swap(pieces[k ^ hop], "seq", hop))
    return pieces


def twin_rows(values):
    return swap(values, "dp", 2)


def returned(chunks):
    return [chunks[0]] + [swap(chunks[j], "seq", j) for j in range(1, len(chunks))]


def summed(pieces):
    total = pieces[0].astype(f32)
    for piece in pieces[1:]:
        total = total + piece.astype(f32)
    return total


def halves_of(arrays, half):
    picked = []
    for array in arrays:
        rows = array.shape[0] // 2
        picked.append(array[half * rows : (half + 1) * rows])
    return jnp.concatenate(picked, axis=0)


def line_exchange(values):
    dp_parts = lax.axis_size("dp")
    groups = [list(range(c, dp_parts, 2)) for c in (0, 1)]
    return lax.all_to_all(values, "dp", 0, 0, tiled=True, axis_index_groups=groups)


def line_pack(arrays, lines, *others):
    both = jnp.concatenate([halves_of(arrays, 0), halves_of(arrays, 1)], axis=0)
    return line_exchange(after(jnp.concatenate([both] * (lines // 2), axis=0), *others))


def line_total(pieces, lines, spans):
    rows = pieces.shape[0] // lines
    split = [pieces[k * rows : (k + 1) * rows] for k in range(lines)]
    low = summed(split[0::2])
    high = summed(split[1::2])
    return [
        jnp.concatenate([low[first : first + n], high[first : first + n]], axis=0) for first, n in spans
    ]


def doubled(values, axis):
    size = lax.axis_size(axis)
    mask = 1
    while mask < size:
        values = values + swap(values, axis, mask)
        mask *= 2
    return values


def chip_line_sum(values):
    values = summed([values] + [swap(values, "dp", k) for k in range(2, lax.axis_size("dp"), 2)])
    return values + swap(values, "dp", 1)


def group_sum(values):
    return summed([values] + [swap(values, "seq", k) for k in range(1, lax.axis_size("seq"))])


def shards(
    tokens,
    lengths,
    cotangent,
    attn_norm_gain,
    w_query,
    w_key,
    w_value,
    w_strength,
    conv_weight,
    head_gain,
    w_output,
    ffn_norm_gain,
    w_gate,
    w_up,
    w_down,
):
    local, model = tokens.shape
    seq_parts = lax.axis_size("seq")
    seq_place = lax.axis_index("seq")
    dp_parts = lax.axis_size("dp")
    dp_place = lax.axis_index("dp")
    lines = dp_parts // 2
    group_tok = local * seq_parts
    full_width = w_query.shape[1]
    full_heads = w_strength.shape[1]
    width = full_width // 2
    heads = full_heads // 2
    extra = 16
    units = w_gate.shape[1] // 2
    side = model // 2
    per = local // SPAN
    odd = dp_place >> 1 & 1

    def scalar(value):
        return jnp.full((1,), value, jnp.int32)

    def twin(values):
        return swap(values, "dp", 1)

    core = scalar(dp_place & 1)
    place = scalar(seq_place)
    rows_f32 = jax.ShapeDtypeStruct((local, model), f32)
    rows_b16 = jax.ShapeDtypeStruct((local, model), bf16)
    gain_f32 = jax.ShapeDtypeStruct((1, model), f32)

    reset_own, live = segment_tables(lengths[0], group_tok)
    live_col = lax.dynamic_slice_in_dim(live, seq_place * local, local)[:, None]
    taps = lax.dynamic_slice_in_dim(conv_weight.astype(f32).reshape(3 * CONV, full_width), odd * width, width, 1)
    gain_h = head_gain.astype(f32)[None]
    gain_one = attn_norm_gain.astype(f32)[None]
    gain_two = ffn_norm_gain.astype(f32)[None]

    tokens_twin = twin_rows(tokens)
    reset_twin = twin_rows(jnp.concatenate([reset_own, live]))
    cot_twin = twin_rows(cotangent)
    reset_twin, live_twin = reset_twin[: reset_own.shape[0]], reset_twin[reset_own.shape[0] :]
    live_twin_col = lax.dynamic_slice_in_dim(live_twin, seq_place * local, local)[:, None]
    hidden_own, hidden_twin = on_core(
        functools.partial(first_kernel, dp_parts), "first_norm", (rows_b16,) * 2, core, gain_one, tokens, tokens_twin
    )
    pad = jnp.zeros((extra - heads, w_strength.shape[0]), bf16)
    strength_t = w_strength.T
    strength_rows = jnp.concatenate([strength_t[:heads], pad, strength_t[heads:], pad], axis=0)
    mix_in = line_pack(
        (w_query.T, w_key.T, w_value.T, strength_rows, w_output), lines, tokens_twin, reset_twin, cot_twin
    )
    near_hidden = seq_relayed(hidden_own, True)
    far_hidden = seq_relayed(hidden_twin, False)
    reset = jnp.concatenate([reset_own, reset_twin])
    late_cot = on_core(
        functools.partial(cot_kernel, dp_parts),
        "live_rows",
        (jax.ShapeDtypeStruct((2 * local, model), bf16),),
        core,
        cotangent,
        live_col,
        cot_twin,
        live_twin_col,
    )[0]
    mix_near = after(mix_in, tuple(near_hidden), tuple(far_hidden))
    mix_packs = (mix_near, twin(after(mix_near, late_cot)))
    o_first = 3 * width + extra

    ffn_in = line_pack((w_gate.T, w_up.T, w_down), lines, mix_packs[1])
    cots_all = lax.all_gather(after(late_cot, mix_near), "seq", axis=0, tiled=True)
    hidden_0, x_0, logit_0 = mix_product(lines, near_hidden, mix_packs, 3 * width, extra)
    hidden_1, x_1, logit_1 = mix_product(lines, far_hidden, mix_packs, 3 * width, extra)
    normed, mixed, kept = delta_forward(per, reset, place, (x_0, x_1), (logit_0, logit_1), taps, gain_h)
    o_span = ((o_first, width),)
    far_chunks, near_chunks = team_product(lines, ((normed[1],), (normed[0],)), o_span, mix_packs, seq_parts)
    far_sum = summed(returned(far_chunks)).astype(bf16)
    near_got = returned(near_chunks)
    resid, second_own = on_core(
        functools.partial(middle_kernel, dp_parts),
        "middle_norm",
        (rows_f32, rows_b16),
        core,
        tokens,
        gain_two,
        *near_got,
        twin_rows(far_sum),
    )
    second_twin = twin_rows(second_own)
    near_second = seq_pieces(second_own)
    far_second = seq_pieces(second_twin)
    ffn_near = after(ffn_in, second_own)
    ffn_packs = (ffn_near, twin(ffn_near))
    s_0, f_0, act_0, d_gate_0, d_up_0, *near_chunks = ffn_part(lines, 0, place, near_second, cots_all, ffn_packs)
    near_got = returned(near_chunks)
    far_second = after(tuple(far_second), near_chunks[0])
    s_1, f_1, act_1, d_gate_1, d_up_1, *far_chunks = ffn_part(lines, 1, place, far_second, cots_all, ffn_packs)
    acts, d_gates, d_ups, far_chunks = lax.optimization_barrier(
        ((act_0, act_1), (d_gate_0, d_gate_1), (d_up_0, d_up_1), tuple(far_chunks), tuple(near_got))
    )[:4]
    far_got = returned(far_chunks)

    def kept_sum(lefts, rights):
        def product(first, kind):
            return (
                dot(lefts[0], rights[0][:, first : first + side], TN)
                + dot(lefts[1], rights[1][:, first : first + side], TN)
            ).astype(kind)

        return product(0, bf16), product(side, bf16)

    seconds, cots = (s_0, s_1), (f_0, f_1)
    gate_kept, gate_sent = kept_sum(d_gates, seconds)
    up_kept, up_sent = kept_sum(d_ups, seconds)
    down_kept, down_sent = kept_sum(acts, cots)
    far_got = after(tuple(far_got), gate_sent, up_sent, down_sent)
    far_sum = summed(far_got).astype(bf16)
    back = twin_rows(far_sum)
    ffn_cut = line_cut(
        lines, (gate_kept, up_kept, down_kept), after((twin(gate_sent), twin(up_sent), twin(down_sent)), far_sum)
    )
    back = after(back, ffn_cut)
    d_resid, d_branch_own, grad_gain_two = on_core(
        functools.partial(back_kernel, dp_parts),
        "middle_back",
        (rows_f32, rows_b16, gain_f32),
        core,
        resid,
        gain_two,
        cotangent,
        live_col,
        *near_got,
        back,
    )
    d_branch_twin = twin_rows(d_branch_own)
    near_branch = seq_pieces(d_branch_own)
    far_branch = seq_pieces(d_branch_twin)
    ffn_back = line_exchange(after(ffn_cut, d_branch_twin))
    final = finish_product(
        lines, place, after((act_0, act_1), d_branch_own), (2 * units, units), ffn_packs, seq_parts
    )
    far_branch = after(tuple(far_branch), final)
    near_branch = after(tuple(near_branch), far_branch)
    b_0, d_normed_0 = branch_back(lines, near_branch, mix_packs, o_first, width)
    b_1, d_normed_1 = branch_back(lines, far_branch, mix_packs, o_first, width)
    final_sums = lax.psum_scatter(after(final, tuple(far_branch), tuple(near_branch)), "seq", scatter_dimension=0, tiled=True)
    (d_x_0, d_x_1), d_taps, grad_head = delta_backward(
        per,
        reset,
        place,
        (x_0, x_1),
        (logit_0, logit_1),
        taps,
        gain_h,
        mixed,
        (d_normed_0, d_normed_1),
        kept,
    )
    x_span = ((0, 3 * width + extra),)
    far_chunks, near_chunks, gain_sum = team_product(
        lines, ((d_x_1,), (d_x_0,)), x_span, mix_packs, seq_parts, (hidden_1, hidden_0)
    )
    far_got = returned(far_chunks)
    near_got = returned(near_chunks)
    d_x_0, d_x_1 = after((d_x_0, d_x_1), gain_sum)
    x_kept, x_sent = kept_sum((d_x_0, d_x_1), (hidden_0, hidden_1))
    x_got = twin(x_sent)
    o_kept, o_sent = kept_sum(normed, after((b_0, b_1), x_sent))
    o_got = twin(o_sent)
    grad_gate, grad_up, grad_down = line_total(
        ffn_back, lines, ((0, units), (units, units), (2 * units, units))
    )
    by_core = gain_sum.reshape(2, lines, -1)
    by_core = jnp.where((dp_place & 1) == 1, by_core[::-1], by_core)
    grad_gain_one = by_core.transpose(1, 0, 2).reshape(1, model) / gain_one
    early = jnp.zeros((3 * CONV, model), f32)
    early = lax.dynamic_update_slice_in_dim(early, d_taps, seq_place * full_width + odd * width, 1)
    gains = jnp.concatenate([grad_gain_one, grad_gain_two, early], axis=0).reshape(-1, DH)
    gains = chip_line_sum(jnp.concatenate([gains, grad_head], axis=0))
    mix_cut = line_cut(lines, (x_kept, o_kept), after((x_got, o_got), gains, tuple(far_got), grad_gate, grad_up, grad_down))
    mix_back = line_exchange(mix_cut)
    mix_spans = (
        (0, width),
        (width, width),
        (2 * width, width),
        (3 * width, heads),
        (o_first, width),
    )
    grad_query, grad_key, grad_value, grad_strength, grad_out = line_total(mix_back, lines, mix_spans)
    far_sum = summed(after(tuple(far_got), mix_cut, tuple(near_got))).astype(bf16)
    back = twin_rows(far_sum)
    final_twin = twin_rows(after(final_sums, far_sum)[local:])
    output = on_core(
        functools.partial(finish_kernel, dp_parts),
        "finish_rows",
        (rows_b16,),
        core,
        resid,
        live_col,
        final_sums[:local],
        final_twin,
    )[0]
    back = after(back, grad_query)
    input_grad = on_core(
        functools.partial(last_kernel, dp_parts),
        "last_norm",
        (rows_f32,),
        core,
        tokens,
        gain_one,
        d_resid,
        *near_got,
        back,
    )[0]
    gains = group_sum(after(gains, far_sum))
    wide = gains[:-1].reshape(-1, model)
    conv_grad = lax.dynamic_slice_in_dim(wide[2:], seq_place * full_width, full_width, 1)
    conv_grad = conv_grad.reshape(3, CONV, full_width)
    return (
        output,
        input_grad,
        wide[0],
        grad_query.T,
        grad_key.T,
        grad_value.T,
        grad_strength.T,
        conv_grad,
        gains[-1],
        grad_out,
        wide[1],
        grad_gate.T,
        grad_up.T,
        grad_down,
    )


def solution(mesh):
    placed = (
        P(("dp", "seq"), None),
        P("dp", None),
        P(("dp", "seq"), None),
        P(),
        P("dp", "seq"),
        P("dp", "seq"),
        P("dp", "seq"),
        P("dp", "seq"),
        P(None, None, "seq"),
        P(),
        P("seq", "dp"),
        P(),
        P("dp", "seq"),
        P("dp", "seq"),
        P("seq", "dp"),
    )
    return jax.shard_map(
        shards,
        mesh=mesh,
        in_specs=placed,
        out_specs=(
            P(("dp", "seq"), None),
            P(("dp", "seq"), None),
            P(),
            P("dp", "seq"),
            P("dp", "seq"),
            P("dp", "seq"),
            P("dp", "seq"),
            P(None, None, "seq"),
            P(),
            P("seq", "dp"),
            P(),
            P("dp", "seq"),
            P("dp", "seq"),
            P("seq", "dp"),
        ),
        check_vma=False,
    )
```

```python
import functools

import jax
import jax.numpy as jnp
from jax import lax
from jax.experimental import pallas as pl
from jax.experimental.pallas import tpu as pltpu
from jax.sharding import PartitionSpec as P

DH = 128
CONV = 4
SPAN = 64
HALO = 8
epsilon = 1e-06
f32 = jnp.float32
bf16 = jnp.bfloat16

NN = (((1,), (0,)), ((), ()))
NT = (((1,), (1,)), ((), ()))
TN = (((0,), (0,)), ((), ()))


def mm(left, right, dims=NN):
    return lax.dot_general(left.astype(bf16), right.astype(bf16), dims, preferred_element_type=f32)


def mm3(left, right, dims=NN):
    lh = left.astype(bf16)
    ll = (left - lh.astype(f32)).astype(bf16)
    rh = right.astype(bf16)
    rl = (right - rh.astype(f32)).astype(bf16)
    out = lax.dot_general(ll, rh, dims, preferred_element_type=f32)
    out = out + lax.dot_general(lh, rl, dims, preferred_element_type=f32)
    return out + lax.dot_general(lh, rh, dims, preferred_element_type=f32)


def tri_masks(rows):
    r = lax.broadcasted_iota(jnp.int32, (rows, rows), 0)
    c = lax.broadcasted_iota(jnp.int32, (rows, rows), 1)
    same = (r // SPAN) == (c // SPAN)
    return r, c, same


def unit_lower_inverse(lower, r, c):
    eye = (r == c).astype(f32)
    half = 1
    inverse = eye
    while half < SPAN:
        pair = ((r // (2 * half)) == (c // (2 * half))) & ((r // half) != (c // half))
        corner = jnp.where(pair, lower, 0.0)
        if half == 1:
            inverse = eye - corner
        else:
            inverse = inverse - mm(mm(inverse, corner), inverse)
        half *= 2
    resid = eye - inverse - mm3(lower, inverse)
    return inverse + mm(inverse, resid)


def rolled(block, halo_before, lag):
    if lag == 0:
        return block
    whole = jnp.concatenate([halo_before, block], axis=0)
    return pltpu.roll(whole, lag, 0)[HALO:]


def rolled_back(block, halo_after, lag):
    if lag == 0:
        return block
    whole = jnp.concatenate([block, halo_after], axis=0)
    return pltpu.roll(whole, whole.shape[0] - lag, 0)[: block.shape[0]]


def sigmoid(v):
    return 1.0 / (1.0 + jnp.exp(-v))


def row_start(place_ref, c, per):
    chunk = lax.div(c, per)
    return pl.multiple_of(((chunk ^ place_ref[0]) * per + lax.rem(c, per)) * SPAN, SPAN)


def conv_block(x_ref, conv_ref, start, before, keep, part, head, width):
    cols = pl.ds(part * width + head * DH, DH)
    block = x_ref[pl.ds(start, SPAN), cols].astype(f32)
    halo = x_ref[pl.ds(before, 16), cols].astype(f32)[16 - HALO :] * keep
    shifted = [rolled(block, halo, lag) for lag in range(CONV)]
    taps = [conv_ref[pl.ds(part * CONV + lag, 1), pl.ds(head * DH, DH)] for lag in range(CONV)]
    total = taps[0] * shifted[0]
    for lag in range(1, CONV):
        total = total + taps[lag] * shifted[lag]
    return total, shifted, taps


def strengths(logit_refs, start, heads):
    columns = []
    for logit_ref in logit_refs:
        block = sigmoid(logit_ref[pl.ds(start, SPAN), :]).astype(bf16).astype(f32)
        columns += [block[:, h : h + 1] for h in range(heads)]
    return jnp.concatenate(columns, axis=0)


def fwd_kernel(per, groups, reset_ref, place_ref, conv_ref, gain_ref, *refs):
    x_refs, logit_refs = refs[:groups], refs[groups : 2 * groups]
    normed_refs, mixed_refs = refs[2 * groups : 3 * groups], refs[3 * groups : 4 * groups]
    t_ref, s_ref, n_ref, q_s, k_s, u_s, w_s, p_s, state = refs[4 * groups :]
    length = x_refs[0].shape[0]
    width = x_refs[0].shape[1] // 3
    heads = width // DH
    blocks = length // SPAN
    pairs = [(g, h) for g in range(groups) for h in range(heads)]
    rows = len(pairs) * SPAN
    r, c_, same = tri_masks(rows)
    strict = same & (r > c_)
    incl = same & (r >= c_)

    def local_pair(i, carry):
        return local(2 * i + 1, local(2 * i, carry))

    def local(c, carry):
        start = row_start(place_ref, c, per)
        before = pl.multiple_of(row_start(place_ref, jnp.maximum(c - 1, 0), per) + (SPAN - 16), 16)
        parts = []
        for part in range(3):
            pieces = []
            for g, h in pairs:
                keep = 1.0 - reset_ref[g * blocks + c]
                z, _, _ = conv_block(x_refs[g], conv_ref, start, before, keep, part, h, width)
                pieces.append(z)
            z = jnp.concatenate(pieces, axis=0)
            parts.append(z * sigmoid(z))
        q, k, v = parts
        q = q * lax.rsqrt(jnp.sum(q * q, axis=-1, keepdims=True) + epsilon)
        k = k * lax.rsqrt(jnp.sum(k * k, axis=-1, keepdims=True) + epsilon)
        b = strengths(logit_refs, start, heads)
        gram = mm3(k, k, NT)
        lower = jnp.where(strict, gram * b, 0.0)
        inverse = unit_lower_inverse(lower, r, c_)
        p_s[c] = jnp.where(incl, mm(q, k, NT), 0.0).astype(bf16)
        t_ref[c] = inverse.astype(bf16)
        solved = mm(inverse, jnp.concatenate([b * k, b * v], axis=1))
        w_s[c] = solved[:, :DH].astype(bf16)
        u_s[c] = solved[:, DH:]
        q_s[c] = q.astype(bf16)
        k_s[c] = k.astype(bf16)
        return carry

    lax.fori_loop(0, blocks // 2, local_pair, 0)
    state[...] = jnp.zeros_like(state)
    gain = gain_ref[...]

    def scan(c, carry):
        start = row_start(place_ref, c, per)
        news = []
        reads = []
        for at, (g, h) in enumerate(pairs):
            keep = 1.0 - reset_ref[g * blocks + c]
            here = pl.ds(at * SPAN, SPAN)
            s = state[pl.ds(at * DH, DH), :] * keep
            low = s.astype(bf16)
            s_ref[c, pl.ds(at * DH, DH), :] = low
            both = jnp.concatenate([w_s[c, here, :], q_s[c, here, :]], axis=0)
            got = mm(both, low)
            fresh = u_s[c, here, :] - got[:SPAN]
            state[pl.ds(at * DH, DH), :] = s + mm(k_s[c, here, :], fresh, TN)
            news.append(fresh)
            reads.append(got[SPAN:])
        fresh = jnp.concatenate(news, axis=0).astype(bf16)
        n_ref[c] = fresh
        out = jnp.concatenate(reads, axis=0) + mm(p_s[c], fresh)
        mixed = out.astype(bf16)
        wide = mixed.astype(f32)
        normed = (wide * lax.rsqrt(jnp.mean(wide * wide, axis=-1, keepdims=True) + epsilon) * gain).astype(bf16)
        for at, (g, h) in enumerate(pairs):
            cols = pl.ds(h * DH, DH)
            mixed_refs[g][pl.ds(start, SPAN), cols] = mixed[at * SPAN : (at + 1) * SPAN]
            normed_refs[g][pl.ds(start, SPAN), cols] = normed[at * SPAN : (at + 1) * SPAN]
        return carry

    lax.fori_loop(0, blocks, scan, 0)


def delta_forward(per, reset, place, xs, logits, conv, gain):
    groups = len(xs)
    length = xs[0].shape[0]
    width = xs[0].shape[1] // 3
    heads = groups * (width // DH)
    blocks = length // SPAN
    rows = heads * SPAN
    shape = jax.ShapeDtypeStruct
    vmem = pl.BlockSpec(memory_space=pltpu.VMEM)
    smem = pl.BlockSpec(memory_space=pltpu.SMEM)
    out = pl.pallas_call(
        functools.partial(fwd_kernel, per, groups),
        out_shape=(shape((length, width), bf16),) * (2 * groups)
        + (
            shape((blocks, rows, rows), bf16),
            shape((blocks, heads * DH, DH), bf16),
            shape((blocks, rows, DH), bf16),
        ),
        in_specs=[smem, smem] + [vmem] * (2 + 2 * groups),
        out_specs=(vmem,) * (2 * groups + 3),
        scratch_shapes=[
            pltpu.VMEM((blocks, rows, DH), bf16),
            pltpu.VMEM((blocks, rows, DH), bf16),
            pltpu.VMEM((blocks, rows, DH), f32),
            pltpu.VMEM((blocks, rows, DH), bf16),
            pltpu.VMEM((blocks, rows, rows), bf16),
            pltpu.VMEM((heads * DH, DH), f32),
        ],
        name="delta_forward",
    )(reset, place, conv, gain, *xs, *logits)
    return out[:groups], out[groups : 2 * groups], out[2 * groups :]


def bwd_kernel(per, groups, reset_ref, place_ref, conv_ref, gain_ref, *refs):
    x_refs, logit_refs = refs[:groups], refs[groups : 2 * groups]
    mixed_refs, dnorm_refs = refs[2 * groups : 3 * groups], refs[3 * groups : 4 * groups]
    t_ref, s_ref, n_ref = refs[4 * groups : 4 * groups + 3]
    dx_refs = refs[4 * groups + 3 : 5 * groups + 3]
    dconv_ref, dgain_ref, q_s, k_s, v_s, iq_s, ik_s, do_s, g_s, kt_s, ds_s, dstate = refs[5 * groups + 3 :]
    length = x_refs[0].shape[0]
    width = x_refs[0].shape[1] // 3
    heads = width // DH
    blocks = length // SPAN
    pairs = [(g, h) for g in range(groups) for h in range(heads)]
    rows = len(pairs) * SPAN
    r, c_, same = tri_masks(rows)
    strict = same & (r > c_)
    incl = same & (r >= c_)
    gain = gain_ref[...]

    def stack(some, start):
        return jnp.concatenate([some[g][pl.ds(start, SPAN), pl.ds(h * DH, DH)] for g, h in pairs], axis=0)

    def local_pair(i, total):
        return local(2 * i + 1, local(2 * i, total))

    def local(c, total):
        start = row_start(place_ref, c, per)
        before = pl.multiple_of(row_start(place_ref, jnp.maximum(c - 1, 0), per) + (SPAN - 16), 16)
        parts = []
        for part in range(3):
            pieces = []
            for g, h in pairs:
                keep = 1.0 - reset_ref[g * blocks + c]
                z, _, _ = conv_block(x_refs[g], conv_ref, start, before, keep, part, h, width)
                pieces.append(z)
            z = jnp.concatenate(pieces, axis=0)
            parts.append(z * sigmoid(z))
        q, k, v = parts
        iq = lax.rsqrt(jnp.sum(q * q, axis=-1, keepdims=True) + epsilon)
        ik = lax.rsqrt(jnp.sum(k * k, axis=-1, keepdims=True) + epsilon)
        q = q * iq
        k = k * ik
        q_s[c] = q
        k_s[c] = k
        v_s[c] = v
        iq_s[c] = jnp.broadcast_to(iq, (rows, DH))
        ik_s[c] = jnp.broadcast_to(ik, (rows, DH))
        mixed = stack(mixed_refs, start).astype(f32)
        dnorm = stack(dnorm_refs, start)
        inv = lax.rsqrt(jnp.mean(mixed * mixed, axis=-1, keepdims=True) + epsilon)
        u = mixed * inv
        total = total + jnp.sum(dnorm * u, axis=0, keepdims=True)
        dg = dnorm * gain
        do = ((dg - u * jnp.mean(dg * u, axis=-1, keepdims=True)) * inv).astype(bf16)
        do_s[c] = do
        p = jnp.where(incl, mm(q, k, NT), 0.0)
        t = t_ref[c]
        pre = mm(p, do, TN)
        got = mm(t, jnp.concatenate([pre, k], axis=1), TN)
        g_s[c] = got[:, :DH]
        kt_s[c] = got[:, DH:].astype(bf16)
        return total

    dgain_ref[...] = lax.fori_loop(0, blocks // 2, local_pair, jnp.zeros((1, DH), f32))
    dstate[...] = jnp.zeros_like(dstate)

    def scan(i, carry):
        c = blocks - 1 - i
        start = row_start(place_ref, c, per)
        b = strengths(logit_refs, start, heads)
        k = k_s[c]
        bk = (b * k).astype(bf16)
        for at, (g_, h) in enumerate(pairs):
            keep = 1.0 - reset_ref[g_ * blocks + c]
            hr = pl.ds(at * SPAN, SPAN)
            ds = dstate[pl.ds(at * DH, DH), :]
            low = ds.astype(bf16)
            ds_s[c, pl.ds(at * DH, DH), :] = low
            g = g_s[c, hr, :] + mm(kt_s[c, hr, :], low)
            g_s[c, hr, :] = g
            ql = q_s[c, hr, :].astype(bf16)
            both = jnp.concatenate([ql, bk[at * SPAN : (at + 1) * SPAN]], axis=0)
            other = jnp.concatenate([do_s[c, hr, :], (-g).astype(bf16)], axis=0)
            dstate[pl.ds(at * DH, DH), :] = (ds + mm(both, other, TN)) * keep
        return carry

    lax.fori_loop(0, blocks, scan, 0)
    dconv_ref[...] = jnp.zeros_like(dconv_ref)
    extra = dx_refs[0].shape[1] - 3 * width
    lane = lax.broadcasted_iota(jnp.int32, (SPAN, extra), 1)

    def last(i, carry):
        c = blocks - 1 - i
        start = row_start(place_ref, c, per)
        before = pl.multiple_of(row_start(place_ref, jnp.maximum(c - 1, 0), per) + (SPAN - 16), 16)
        b = strengths(logit_refs, start, heads)
        q, k, v = q_s[c], k_s[c], v_s[c]
        g, n, do = g_s[c], n_ref[c], do_s[c]
        gl = g.astype(bf16)
        both = jnp.concatenate([do, gl], axis=0)
        outer = mm(both, n, NT)
        dp = jnp.where(incl, outer[:rows], 0.0).astype(bf16)
        da = jnp.where(strict, -outer[rows:], 0.0).astype(bf16)
        down = mm(jnp.concatenate([dp, da], axis=0), k)
        up = mm(jnp.concatenate([dp, da], axis=0), jnp.concatenate([q, b * k], axis=0), TN)
        sides = []
        nds = []
        for at in range(len(pairs)):
            s = s_ref[c, pl.ds(at * DH, DH), :]
            hr = slice(at * SPAN, (at + 1) * SPAN)
            sides.append(mm(jnp.concatenate([do[hr], gl[hr]], axis=0), s, NT))
            nds.append(mm(n[hr], ds_s[c, pl.ds(at * DH, DH), :], NT))
        dos = jnp.concatenate([x[:SPAN] for x in sides], axis=0)
        gs = jnp.concatenate([x[SPAN:] for x in sides], axis=0)
        dq = dos + down[:rows]
        y = down[rows:] - gs
        dk = up + jnp.concatenate(nds, axis=0) + b * y
        dv = b * g
        db = jnp.sum(k * y + v * g, axis=-1, keepdims=True)
        dq = (dq - q * jnp.sum(q * dq, axis=-1, keepdims=True)) * iq_s[c]
        dk = (dk - k * jnp.sum(k * dk, axis=-1, keepdims=True)) * ik_s[c]
        for g_ in range(groups):
            row = jnp.zeros((SPAN, extra), f32)
            for h in range(heads):
                at = g_ * heads + h
                row = jnp.where(lane == h, db[at * SPAN : (at + 1) * SPAN], row)
            sg = sigmoid(logit_refs[g_][pl.ds(start, SPAN), :])
            dl = (row.astype(bf16).astype(f32) * sg * (1.0 - sg)).astype(bf16)
            dx_refs[g_][pl.ds(start, SPAN), pl.ds(3 * width, extra)] = dl
        new_carry = []
        for part, grad in enumerate((dq, dk, dv)):
            for at, (g_, h) in enumerate(pairs):
                keep = 1.0 - reset_ref[g_ * blocks + c]
                z, shifted, taps = conv_block(x_refs[g_], conv_ref, start, before, keep, part, h, width)
                sz = sigmoid(z)
                dz = grad[at * SPAN : (at + 1) * SPAN] * (sz * (1.0 + z * (1.0 - sz)))
                rest = carry[part * len(pairs) + at]
                total = taps[0] * dz
                for lag in range(1, CONV):
                    total = total + taps[lag] * rolled_back(dz, rest, lag)
                dx_refs[g_][pl.ds(start, SPAN), pl.ds(part * width + h * DH, DH)] = total.astype(bf16)
                for lag in range(CONV):
                    spot = pl.ds(part * CONV + lag, 1), pl.ds(h * DH, DH)
                    dconv_ref[spot] = dconv_ref[spot] + jnp.sum(dz * shifted[lag], axis=0, keepdims=True)
                new_carry.append(dz[:HALO] * keep)
        return tuple(new_carry)

    zero = jnp.zeros((HALO, DH), f32)
    lax.fori_loop(0, blocks, last, (zero,) * (3 * len(pairs)))


def delta_backward(per, reset, place, xs, logits, conv, gain, mixeds, dnorms, kept):
    groups = len(xs)
    length = xs[0].shape[0]
    width = xs[0].shape[1] // 3
    extra = logits[0].shape[1]
    heads = groups * (width // DH)
    blocks = length // SPAN
    rows = heads * SPAN
    shape = jax.ShapeDtypeStruct
    vmem = pl.BlockSpec(memory_space=pltpu.VMEM)
    smem = pl.BlockSpec(memory_space=pltpu.SMEM)
    out = pl.pallas_call(
        functools.partial(bwd_kernel, per, groups),
        out_shape=(shape((length, 3 * width + extra), bf16),) * groups
        + (shape((3 * CONV, width), f32), shape((1, DH), f32)),
        in_specs=[smem, smem] + [vmem] * (2 + 4 * groups + 3),
        out_specs=(vmem,) * (groups + 2),
        scratch_shapes=[pltpu.VMEM((blocks, rows, DH), f32)] * 5
        + [
            pltpu.VMEM((blocks, rows, DH), bf16),
            pltpu.VMEM((blocks, rows, DH), f32),
            pltpu.VMEM((blocks, rows, DH), bf16),
            pltpu.VMEM((blocks, heads * DH, DH), bf16),
            pltpu.VMEM((heads * DH, DH), f32),
        ],
        name="delta_backward",
    )(reset, place, conv, gain, *xs, *logits, *mixeds, *dnorms, *kept)
    return out[:groups], out[groups], out[groups + 1]


def slot_of(block, core, parts):
    return ((block & 1) ^ core) * (parts // 2) + block // 2


def put_columns(values, out_ref, core, parts):
    depth = values.shape[1] // parts
    for block in range(parts):
        start = pl.multiple_of(slot_of(block, core, parts) * depth, depth)
        out_ref[:, pl.ds(start, depth)] = values[:, block * depth : (block + 1) * depth]


def column_sum(pieces, core, parts):
    depth = pieces[0].shape[1] // parts
    blocks = []
    for block in range(parts):
        start = pl.multiple_of(slot_of(block, core, parts) * depth, depth)
        total = pieces[0][:, pl.ds(start, depth)].astype(f32)
        for piece in pieces[1:]:
            total = total + piece[:, pl.ds(start, depth)].astype(f32)
        blocks.append(total)
    return jnp.concatenate(blocks, axis=1)


def on_core(kernel, name, shapes, core, *arrays):
    vmem = pl.BlockSpec(memory_space=pltpu.VMEM)
    smem = pl.BlockSpec(memory_space=pltpu.SMEM)
    return pl.pallas_call(
        kernel,
        out_shape=shapes,
        in_specs=[smem] + [vmem] * len(arrays),
        out_specs=(vmem,) * len(shapes),
        name=name,
    )(core, *arrays)


def first_kernel(parts, core_ref, gain_ref, x_ref, y_ref, hidden_ref, twin_ref):
    for rows_ref, out_ref in ((x_ref, hidden_ref), (y_ref, twin_ref)):
        x = rows_ref[...].astype(f32)
        scale = lax.rsqrt(jnp.mean(x * x, axis=-1, keepdims=True) + epsilon)
        put_columns((x * scale * gain_ref[...]).astype(bf16), out_ref, core_ref[0], parts)


def cot_kernel(parts, core_ref, x_ref, live_ref, y_ref, live_twin_ref, out_ref):
    rows = x_ref.shape[0]
    put_columns((x_ref[...].astype(f32) * live_ref[...]).astype(bf16), out_ref.at[:rows], core_ref[0], parts)
    put_columns((y_ref[...].astype(f32) * live_twin_ref[...]).astype(bf16), out_ref.at[rows:], core_ref[0], parts)


def middle_kernel(parts, core_ref, x_ref, gain_ref, *refs):
    pieces, (resid_ref, second_ref) = refs[:-2], refs[-2:]
    resid = x_ref[...].astype(f32) + column_sum(pieces, core_ref[0], parts)
    resid_ref[...] = resid
    scale = lax.rsqrt(jnp.mean(resid * resid, axis=-1, keepdims=True) + epsilon)
    put_columns((resid * scale * gain_ref[...]).astype(bf16), second_ref, core_ref[0], parts)


def norm_back(base, gain, grad):
    scale = lax.rsqrt(jnp.mean(base * base, axis=-1, keepdims=True) + epsilon)
    unit = base * scale
    d_unit = grad * gain
    d_base = (d_unit - unit * jnp.mean(d_unit * unit, axis=-1, keepdims=True)) * scale
    return d_base, jnp.sum(grad * unit, axis=0, keepdims=True)


def back_kernel(parts, core_ref, resid_ref, gain_ref, cot_ref, live_ref, *refs):
    pieces, (d_resid_ref, d_branch_ref, d_gain_ref) = refs[:-3], refs[-3:]
    d_norm, d_gain_ref[...] = norm_back(resid_ref[...], gain_ref[...], column_sum(pieces, core_ref[0], parts))
    d_resid = cot_ref[...].astype(f32) * live_ref[...] + d_norm
    d_resid_ref[...] = d_resid
    put_columns(d_resid.astype(bf16), d_branch_ref, core_ref[0], parts)


def last_kernel(parts, core_ref, x_ref, gain_ref, d_resid_ref, *refs):
    pieces, grad_ref = refs[:-1], refs[-1]
    d_norm, _ = norm_back(
        x_ref[...].astype(f32), gain_ref[...], column_sum(pieces, core_ref[0], parts)
    )
    grad_ref[...] = d_resid_ref[...] + d_norm


def finish_kernel(parts, core_ref, resid_ref, live_ref, *refs):
    pieces, out_ref = refs[:-1], refs[-1]
    out_ref[...] = ((resid_ref[...] + column_sum(pieces, core_ref[0], parts)) * live_ref[...]).astype(bf16)


def row_copies(pieces, whole, sems):
    rows = pieces[0].shape[0]
    return [
        pltpu.make_async_copy(piece, whole.at[pl.ds(j * rows, rows), :], sems.at[j])
        for j, piece in enumerate(pieces)
    ]


def weight_copies(packs, whole, sems, lines, first, units):
    depth = packs[0].shape[1]
    stride = packs[0].shape[0] // lines
    copies = []
    for side, pack in enumerate(packs):
        for k in range(lines):
            start = (side * lines + k) * depth
            copies.append(
                pltpu.make_async_copy(
                    pack.at[pl.ds(k * stride + first, units), :],
                    whole.at[:, pl.ds(start, depth)],
                    sems.at[side * lines + k],
                )
            )
    return copies


def started(copies):
    for copy in copies:
        copy.start()
    return copies


def waited(copies):
    for copy in copies:
        copy.wait()


def mix_kernel(lines, count, width, near, far, *refs):
    pieces, (rows_ref, x_ref, logit_ref, buf, row_sems, sems) = refs[:count], refs[count:]
    copies = started(row_copies(pieces, rows_ref, row_sems))
    copies += started(weight_copies((near, far), buf, sems, lines, 0, buf.shape[0]))
    waited(copies)
    out = lax.dot_general(rows_ref[...], buf[...], NT, preferred_element_type=f32)
    x_ref[...] = out[:, :width].astype(bf16)
    logit_ref[...] = out[:, width:]


def mix_product(lines, pieces, packs, width, extra):
    vmem = pl.BlockSpec(memory_space=pltpu.VMEM)
    smem = pl.BlockSpec(memory_space=pltpu.SMEM)
    hbm = pl.BlockSpec(memory_space=pl.ANY)
    tokens = pieces[0].shape[0] * len(pieces)
    model = pieces[0].shape[1]
    shape = jax.ShapeDtypeStruct
    return pl.pallas_call(
        functools.partial(mix_kernel, lines, len(pieces), width),
        out_shape=(shape((tokens, model), bf16), shape((tokens, width), bf16), shape((tokens, extra), f32)),
        in_specs=[hbm] * (2 + len(pieces)),
        out_specs=(vmem,) * 3,
        scratch_shapes=[
            pltpu.VMEM((width + extra, model), bf16),
            pltpu.SemaphoreType.DMA((len(pieces),)),
            pltpu.SemaphoreType.DMA((2 * lines,)),
        ],
        cost_estimate=pl.CostEstimate(
            flops=2 * tokens * model * (width + extra), bytes_accessed=2 * model * (2 * tokens + width), transcendentals=0
        ),
        name="mix_product",
    )(*packs, *pieces)


def branch_kernel(lines, count, first, near, far, *refs):
    pieces, (rows_ref, out_ref, buf, row_sems, sems) = refs[:count], refs[count:]
    copies = started(row_copies(pieces, rows_ref, row_sems))
    copies += started(weight_copies((near, far), buf, sems, lines, first, buf.shape[0]))
    waited(copies)
    out_ref[...] = lax.dot_general(rows_ref[...], buf[...], NT, preferred_element_type=f32)


def branch_back(lines, pieces, packs, first, units):
    vmem = pl.BlockSpec(memory_space=pltpu.VMEM)
    smem = pl.BlockSpec(memory_space=pltpu.SMEM)
    hbm = pl.BlockSpec(memory_space=pl.ANY)
    tokens = pieces[0].shape[0] * len(pieces)
    model = pieces[0].shape[1]
    shape = jax.ShapeDtypeStruct
    return pl.pallas_call(
        functools.partial(branch_kernel, lines, len(pieces), first),
        out_shape=(shape((tokens, model), bf16), shape((tokens, units), f32)),
        in_specs=[hbm] * (2 + len(pieces)),
        out_specs=(vmem,) * 2,
        scratch_shapes=[
            pltpu.VMEM((units, model), bf16),
            pltpu.SemaphoreType.DMA((len(pieces),)),
            pltpu.SemaphoreType.DMA((2 * lines,)),
        ],
        cost_estimate=pl.CostEstimate(
            flops=2 * tokens * model * units, bytes_accessed=2 * model * (2 * tokens + units), transcendentals=0
        ),
        name="branch_back",
    )(*packs, *pieces)


def ffn_kernel(lines, count, half, seq_ref, near, far, cots, *refs):
    seconds = refs[:count]
    s_ref, f_ref, act_ref, dgate_ref, dup_ref = refs[count : count + 5]
    chunk_refs, (bufs, row_sems, sems) = refs[count + 5 : 2 * count + 5], refs[2 * count + 5 :]
    rows = seconds[0].shape[0]
    units = act_ref.shape[1]
    first = started(row_copies(seconds, s_ref, row_sems.at[0]))
    weights = []
    for j in range(3):
        weights.append(
            started(weight_copies((near, far), bufs.at[j], sems.at[j], lines, j * units, units))
        )
    later = []
    for j in range(count):
        start = pl.multiple_of(((seq_ref[0] ^ j) * 2 + half) * rows, rows)
        later.append(
            pltpu.make_async_copy(
                cots.at[pl.ds(start, rows), :], f_ref.at[pl.ds(j * rows, rows), :], row_sems.at[1, j]
            )
        )
    started(later)
    waited(first + weights[0])
    gate = lax.dot_general(s_ref[...], bufs[0], NT, preferred_element_type=f32)
    waited(weights[1])
    upper = lax.dot_general(s_ref[...], bufs[1], NT, preferred_element_type=f32)
    sg = sigmoid(gate)
    soft = gate * sg
    act_ref[...] = (soft * upper).astype(bf16)
    slope = upper * (sg * (1.0 + gate * (1.0 - sg)))
    waited(later + weights[2])
    d_act = lax.dot_general(f_ref[...], bufs[2], NT, preferred_element_type=f32)
    d_gate = (d_act * slope).astype(bf16)
    d_up = (d_act * soft).astype(bf16)
    dgate_ref[...] = d_gate
    dup_ref[...] = d_up
    tile = s_ref.shape[1] // 4
    for t in range(4):
        cols = slice(t * tile, (t + 1) * tile)
        out = lax.dot_general(d_gate, bufs[0, :, cols], NN, preferred_element_type=f32)
        out = out + lax.dot_general(d_up, bufs[1, :, cols], NN, preferred_element_type=f32)
        for j, chunk in enumerate(chunk_refs):
            chunk[:, cols] = out[j * rows : (j + 1) * rows].astype(bf16)


def ffn_part(lines, half, seq, seconds, cots, packs):
    vmem = pl.BlockSpec(memory_space=pltpu.VMEM)
    smem = pl.BlockSpec(memory_space=pltpu.SMEM)
    hbm = pl.BlockSpec(memory_space=pl.ANY)
    count = len(seconds)
    tokens = seconds[0].shape[0] * count
    model = seconds[0].shape[1]
    units = packs[0].shape[0] // (3 * lines)
    shape = jax.ShapeDtypeStruct
    return pl.pallas_call(
        functools.partial(ffn_kernel, lines, count, half),
        out_shape=(shape((tokens, model), bf16),) * 2
        + (shape((tokens, units), bf16),) * 3
        + (shape((tokens // count, model), bf16),) * count,
        in_specs=[smem] + [hbm] * (3 + count),
        out_specs=(vmem,) * (5 + count),
        scratch_shapes=[
            pltpu.VMEM((3, units, model), bf16),
            pltpu.SemaphoreType.DMA((2, count)),
            pltpu.SemaphoreType.DMA((3, 2 * lines)),
        ],
        cost_estimate=pl.CostEstimate(
            flops=10 * tokens * units * model, bytes_accessed=6 * units * model + 8 * tokens * model, transcendentals=tokens * units
        ),
        name="ffn_part",
    )(seq, *packs, cots, *seconds)


def product_kernel(halves, spans, steps, fold, stride, count, gains, *refs):
    terms = len(spans)
    lefts = refs[: halves * terms]
    near_ref, far_ref = refs[halves * terms : halves * terms + 2]
    unit_refs = refs[halves * terms + 2 : halves * terms + 2 + gains]
    outs = refs[halves * terms + 2 + gains :]
    step = pl.program_id(0)
    rows = outs[0].shape[0]
    depth = near_ref.shape[1]

    def run(pack):
        if gains:
            outs[-1][...] = jnp.zeros_like(outs[-1])
        for half in range(halves):
            for k in range(fold):
                total = None
                for left, (first, units) in zip(lefts[half * terms : (half + 1) * terms], spans):
                    at = k * stride + first
                    part = lax.dot_general(left[...], pack[at : at + units, :], NN, preferred_element_type=f32)
                    total = part if total is None else total + part
                cols = slice(k * depth, (k + 1) * depth)
                if gains:
                    unit = unit_refs[half][:, cols].astype(f32)
                    outs[-1][:, cols] = outs[-1][:, cols] + jnp.sum(total * unit, axis=0, keepdims=True)
                for j in range(count):
                    outs[half * count + j][:, cols] = total[j * rows : (j + 1) * rows].astype(bf16)

    @pl.when(step < steps)
    def _():
        run(near_ref)

    @pl.when(step >= steps)
    def _():
        run(far_ref)


def team_product(lines, lefts, spans, packs, count, units=()):
    halves = len(lefts)
    flat = [left for half in lefts for left in half]
    tokens = flat[0].shape[0]
    fold = 2
    stride = packs[0].shape[0] // lines
    depth = packs[0].shape[1]
    steps = lines // fold
    rows = tokens // count
    inner = sum(n for _, n in spans)
    tile = pl.BlockSpec((tokens, fold * depth), lambda t: (0, t))
    total = pl.BlockSpec((1, fold * depth), lambda t: (0, t))
    out = pl.pallas_call(
        functools.partial(product_kernel, halves, spans, steps, fold, stride, count, len(units)),
        grid=(2 * steps,),
        in_specs=[pl.BlockSpec(left.shape, lambda t: (0, 0)) for left in flat]
        + [
            pl.BlockSpec((fold * stride, depth), lambda t: (jnp.minimum(t, steps - 1), 0)),
            pl.BlockSpec((fold * stride, depth), lambda t: (jnp.maximum(t - steps, 0), 0)),
        ]
        + [tile] * len(units),
        out_specs=[pl.BlockSpec((rows, fold * depth), lambda t: (0, t))] * (count * halves)
        + [total] * (len(units) > 0),
        out_shape=[jax.ShapeDtypeStruct((rows, 2 * lines * depth), bf16)] * (count * halves)
        + [jax.ShapeDtypeStruct((1, 2 * lines * depth), f32)] * (len(units) > 0),
        cost_estimate=pl.CostEstimate(
            flops=4 * halves * tokens * inner * lines * depth,
            bytes_accessed=4 * stride * lines * depth + 4 * halves * tokens * lines * depth,
            transcendentals=0,
        ),
        name="team_product",
    )(*flat, *packs, *units)
    return [out[half * count : (half + 1) * count] for half in range(halves)] + list(out[halves * count :])


def finish_product_kernel(halves, first, units, steps, fold, stride, count, seq_ref, *refs):
    lefts = refs[:halves]
    near_ref, far_ref, out_ref = refs[halves:]
    step = pl.program_id(0)
    rows = lefts[0].shape[0] // count
    depth = near_ref.shape[1]

    def run(pack):
        for half, left in enumerate(lefts):
            for k in range(fold):
                at = k * stride + first
                total = lax.dot_general(left[...], pack[at : at + units, :], NN, preferred_element_type=f32)
                for j in range(count):
                    start = pl.multiple_of(((seq_ref[0] ^ j) * halves + half) * rows, rows)
                    out_ref[pl.ds(start, rows), k * depth : (k + 1) * depth] = total[j * rows : (j + 1) * rows].astype(bf16)

    @pl.when(step < steps)
    def _():
        run(near_ref)

    @pl.when(step >= steps)
    def _():
        run(far_ref)


def finish_product(lines, seq, lefts, span, packs, count):
    first, units = span
    tokens = lefts[0].shape[0]
    fold = 2
    stride = packs[0].shape[0] // lines
    depth = packs[0].shape[1]
    steps = lines // fold
    whole = tokens * len(lefts)
    grid_spec = pltpu.PrefetchScalarGridSpec(
        num_scalar_prefetch=1,
        grid=(2 * steps,),
        in_specs=[pl.BlockSpec(left.shape, lambda t, s: (0, 0)) for left in lefts]
        + [
            pl.BlockSpec((fold * stride, depth), lambda t, s: (jnp.minimum(t, steps - 1), 0)),
            pl.BlockSpec((fold * stride, depth), lambda t, s: (jnp.maximum(t - steps, 0), 0)),
        ],
        out_specs=pl.BlockSpec((whole, fold * depth), lambda t, s: (0, t)),
    )
    return pl.pallas_call(
        functools.partial(finish_product_kernel, len(lefts), first, units, steps, fold, stride, count),
        grid_spec=grid_spec,
        out_shape=jax.ShapeDtypeStruct((whole, 2 * lines * depth), bf16),
        cost_estimate=pl.CostEstimate(
            flops=4 * whole * units * lines * depth,
            bytes_accessed=4 * stride * lines * depth + 4 * whole * lines * depth,
            transcendentals=0,
        ),
        name="finish_product",
    )(seq, *lefts, *packs)


def cut_kernel(lines, count, *refs):
    kept, got, out_ref = refs[:count], refs[count : 2 * count], refs[2 * count]
    depth = out_ref.shape[1]
    stride = out_ref.shape[0] // lines
    first = 0
    for left, right in zip(kept, got):
        rows = left.shape[0]
        for k in range(lines):
            cols = slice(k * depth, (k + 1) * depth)
            out_ref[k * stride + first : k * stride + first + rows, :] = (
                left[:, cols].astype(f32) + right[:, cols].astype(f32)
            ).astype(bf16)
        first += rows


def line_cut(lines, kept, got):
    vmem = pl.BlockSpec(memory_space=pltpu.VMEM)
    rows = sum(left.shape[0] for left in kept)
    return pl.pallas_call(
        functools.partial(cut_kernel, lines, len(kept)),
        out_shape=jax.ShapeDtypeStruct((lines * rows, kept[0].shape[1] // lines), bf16),
        in_specs=[vmem] * (2 * len(kept)),
        out_specs=vmem,
        name="line_cut",
    )(*kept, *got)


def rms_scale(value, gain):
    return value * lax.rsqrt(jnp.mean(value * value, axis=-1, keepdims=True) + epsilon) * gain


def segment_tables(lengths_row, group_tok):
    offsets = jnp.cumsum(lengths_row) - lengths_row
    total = jnp.sum(lengths_row)
    starts = jnp.concatenate([offsets, total[None]])
    block_first = jnp.arange(group_tok // SPAN, dtype=jnp.int32) * SPAN
    reset = jnp.any(block_first[:, None] == starts[None, :], axis=1).astype(f32)
    live = (jnp.arange(group_tok, dtype=jnp.int32) < total).astype(f32)
    return reset, live


def swap(values, axis, mask):
    size = lax.axis_size(axis)
    return lax.ppermute(values, axis, [(i, i ^ mask) for i in range(size)])


def dot(left, right, dims, kind=f32):
    return lax.dot_general(left, right, dims, preferred_element_type=f32).astype(kind)


def after(values, *others):
    return lax.optimization_barrier((values, *others))[0]


def added(first, second):
    return (first.astype(f32) + second.astype(f32)).astype(bf16)


def seq_pieces(values):
    return [values] + [swap(values, "seq", k) for k in range(1, lax.axis_size("seq"))]


def seq_relayed(values, upward):
    pieces = [values]
    for k in range(1, lax.axis_size("seq")):
        hop = 1 << (k.bit_length() - 1) if upward else k & -k
        pieces.append(swap(pieces[k ^ hop], "seq", hop))
    return pieces


def twin_rows(values):
    return swap(values, "dp", 2)


def returned(chunks):
    return [chunks[0]] + [swap(chunks[j], "seq", j) for j in range(1, len(chunks))]


def summed(pieces):
    total = pieces[0].astype(f32)
    for piece in pieces[1:]:
        total = total + piece.astype(f32)
    return total


def halves_of(arrays, half):
    picked = []
    for array in arrays:
        rows = array.shape[0] // 2
        picked.append(array[half * rows : (half + 1) * rows])
    return jnp.concatenate(picked, axis=0)


def line_exchange(values):
    dp_parts = lax.axis_size("dp")
    groups = [list(range(c, dp_parts, 2)) for c in (0, 1)]
    return lax.all_to_all(values, "dp", 0, 0, tiled=True, axis_index_groups=groups)


def line_pack(arrays, lines, *others):
    both = jnp.concatenate([halves_of(arrays, 0), halves_of(arrays, 1)], axis=0)
    return line_exchange(after(jnp.concatenate([both] * (lines // 2), axis=0), *others))


def line_total(pieces, lines, spans):
    rows = pieces.shape[0] // lines
    split = [pieces[k * rows : (k + 1) * rows] for k in range(lines)]
    low = summed(split[0::2])
    high = summed(split[1::2])
    return [
        jnp.concatenate([low[first : first + n], high[first : first + n]], axis=0) for first, n in spans
    ]


def doubled(values, axis):
    size = lax.axis_size(axis)
    mask = 1
    while mask < size:
        values = values + swap(values, axis, mask)
        mask *= 2
    return values


def chip_line_sum(values):
    values = summed([values] + [swap(values, "dp", k) for k in range(2, lax.axis_size("dp"), 2)])
    return values + swap(values, "dp", 1)


def group_sum(values):
    return summed([values] + [swap(values, "seq", k) for k in range(1, lax.axis_size("seq"))])


def shards(
    tokens,
    lengths,
    cotangent,
    attn_norm_gain,
    w_query,
    w_key,
    w_value,
    w_strength,
    conv_weight,
    head_gain,
    w_output,
    ffn_norm_gain,
    w_gate,
    w_up,
    w_down,
):
    local, model = tokens.shape
    seq_parts = lax.axis_size("seq")
    seq_place = lax.axis_index("seq")
    dp_parts = lax.axis_size("dp")
    dp_place = lax.axis_index("dp")
    lines = dp_parts // 2
    group_tok = local * seq_parts
    full_width = w_query.shape[1]
    full_heads = w_strength.shape[1]
    width = full_width // 2
    heads = full_heads // 2
    extra = 16
    units = w_gate.shape[1] // 2
    side = model // 2
    per = local // SPAN
    odd = dp_place >> 1 & 1

    def scalar(value):
        return jnp.full((1,), value, jnp.int32)

    def twin(values):
        return swap(values, "dp", 1)

    core = scalar(dp_place & 1)
    place = scalar(seq_place)
    rows_f32 = jax.ShapeDtypeStruct((local, model), f32)
    rows_b16 = jax.ShapeDtypeStruct((local, model), bf16)
    gain_f32 = jax.ShapeDtypeStruct((1, model), f32)

    reset_own, live = segment_tables(lengths[0], group_tok)
    live_col = lax.dynamic_slice_in_dim(live, seq_place * local, local)[:, None]
    taps = lax.dynamic_slice_in_dim(conv_weight.astype(f32).reshape(3 * CONV, full_width), odd * width, width, 1)
    gain_h = head_gain.astype(f32)[None]
    gain_one = attn_norm_gain.astype(f32)[None]
    gain_two = ffn_norm_gain.astype(f32)[None]

    tokens_twin = twin_rows(tokens)
    reset_twin = twin_rows(jnp.concatenate([reset_own, live]))
    reset_twin, live_twin = reset_twin[: reset_own.shape[0]], reset_twin[reset_own.shape[0] :]
    live_twin_col = lax.dynamic_slice_in_dim(live_twin, seq_place * local, local)[:, None]
    hidden_own, hidden_twin = on_core(
        functools.partial(first_kernel, dp_parts), "first_norm", (rows_b16,) * 2, core, gain_one, tokens, tokens_twin
    )
    pad = jnp.zeros((extra - heads, w_strength.shape[0]), bf16)
    strength_t = w_strength.T
    strength_rows = jnp.concatenate([strength_t[:heads], pad, strength_t[heads:], pad], axis=0)
    mix_in = line_pack(
        (w_query.T, w_key.T, w_value.T, strength_rows, w_output), lines, tokens_twin, reset_twin
    )
    near_hidden = seq_relayed(hidden_own, True)
    far_hidden = seq_relayed(hidden_twin, False)
    reset = jnp.concatenate([reset_own, reset_twin])
    cot_twin = twin_rows(after(cotangent, tuple(far_hidden[:2])))
    late_cot = on_core(
        functools.partial(cot_kernel, dp_parts),
        "live_rows",
        (jax.ShapeDtypeStruct((2 * local, model), bf16),),
        core,
        cotangent,
        live_col,
        cot_twin,
        live_twin_col,
    )[0]
    mix_near = after(mix_in, tuple(near_hidden), tuple(far_hidden))
    mix_packs = (mix_near, twin(after(mix_near, late_cot)))
    o_first = 3 * width + extra

    ffn_in = line_pack((w_gate.T, w_up.T, w_down), lines, mix_packs[1])
    cots_all = lax.all_gather(after(late_cot, mix_near), "seq", axis=0, tiled=True)
    hidden_0, x_0, logit_0 = mix_product(lines, near_hidden, mix_packs, 3 * width, extra)
    hidden_1, x_1, logit_1 = mix_product(lines, far_hidden, mix_packs, 3 * width, extra)
    normed, mixed, kept = delta_forward(per, reset, place, (x_0, x_1), (logit_0, logit_1), taps, gain_h)
    o_span = ((o_first, width),)
    far_chunks, near_chunks = team_product(lines, ((normed[1],), (normed[0],)), o_span, mix_packs, seq_parts)
    far_sum = summed(returned(far_chunks)).astype(bf16)
    near_got = returned(near_chunks)
    resid, second_own = on_core(
        functools.partial(middle_kernel, dp_parts),
        "middle_norm",
        (rows_f32, rows_b16),
        core,
        tokens,
        gain_two,
        *near_got,
        twin_rows(far_sum),
    )
    second_twin = twin_rows(second_own)
    near_second = seq_pieces(second_own)
    far_second = seq_pieces(second_twin)
    ffn_near = after(ffn_in, second_own)
    ffn_packs = (ffn_near, twin(ffn_near))
    s_0, f_0, act_0, d_gate_0, d_up_0, *near_chunks = ffn_part(lines, 0, place, near_second, cots_all, ffn_packs)
    near_got = returned(near_chunks)
    far_second = after(tuple(far_second), near_chunks[0])
    s_1, f_1, act_1, d_gate_1, d_up_1, *far_chunks = ffn_part(lines, 1, place, far_second, cots_all, ffn_packs)
    acts, d_gates, d_ups, far_chunks = lax.optimization_barrier(
        ((act_0, act_1), (d_gate_0, d_gate_1), (d_up_0, d_up_1), tuple(far_chunks), tuple(near_got))
    )[:4]
    far_got = returned(far_chunks)

    def kept_sum(lefts, rights):
        def product(first, kind):
            return (
                dot(lefts[0], rights[0][:, first : first + side], TN)
                + dot(lefts[1], rights[1][:, first : first + side], TN)
            ).astype(kind)

        return product(0, bf16), product(side, bf16)

    seconds, cots = (s_0, s_1), (f_0, f_1)
    gate_kept, gate_sent = kept_sum(d_gates, seconds)
    up_kept, up_sent = kept_sum(d_ups, seconds)
    down_kept, down_sent = kept_sum(acts, cots)
    far_got = after(tuple(far_got), gate_sent, up_sent, down_sent)
    far_sum = summed(far_got).astype(bf16)
    back = twin_rows(far_sum)
    ffn_cut = line_cut(
        lines, (gate_kept, up_kept, down_kept), after((twin(gate_sent), twin(up_sent), twin(down_sent)), far_sum)
    )
    back = after(back, ffn_cut)
    d_resid, d_branch_own, grad_gain_two = on_core(
        functools.partial(back_kernel, dp_parts),
        "middle_back",
        (rows_f32, rows_b16, gain_f32),
        core,
        resid,
        gain_two,
        cotangent,
        live_col,
        *near_got,
        back,
    )
    d_branch_twin = twin_rows(d_branch_own)
    near_branch = seq_pieces(d_branch_own)
    far_branch = seq_pieces(d_branch_twin)
    ffn_back = line_exchange(after(ffn_cut, d_branch_twin))
    final = finish_product(
        lines, place, after((act_0, act_1), tuple(near_branch)), (2 * units, units), ffn_packs, seq_parts
    )
    far_pieces = tuple(far_branch)
    far_branch = after(far_pieces, final)
    b_0, d_normed_0 = branch_back(lines, after(tuple(near_branch), final), mix_packs, o_first, width)
    b_1, d_normed_1 = branch_back(lines, far_branch, mix_packs, o_first, width)
    final_sums = lax.psum_scatter(after(final, far_pieces, tuple(near_branch)), "seq", scatter_dimension=0, tiled=True)
    (d_x_0, d_x_1), d_taps, grad_head = delta_backward(
        per,
        reset,
        place,
        (x_0, x_1),
        (logit_0, logit_1),
        taps,
        gain_h,
        mixed,
        (d_normed_0, d_normed_1),
        kept,
    )
    x_span = ((0, 3 * width + extra),)
    far_chunks, near_chunks, gain_sum = team_product(
        lines, ((d_x_1,), (d_x_0,)), x_span, mix_packs, seq_parts, (hidden_1, hidden_0)
    )
    far_got = returned(far_chunks)
    near_got = returned(near_chunks)
    d_x_0, d_x_1 = after((d_x_0, d_x_1), gain_sum)
    x_kept, x_sent = kept_sum((d_x_0, d_x_1), (hidden_0, hidden_1))
    x_got = twin(x_sent)
    o_kept, o_sent = kept_sum(normed, after((b_0, b_1), x_sent))
    o_got = twin(o_sent)
    grad_gate, grad_up, grad_down = line_total(
        ffn_back, lines, ((0, units), (units, units), (2 * units, units))
    )
    by_core = gain_sum.reshape(2, lines, -1)
    by_core = jnp.where((dp_place & 1) == 1, by_core[::-1], by_core)
    grad_gain_one = by_core.transpose(1, 0, 2).reshape(1, model) / gain_one
    early = jnp.zeros((3 * CONV, model), f32)
    early = lax.dynamic_update_slice_in_dim(early, d_taps, seq_place * full_width + odd * width, 1)
    gains = jnp.concatenate([grad_gain_one, grad_gain_two, early], axis=0).reshape(-1, DH)
    gains = chip_line_sum(jnp.concatenate([gains, grad_head], axis=0))
    mix_cut = line_cut(lines, (x_kept, o_kept), after((x_got, o_got), gains, tuple(far_got), grad_gate, grad_up, grad_down))
    mix_back = line_exchange(mix_cut)
    mix_spans = (
        (0, width),
        (width, width),
        (2 * width, width),
        (3 * width, heads),
        (o_first, width),
    )
    grad_query, grad_key, grad_value, grad_strength, grad_out = line_total(mix_back, lines, mix_spans)
    far_sum = summed(after(tuple(far_got), mix_cut, tuple(near_got))).astype(bf16)
    back = twin_rows(far_sum)
    final_twin = twin_rows(after(final_sums, far_sum)[local:])
    output = on_core(
        functools.partial(finish_kernel, dp_parts),
        "finish_rows",
        (rows_b16,),
        core,
        resid,
        live_col,
        final_sums[:local],
        final_twin,
    )[0]
    back = after(back, grad_query)
    input_grad = on_core(
        functools.partial(last_kernel, dp_parts),
        "last_norm",
        (rows_f32,),
        core,
        tokens,
        gain_one,
        d_resid,
        *near_got,
        back,
    )[0]
    gains = group_sum(after(gains, far_sum))
    wide = gains[:-1].reshape(-1, model)
    conv_grad = lax.dynamic_slice_in_dim(wide[2:], seq_place * full_width, full_width, 1)
    conv_grad = conv_grad.reshape(3, CONV, full_width)
    return (
        output,
        input_grad,
        wide[0],
        grad_query.T,
        grad_key.T,
        grad_value.T,
        grad_strength.T,
        conv_grad,
        gains[-1],
        grad_out,
        wide[1],
        grad_gate.T,
        grad_up.T,
        grad_down,
    )


def solution(mesh):
    placed = (
        P(("dp", "seq"), None),
        P("dp", None),
        P(("dp", "seq"), None),
        P(),
        P("dp", "seq"),
        P("dp", "seq"),
        P("dp", "seq"),
        P("dp", "seq"),
        P(None, None, "seq"),
        P(),
        P("seq", "dp"),
        P(),
        P("dp", "seq"),
        P("dp", "seq"),
        P("seq", "dp"),
    )
    return jax.shard_map(
        shards,
        mesh=mesh,
        in_specs=placed,
        out_specs=(
            P(("dp", "seq"), None),
            P(("dp", "seq"), None),
            P(),
            P("dp", "seq"),
            P("dp", "seq"),
            P("dp", "seq"),
            P("dp", "seq"),
            P(None, None, "seq"),
            P(),
            P("seq", "dp"),
            P(),
            P("dp", "seq"),
            P("dp", "seq"),
            P("seq", "dp"),
        ),
        check_vma=False,
    )
```

```python
import functools

import jax
import jax.numpy as jnp
from jax import lax
from jax.experimental import pallas as pl
from jax.experimental.pallas import tpu as pltpu
from jax.sharding import PartitionSpec as P

DH = 128
CONV = 4
SPAN = 64
HALO = 8
epsilon = 1e-06
f32 = jnp.float32
bf16 = jnp.bfloat16

NN = (((1,), (0,)), ((), ()))
NT = (((1,), (1,)), ((), ()))
TN = (((0,), (0,)), ((), ()))


def mm(left, right, dims=NN):
    return lax.dot_general(left.astype(bf16), right.astype(bf16), dims, preferred_element_type=f32)


def mm3(left, right, dims=NN):
    lh = left.astype(bf16)
    ll = (left - lh.astype(f32)).astype(bf16)
    rh = right.astype(bf16)
    rl = (right - rh.astype(f32)).astype(bf16)
    out = lax.dot_general(ll, rh, dims, preferred_element_type=f32)
    out = out + lax.dot_general(lh, rl, dims, preferred_element_type=f32)
    return out + lax.dot_general(lh, rh, dims, preferred_element_type=f32)


def tri_masks(rows):
    r = lax.broadcasted_iota(jnp.int32, (rows, rows), 0)
    c = lax.broadcasted_iota(jnp.int32, (rows, rows), 1)
    same = (r // SPAN) == (c // SPAN)
    return r, c, same


def unit_lower_inverse(lower, r, c):
    eye = (r == c).astype(f32)
    half = 1
    inverse = eye
    while half < SPAN:
        pair = ((r // (2 * half)) == (c // (2 * half))) & ((r // half) != (c // half))
        corner = jnp.where(pair, lower, 0.0)
        if half == 1:
            inverse = eye - corner
        else:
            inverse = inverse - mm(mm(inverse, corner), inverse)
        half *= 2
    resid = eye - inverse - mm3(lower, inverse)
    return inverse + mm(inverse, resid)


def rolled(block, halo_before, lag):
    if lag == 0:
        return block
    whole = jnp.concatenate([halo_before, block], axis=0)
    return pltpu.roll(whole, lag, 0)[HALO:]


def rolled_back(block, halo_after, lag):
    if lag == 0:
        return block
    whole = jnp.concatenate([block, halo_after], axis=0)
    return pltpu.roll(whole, whole.shape[0] - lag, 0)[: block.shape[0]]


def sigmoid(v):
    return 1.0 / (1.0 + jnp.exp(-v))


def row_start(place_ref, c, per):
    chunk = lax.div(c, per)
    return pl.multiple_of(((chunk ^ place_ref[0]) * per + lax.rem(c, per)) * SPAN, SPAN)


def conv_block(x_ref, conv_ref, start, before, keep, part, head, width):
    cols = pl.ds(part * width + head * DH, DH)
    block = x_ref[pl.ds(start, SPAN), cols].astype(f32)
    halo = x_ref[pl.ds(before, 16), cols].astype(f32)[16 - HALO :] * keep
    shifted = [rolled(block, halo, lag) for lag in range(CONV)]
    taps = [conv_ref[pl.ds(part * CONV + lag, 1), pl.ds(head * DH, DH)] for lag in range(CONV)]
    total = taps[0] * shifted[0]
    for lag in range(1, CONV):
        total = total + taps[lag] * shifted[lag]
    return total, shifted, taps


def strengths(logit_refs, start, heads):
    columns = []
    for logit_ref in logit_refs:
        block = sigmoid(logit_ref[pl.ds(start, SPAN), :]).astype(bf16).astype(f32)
        columns += [block[:, h : h + 1] for h in range(heads)]
    return jnp.concatenate(columns, axis=0)


def fwd_kernel(per, groups, reset_ref, place_ref, conv_ref, gain_ref, *refs):
    x_refs, logit_refs = refs[:groups], refs[groups : 2 * groups]
    normed_refs, mixed_refs = refs[2 * groups : 3 * groups], refs[3 * groups : 4 * groups]
    t_ref, s_ref, n_ref, q_s, k_s, u_s, w_s, p_s, state = refs[4 * groups :]
    length = x_refs[0].shape[0]
    width = x_refs[0].shape[1] // 3
    heads = width // DH
    blocks = length // SPAN
    pairs = [(g, h) for g in range(groups) for h in range(heads)]
    rows = len(pairs) * SPAN
    r, c_, same = tri_masks(rows)
    strict = same & (r > c_)
    incl = same & (r >= c_)

    def local_pair(i, carry):
        return local(2 * i + 1, local(2 * i, carry))

    def local(c, carry):
        start = row_start(place_ref, c, per)
        before = pl.multiple_of(row_start(place_ref, jnp.maximum(c - 1, 0), per) + (SPAN - 16), 16)
        parts = []
        for part in range(3):
            pieces = []
            for g, h in pairs:
                keep = 1.0 - reset_ref[g * blocks + c]
                z, _, _ = conv_block(x_refs[g], conv_ref, start, before, keep, part, h, width)
                pieces.append(z)
            z = jnp.concatenate(pieces, axis=0)
            parts.append(z * sigmoid(z))
        q, k, v = parts
        q = q * lax.rsqrt(jnp.sum(q * q, axis=-1, keepdims=True) + epsilon)
        k = k * lax.rsqrt(jnp.sum(k * k, axis=-1, keepdims=True) + epsilon)
        b = strengths(logit_refs, start, heads)
        gram = mm3(k, k, NT)
        lower = jnp.where(strict, gram * b, 0.0)
        inverse = unit_lower_inverse(lower, r, c_)
        p_s[c] = jnp.where(incl, mm(q, k, NT), 0.0).astype(bf16)
        t_ref[c] = inverse.astype(bf16)
        solved = mm(inverse, jnp.concatenate([b * k, b * v], axis=1))
        w_s[c] = solved[:, :DH].astype(bf16)
        u_s[c] = solved[:, DH:]
        q_s[c] = q.astype(bf16)
        k_s[c] = k.astype(bf16)
        return carry

    lax.fori_loop(0, blocks // 2, local_pair, 0)
    state[...] = jnp.zeros_like(state)
    gain = gain_ref[...]

    def scan(c, carry):
        start = row_start(place_ref, c, per)
        news = []
        reads = []
        for at, (g, h) in enumerate(pairs):
            keep = 1.0 - reset_ref[g * blocks + c]
            here = pl.ds(at * SPAN, SPAN)
            s = state[pl.ds(at * DH, DH), :] * keep
            low = s.astype(bf16)
            s_ref[c, pl.ds(at * DH, DH), :] = low
            both = jnp.concatenate([w_s[c, here, :], q_s[c, here, :]], axis=0)
            got = mm(both, low)
            fresh = u_s[c, here, :] - got[:SPAN]
            state[pl.ds(at * DH, DH), :] = s + mm(k_s[c, here, :], fresh, TN)
            news.append(fresh)
            reads.append(got[SPAN:])
        fresh = jnp.concatenate(news, axis=0).astype(bf16)
        n_ref[c] = fresh
        out = jnp.concatenate(reads, axis=0) + mm(p_s[c], fresh)
        mixed = out.astype(bf16)
        wide = mixed.astype(f32)
        normed = (wide * lax.rsqrt(jnp.mean(wide * wide, axis=-1, keepdims=True) + epsilon) * gain).astype(bf16)
        for at, (g, h) in enumerate(pairs):
            cols = pl.ds(h * DH, DH)
            mixed_refs[g][pl.ds(start, SPAN), cols] = mixed[at * SPAN : (at + 1) * SPAN]
            normed_refs[g][pl.ds(start, SPAN), cols] = normed[at * SPAN : (at + 1) * SPAN]
        return carry

    lax.fori_loop(0, blocks, scan, 0)


def delta_forward(per, reset, place, xs, logits, conv, gain):
    groups = len(xs)
    length = xs[0].shape[0]
    width = xs[0].shape[1] // 3
    heads = groups * (width // DH)
    blocks = length // SPAN
    rows = heads * SPAN
    shape = jax.ShapeDtypeStruct
    vmem = pl.BlockSpec(memory_space=pltpu.VMEM)
    smem = pl.BlockSpec(memory_space=pltpu.SMEM)
    out = pl.pallas_call(
        functools.partial(fwd_kernel, per, groups),
        out_shape=(shape((length, width), bf16),) * (2 * groups)
        + (
            shape((blocks, rows, rows), bf16),
            shape((blocks, heads * DH, DH), bf16),
            shape((blocks, rows, DH), bf16),
        ),
        in_specs=[smem, smem] + [vmem] * (2 + 2 * groups),
        out_specs=(vmem,) * (2 * groups + 3),
        scratch_shapes=[
            pltpu.VMEM((blocks, rows, DH), bf16),
            pltpu.VMEM((blocks, rows, DH), bf16),
            pltpu.VMEM((blocks, rows, DH), f32),
            pltpu.VMEM((blocks, rows, DH), bf16),
            pltpu.VMEM((blocks, rows, rows), bf16),
            pltpu.VMEM((heads * DH, DH), f32),
        ],
        name="delta_forward",
    )(reset, place, conv, gain, *xs, *logits)
    return out[:groups], out[groups : 2 * groups], out[2 * groups :]


def bwd_kernel(per, groups, reset_ref, place_ref, conv_ref, gain_ref, *refs):
    x_refs, logit_refs = refs[:groups], refs[groups : 2 * groups]
    mixed_refs, dnorm_refs = refs[2 * groups : 3 * groups], refs[3 * groups : 4 * groups]
    t_ref, s_ref, n_ref = refs[4 * groups : 4 * groups + 3]
    dx_refs = refs[4 * groups + 3 : 5 * groups + 3]
    dconv_ref, dgain_ref, q_s, k_s, v_s, iq_s, ik_s, do_s, g_s, kt_s, ds_s, dstate = refs[5 * groups + 3 :]
    length = x_refs[0].shape[0]
    width = x_refs[0].shape[1] // 3
    heads = width // DH
    blocks = length // SPAN
    pairs = [(g, h) for g in range(groups) for h in range(heads)]
    rows = len(pairs) * SPAN
    r, c_, same = tri_masks(rows)
    strict = same & (r > c_)
    incl = same & (r >= c_)
    gain = gain_ref[...]

    def stack(some, start):
        return jnp.concatenate([some[g][pl.ds(start, SPAN), pl.ds(h * DH, DH)] for g, h in pairs], axis=0)

    def local_pair(i, total):
        return local(2 * i + 1, local(2 * i, total))

    def local(c, total):
        start = row_start(place_ref, c, per)
        before = pl.multiple_of(row_start(place_ref, jnp.maximum(c - 1, 0), per) + (SPAN - 16), 16)
        parts = []
        for part in range(3):
            pieces = []
            for g, h in pairs:
                keep = 1.0 - reset_ref[g * blocks + c]
                z, _, _ = conv_block(x_refs[g], conv_ref, start, before, keep, part, h, width)
                pieces.append(z)
            z = jnp.concatenate(pieces, axis=0)
            parts.append(z * sigmoid(z))
        q, k, v = parts
        iq = lax.rsqrt(jnp.sum(q * q, axis=-1, keepdims=True) + epsilon)
        ik = lax.rsqrt(jnp.sum(k * k, axis=-1, keepdims=True) + epsilon)
        q = q * iq
        k = k * ik
        q_s[c] = q
        k_s[c] = k
        v_s[c] = v
        iq_s[c] = jnp.broadcast_to(iq, (rows, DH))
        ik_s[c] = jnp.broadcast_to(ik, (rows, DH))
        mixed = stack(mixed_refs, start).astype(f32)
        dnorm = stack(dnorm_refs, start)
        inv = lax.rsqrt(jnp.mean(mixed * mixed, axis=-1, keepdims=True) + epsilon)
        u = mixed * inv
        total = total + jnp.sum(dnorm * u, axis=0, keepdims=True)
        dg = dnorm * gain
        do = ((dg - u * jnp.mean(dg * u, axis=-1, keepdims=True)) * inv).astype(bf16)
        do_s[c] = do
        p = jnp.where(incl, mm(q, k, NT), 0.0)
        t = t_ref[c]
        pre = mm(p, do, TN)
        got = mm(t, jnp.concatenate([pre, k], axis=1), TN)
        g_s[c] = got[:, :DH]
        kt_s[c] = got[:, DH:].astype(bf16)
        return total

    dgain_ref[...] = lax.fori_loop(0, blocks // 2, local_pair, jnp.zeros((1, DH), f32))
    dstate[...] = jnp.zeros_like(dstate)

    def scan(i, carry):
        c = blocks - 1 - i
        start = row_start(place_ref, c, per)
        b = strengths(logit_refs, start, heads)
        k = k_s[c]
        bk = (b * k).astype(bf16)
        for at, (g_, h) in enumerate(pairs):
            keep = 1.0 - reset_ref[g_ * blocks + c]
            hr = pl.ds(at * SPAN, SPAN)
            ds = dstate[pl.ds(at * DH, DH), :]
            low = ds.astype(bf16)
            ds_s[c, pl.ds(at * DH, DH), :] = low
            g = g_s[c, hr, :] + mm(kt_s[c, hr, :], low)
            g_s[c, hr, :] = g
            ql = q_s[c, hr, :].astype(bf16)
            both = jnp.concatenate([ql, bk[at * SPAN : (at + 1) * SPAN]], axis=0)
            other = jnp.concatenate([do_s[c, hr, :], (-g).astype(bf16)], axis=0)
            dstate[pl.ds(at * DH, DH), :] = (ds + mm(both, other, TN)) * keep
        return carry

    lax.fori_loop(0, blocks, scan, 0)
    dconv_ref[...] = jnp.zeros_like(dconv_ref)
    extra = dx_refs[0].shape[1] - 3 * width
    lane = lax.broadcasted_iota(jnp.int32, (SPAN, extra), 1)

    def last(i, carry):
        c = blocks - 1 - i
        start = row_start(place_ref, c, per)
        before = pl.multiple_of(row_start(place_ref, jnp.maximum(c - 1, 0), per) + (SPAN - 16), 16)
        b = strengths(logit_refs, start, heads)
        q, k, v = q_s[c], k_s[c], v_s[c]
        g, n, do = g_s[c], n_ref[c], do_s[c]
        gl = g.astype(bf16)
        both = jnp.concatenate([do, gl], axis=0)
        outer = mm(both, n, NT)
        dp = jnp.where(incl, outer[:rows], 0.0).astype(bf16)
        da = jnp.where(strict, -outer[rows:], 0.0).astype(bf16)
        down = mm(jnp.concatenate([dp, da], axis=0), k)
        up = mm(jnp.concatenate([dp, da], axis=0), jnp.concatenate([q, b * k], axis=0), TN)
        sides = []
        nds = []
        for at in range(len(pairs)):
            s = s_ref[c, pl.ds(at * DH, DH), :]
            hr = slice(at * SPAN, (at + 1) * SPAN)
            sides.append(mm(jnp.concatenate([do[hr], gl[hr]], axis=0), s, NT))
            nds.append(mm(n[hr], ds_s[c, pl.ds(at * DH, DH), :], NT))
        dos = jnp.concatenate([x[:SPAN] for x in sides], axis=0)
        gs = jnp.concatenate([x[SPAN:] for x in sides], axis=0)
        dq = dos + down[:rows]
        y = down[rows:] - gs
        dk = up + jnp.concatenate(nds, axis=0) + b * y
        dv = b * g
        db = jnp.sum(k * y + v * g, axis=-1, keepdims=True)
        dq = (dq - q * jnp.sum(q * dq, axis=-1, keepdims=True)) * iq_s[c]
        dk = (dk - k * jnp.sum(k * dk, axis=-1, keepdims=True)) * ik_s[c]
        for g_ in range(groups):
            row = jnp.zeros((SPAN, extra), f32)
            for h in range(heads):
                at = g_ * heads + h
                row = jnp.where(lane == h, db[at * SPAN : (at + 1) * SPAN], row)
            sg = sigmoid(logit_refs[g_][pl.ds(start, SPAN), :])
            dl = (row.astype(bf16).astype(f32) * sg * (1.0 - sg)).astype(bf16)
            dx_refs[g_][pl.ds(start, SPAN), pl.ds(3 * width, extra)] = dl
        new_carry = []
        for part, grad in enumerate((dq, dk, dv)):
            for at, (g_, h) in enumerate(pairs):
                keep = 1.0 - reset_ref[g_ * blocks + c]
                z, shifted, taps = conv_block(x_refs[g_], conv_ref, start, before, keep, part, h, width)
                sz = sigmoid(z)
                dz = grad[at * SPAN : (at + 1) * SPAN] * (sz * (1.0 + z * (1.0 - sz)))
                rest = carry[part * len(pairs) + at]
                total = taps[0] * dz
                for lag in range(1, CONV):
                    total = total + taps[lag] * rolled_back(dz, rest, lag)
                dx_refs[g_][pl.ds(start, SPAN), pl.ds(part * width + h * DH, DH)] = total.astype(bf16)
                for lag in range(CONV):
                    spot = pl.ds(part * CONV + lag, 1), pl.ds(h * DH, DH)
                    dconv_ref[spot] = dconv_ref[spot] + jnp.sum(dz * shifted[lag], axis=0, keepdims=True)
                new_carry.append(dz[:HALO] * keep)
        return tuple(new_carry)

    zero = jnp.zeros((HALO, DH), f32)
    lax.fori_loop(0, blocks, last, (zero,) * (3 * len(pairs)))


def delta_backward(per, reset, place, xs, logits, conv, gain, mixeds, dnorms, kept):
    groups = len(xs)
    length = xs[0].shape[0]
    width = xs[0].shape[1] // 3
    extra = logits[0].shape[1]
    heads = groups * (width // DH)
    blocks = length // SPAN
    rows = heads * SPAN
    shape = jax.ShapeDtypeStruct
    vmem = pl.BlockSpec(memory_space=pltpu.VMEM)
    smem = pl.BlockSpec(memory_space=pltpu.SMEM)
    out = pl.pallas_call(
        functools.partial(bwd_kernel, per, groups),
        out_shape=(shape((length, 3 * width + extra), bf16),) * groups
        + (shape((3 * CONV, width), f32), shape((1, DH), f32)),
        in_specs=[smem, smem] + [vmem] * (2 + 4 * groups + 3),
        out_specs=(vmem,) * (groups + 2),
        scratch_shapes=[pltpu.VMEM((blocks, rows, DH), f32)] * 5
        + [
            pltpu.VMEM((blocks, rows, DH), bf16),
            pltpu.VMEM((blocks, rows, DH), f32),
            pltpu.VMEM((blocks, rows, DH), bf16),
            pltpu.VMEM((blocks, heads * DH, DH), bf16),
            pltpu.VMEM((heads * DH, DH), f32),
        ],
        name="delta_backward",
    )(reset, place, conv, gain, *xs, *logits, *mixeds, *dnorms, *kept)
    return out[:groups], out[groups], out[groups + 1]


def slot_of(block, core, parts):
    return ((block & 1) ^ core) * (parts // 2) + block // 2


def put_columns(values, out_ref, core, parts):
    depth = values.shape[1] // parts
    for block in range(parts):
        start = pl.multiple_of(slot_of(block, core, parts) * depth, depth)
        out_ref[:, pl.ds(start, depth)] = values[:, block * depth : (block + 1) * depth]


def column_sum(pieces, core, parts):
    depth = pieces[0].shape[1] // parts
    blocks = []
    for block in range(parts):
        start = pl.multiple_of(slot_of(block, core, parts) * depth, depth)
        total = pieces[0][:, pl.ds(start, depth)].astype(f32)
        for piece in pieces[1:]:
            total = total + piece[:, pl.ds(start, depth)].astype(f32)
        blocks.append(total)
    return jnp.concatenate(blocks, axis=1)


def on_core(kernel, name, shapes, core, *arrays):
    vmem = pl.BlockSpec(memory_space=pltpu.VMEM)
    smem = pl.BlockSpec(memory_space=pltpu.SMEM)
    return pl.pallas_call(
        kernel,
        out_shape=shapes,
        in_specs=[smem] + [vmem] * len(arrays),
        out_specs=(vmem,) * len(shapes),
        name=name,
    )(core, *arrays)


def first_kernel(parts, core_ref, gain_ref, x_ref, y_ref, hidden_ref, twin_ref):
    for rows_ref, out_ref in ((x_ref, hidden_ref), (y_ref, twin_ref)):
        x = rows_ref[...].astype(f32)
        scale = lax.rsqrt(jnp.mean(x * x, axis=-1, keepdims=True) + epsilon)
        put_columns((x * scale * gain_ref[...]).astype(bf16), out_ref, core_ref[0], parts)


def cot_kernel(parts, core_ref, x_ref, live_ref, y_ref, live_twin_ref, out_ref):
    rows = x_ref.shape[0]
    put_columns((x_ref[...].astype(f32) * live_ref[...]).astype(bf16), out_ref.at[:rows], core_ref[0], parts)
    put_columns((y_ref[...].astype(f32) * live_twin_ref[...]).astype(bf16), out_ref.at[rows:], core_ref[0], parts)


def middle_kernel(parts, core_ref, x_ref, gain_ref, *refs):
    pieces, (resid_ref, second_ref) = refs[:-2], refs[-2:]
    resid = x_ref[...].astype(f32) + column_sum(pieces, core_ref[0], parts)
    resid_ref[...] = resid
    scale = lax.rsqrt(jnp.mean(resid * resid, axis=-1, keepdims=True) + epsilon)
    put_columns((resid * scale * gain_ref[...]).astype(bf16), second_ref, core_ref[0], parts)


def norm_back(base, gain, grad):
    scale = lax.rsqrt(jnp.mean(base * base, axis=-1, keepdims=True) + epsilon)
    unit = base * scale
    d_unit = grad * gain
    d_base = (d_unit - unit * jnp.mean(d_unit * unit, axis=-1, keepdims=True)) * scale
    return d_base, jnp.sum(grad * unit, axis=0, keepdims=True)


def back_kernel(parts, core_ref, resid_ref, gain_ref, cot_ref, live_ref, *refs):
    pieces, (d_resid_ref, d_branch_ref, d_gain_ref) = refs[:-3], refs[-3:]
    d_norm, d_gain_ref[...] = norm_back(resid_ref[...], gain_ref[...], column_sum(pieces, core_ref[0], parts))
    d_resid = cot_ref[...].astype(f32) * live_ref[...] + d_norm
    d_resid_ref[...] = d_resid
    put_columns(d_resid.astype(bf16), d_branch_ref, core_ref[0], parts)


def last_kernel(parts, core_ref, x_ref, gain_ref, d_resid_ref, *refs):
    pieces, grad_ref = refs[:-1], refs[-1]
    d_norm, _ = norm_back(
        x_ref[...].astype(f32), gain_ref[...], column_sum(pieces, core_ref[0], parts)
    )
    grad_ref[...] = d_resid_ref[...] + d_norm


def finish_kernel(parts, core_ref, resid_ref, live_ref, *refs):
    pieces, out_ref = refs[:-1], refs[-1]
    out_ref[...] = ((resid_ref[...] + column_sum(pieces, core_ref[0], parts)) * live_ref[...]).astype(bf16)


def row_copies(pieces, whole, sems):
    rows = pieces[0].shape[0]
    return [
        pltpu.make_async_copy(piece, whole.at[pl.ds(j * rows, rows), :], sems.at[j])
        for j, piece in enumerate(pieces)
    ]


def weight_copies(packs, whole, sems, lines, first, units):
    depth = packs[0].shape[1]
    stride = packs[0].shape[0] // lines
    copies = []
    for side, pack in enumerate(packs):
        for k in range(lines):
            start = (side * lines + k) * depth
            copies.append(
                pltpu.make_async_copy(
                    pack.at[pl.ds(k * stride + first, units), :],
                    whole.at[:, pl.ds(start, depth)],
                    sems.at[side * lines + k],
                )
            )
    return copies


def started(copies):
    for copy in copies:
        copy.start()
    return copies


def waited(copies):
    for copy in copies:
        copy.wait()


def mix_kernel(lines, count, halves, width, near, far, *refs):
    pieces, outs = refs[: halves * count], refs[halves * count : halves * count + 3 * halves]
    buf, row_sems, sems = refs[halves * count + 3 * halves :]
    weights = started(weight_copies((near, far), buf, sems, lines, 0, buf.shape[0]))
    rows = [
        started(row_copies(pieces[half * count : (half + 1) * count], outs[half], row_sems.at[half]))
        for half in range(halves)
    ]
    waited(weights)
    for half in range(halves):
        waited(rows[half])
        out = lax.dot_general(outs[half][...], buf[...], NT, preferred_element_type=f32)
        outs[halves + half][...] = out[:, :width].astype(bf16)
        outs[2 * halves + half][...] = out[:, width:]


def mix_product(lines, pieces, packs, width, extra):
    vmem = pl.BlockSpec(memory_space=pltpu.VMEM)
    hbm = pl.BlockSpec(memory_space=pl.ANY)
    halves, count = len(pieces), len(pieces[0])
    rows, model = pieces[0][0].shape
    tokens = rows * count
    shape = jax.ShapeDtypeStruct
    out = pl.pallas_call(
        functools.partial(mix_kernel, lines, count, halves, width),
        out_shape=(shape((tokens, model), bf16),) * halves
        + (shape((tokens, width), bf16),) * halves
        + (shape((tokens, extra), f32),) * halves,
        in_specs=[hbm] * (2 + halves * count),
        out_specs=(vmem,) * (3 * halves),
        scratch_shapes=[
            pltpu.VMEM((width + extra, model), bf16),
            pltpu.SemaphoreType.DMA((halves, count)),
            pltpu.SemaphoreType.DMA((2 * lines,)),
        ],
        name="mix_product",
    )(*packs, *[piece for half in pieces for piece in half])
    return out[:halves], out[halves : 2 * halves], out[2 * halves :]


def branch_kernel(lines, count, first, near, far, *refs):
    pieces, (rows_ref, out_ref, buf, row_sems, sems) = refs[:count], refs[count:]
    copies = started(row_copies(pieces, rows_ref, row_sems))
    copies += started(weight_copies((near, far), buf, sems, lines, first, buf.shape[0]))
    waited(copies)
    out_ref[...] = lax.dot_general(rows_ref[...], buf[...], NT, preferred_element_type=f32)


def branch_back(lines, pieces, packs, first, units):
    vmem = pl.BlockSpec(memory_space=pltpu.VMEM)
    smem = pl.BlockSpec(memory_space=pltpu.SMEM)
    hbm = pl.BlockSpec(memory_space=pl.ANY)
    tokens = pieces[0].shape[0] * len(pieces)
    model = pieces[0].shape[1]
    shape = jax.ShapeDtypeStruct
    return pl.pallas_call(
        functools.partial(branch_kernel, lines, len(pieces), first),
        out_shape=(shape((tokens, model), bf16), shape((tokens, units), f32)),
        in_specs=[hbm] * (2 + len(pieces)),
        out_specs=(vmem,) * 2,
        scratch_shapes=[
            pltpu.VMEM((units, model), bf16),
            pltpu.SemaphoreType.DMA((len(pieces),)),
            pltpu.SemaphoreType.DMA((2 * lines,)),
        ],
        name="branch_back",
    )(*packs, *pieces)


def ffn_kernel(lines, count, half, seq_ref, near, far, cots, *refs):
    seconds = refs[:count]
    s_ref, f_ref, act_ref, dgate_ref, dup_ref = refs[count : count + 5]
    chunk_refs, (bufs, row_sems, sems) = refs[count + 5 : 2 * count + 5], refs[2 * count + 5 :]
    rows = seconds[0].shape[0]
    units = act_ref.shape[1]
    first = started(row_copies(seconds, s_ref, row_sems.at[0]))
    weights = []
    for j in range(3):
        weights.append(
            started(weight_copies((near, far), bufs.at[j], sems.at[j], lines, j * units, units))
        )
    later = []
    for j in range(count):
        start = pl.multiple_of(((seq_ref[0] ^ j) * 2 + half) * rows, rows)
        later.append(
            pltpu.make_async_copy(
                cots.at[pl.ds(start, rows), :], f_ref.at[pl.ds(j * rows, rows), :], row_sems.at[1, j]
            )
        )
    started(later)
    waited(first + weights[0])
    gate = lax.dot_general(s_ref[...], bufs[0], NT, preferred_element_type=f32)
    waited(weights[1])
    upper = lax.dot_general(s_ref[...], bufs[1], NT, preferred_element_type=f32)
    sg = sigmoid(gate)
    soft = gate * sg
    act_ref[...] = (soft * upper).astype(bf16)
    slope = upper * (sg * (1.0 + gate * (1.0 - sg)))
    waited(later + weights[2])
    d_act = lax.dot_general(f_ref[...], bufs[2], NT, preferred_element_type=f32)
    d_gate = (d_act * slope).astype(bf16)
    d_up = (d_act * soft).astype(bf16)
    dgate_ref[...] = d_gate
    dup_ref[...] = d_up
    tile = s_ref.shape[1] // 4
    for t in range(4):
        cols = slice(t * tile, (t + 1) * tile)
        out = lax.dot_general(d_gate, bufs[0, :, cols], NN, preferred_element_type=f32)
        out = out + lax.dot_general(d_up, bufs[1, :, cols], NN, preferred_element_type=f32)
        for j, chunk in enumerate(chunk_refs):
            chunk[:, cols] = out[j * rows : (j + 1) * rows].astype(bf16)


def ffn_part(lines, half, seq, seconds, cots, packs):
    vmem = pl.BlockSpec(memory_space=pltpu.VMEM)
    smem = pl.BlockSpec(memory_space=pltpu.SMEM)
    hbm = pl.BlockSpec(memory_space=pl.ANY)
    count = len(seconds)
    tokens = seconds[0].shape[0] * count
    model = seconds[0].shape[1]
    units = packs[0].shape[0] // (3 * lines)
    shape = jax.ShapeDtypeStruct
    return pl.pallas_call(
        functools.partial(ffn_kernel, lines, count, half),
        out_shape=(shape((tokens, model), bf16),) * 2
        + (shape((tokens, units), bf16),) * 3
        + (shape((tokens // count, model), bf16),) * count,
        in_specs=[smem] + [hbm] * (3 + count),
        out_specs=(vmem,) * (5 + count),
        scratch_shapes=[
            pltpu.VMEM((3, units, model), bf16),
            pltpu.SemaphoreType.DMA((2, count)),
            pltpu.SemaphoreType.DMA((3, 2 * lines)),
        ],
        name="ffn_part",
    )(seq, *packs, cots, *seconds)


def product_kernel(halves, spans, steps, fold, stride, count, gains, *refs):
    terms = len(spans)
    lefts = refs[: halves * terms]
    near_ref, far_ref = refs[halves * terms : halves * terms + 2]
    unit_refs = refs[halves * terms + 2 : halves * terms + 2 + gains]
    outs = refs[halves * terms + 2 + gains :]
    step = pl.program_id(0)
    rows = outs[0].shape[0]
    depth = near_ref.shape[1]

    def run(pack):
        if gains:
            outs[-1][...] = jnp.zeros_like(outs[-1])
        for half in range(halves):
            for k in range(fold):
                total = None
                for left, (first, units) in zip(lefts[half * terms : (half + 1) * terms], spans):
                    at = k * stride + first
                    part = lax.dot_general(left[...], pack[at : at + units, :], NN, preferred_element_type=f32)
                    total = part if total is None else total + part
                cols = slice(k * depth, (k + 1) * depth)
                if gains:
                    unit = unit_refs[half][:, cols].astype(f32)
                    outs[-1][:, cols] = outs[-1][:, cols] + jnp.sum(total * unit, axis=0, keepdims=True)
                for j in range(count):
                    outs[half * count + j][:, cols] = total[j * rows : (j + 1) * rows].astype(bf16)

    @pl.when(step < steps)
    def _():
        run(near_ref)

    @pl.when(step >= steps)
    def _():
        run(far_ref)


def team_product(lines, lefts, spans, packs, count, units=()):
    halves = len(lefts)
    flat = [left for half in lefts for left in half]
    tokens = flat[0].shape[0]
    fold = 2
    stride = packs[0].shape[0] // lines
    depth = packs[0].shape[1]
    steps = lines // fold
    rows = tokens // count
    inner = sum(n for _, n in spans)
    tile = pl.BlockSpec((tokens, fold * depth), lambda t: (0, t))
    total = pl.BlockSpec((1, fold * depth), lambda t: (0, t))
    out = pl.pallas_call(
        functools.partial(product_kernel, halves, spans, steps, fold, stride, count, len(units)),
        grid=(2 * steps,),
        in_specs=[pl.BlockSpec(left.shape, lambda t: (0, 0)) for left in flat]
        + [
            pl.BlockSpec((fold * stride, depth), lambda t: (jnp.minimum(t, steps - 1), 0)),
            pl.BlockSpec((fold * stride, depth), lambda t: (jnp.maximum(t - steps, 0), 0)),
        ]
        + [tile] * len(units),
        out_specs=[pl.BlockSpec((rows, fold * depth), lambda t: (0, t))] * (count * halves)
        + [total] * (len(units) > 0),
        out_shape=[jax.ShapeDtypeStruct((rows, 2 * lines * depth), bf16)] * (count * halves)
        + [jax.ShapeDtypeStruct((1, 2 * lines * depth), f32)] * (len(units) > 0),
        name="team_product",
    )(*flat, *packs, *units)
    return [out[half * count : (half + 1) * count] for half in range(halves)] + list(out[halves * count :])


def finish_product_kernel(halves, first, units, steps, fold, stride, count, seq_ref, *refs):
    lefts = refs[:halves]
    near_ref, far_ref, out_ref = refs[halves:]
    step = pl.program_id(0)
    rows = lefts[0].shape[0] // count
    depth = near_ref.shape[1]

    def run(pack):
        for half, left in enumerate(lefts):
            for k in range(fold):
                at = k * stride + first
                total = lax.dot_general(left[...], pack[at : at + units, :], NN, preferred_element_type=f32)
                for j in range(count):
                    start = pl.multiple_of(((seq_ref[0] ^ j) * halves + half) * rows, rows)
                    out_ref[pl.ds(start, rows), k * depth : (k + 1) * depth] = total[j * rows : (j + 1) * rows].astype(bf16)

    @pl.when(step < steps)
    def _():
        run(near_ref)

    @pl.when(step >= steps)
    def _():
        run(far_ref)


def finish_product(lines, seq, lefts, span, packs, count):
    first, units = span
    tokens = lefts[0].shape[0]
    fold = 2
    stride = packs[0].shape[0] // lines
    depth = packs[0].shape[1]
    steps = lines // fold
    whole = tokens * len(lefts)
    grid_spec = pltpu.PrefetchScalarGridSpec(
        num_scalar_prefetch=1,
        grid=(2 * steps,),
        in_specs=[pl.BlockSpec(left.shape, lambda t, s: (0, 0)) for left in lefts]
        + [
            pl.BlockSpec((fold * stride, depth), lambda t, s: (jnp.minimum(t, steps - 1), 0)),
            pl.BlockSpec((fold * stride, depth), lambda t, s: (jnp.maximum(t - steps, 0), 0)),
        ],
        out_specs=pl.BlockSpec((whole, fold * depth), lambda t, s: (0, t)),
    )
    return pl.pallas_call(
        functools.partial(finish_product_kernel, len(lefts), first, units, steps, fold, stride, count),
        grid_spec=grid_spec,
        out_shape=jax.ShapeDtypeStruct((whole, 2 * lines * depth), bf16),
        name="finish_product",
    )(seq, *lefts, *packs)


def cut_kernel(lines, count, *refs):
    kept, got, out_ref = refs[:count], refs[count : 2 * count], refs[2 * count]
    depth = out_ref.shape[1]
    stride = out_ref.shape[0] // lines
    first = 0
    for left, right in zip(kept, got):
        rows = left.shape[0]
        for k in range(lines):
            cols = slice(k * depth, (k + 1) * depth)
            out_ref[k * stride + first : k * stride + first + rows, :] = (
                left[:, cols].astype(f32) + right[:, cols].astype(f32)
            ).astype(bf16)
        first += rows


def line_cut(lines, kept, got):
    vmem = pl.BlockSpec(memory_space=pltpu.VMEM)
    rows = sum(left.shape[0] for left in kept)
    return pl.pallas_call(
        functools.partial(cut_kernel, lines, len(kept)),
        out_shape=jax.ShapeDtypeStruct((lines * rows, kept[0].shape[1] // lines), bf16),
        in_specs=[vmem] * (2 * len(kept)),
        out_specs=vmem,
        name="line_cut",
    )(*kept, *got)


def rms_scale(value, gain):
    return value * lax.rsqrt(jnp.mean(value * value, axis=-1, keepdims=True) + epsilon) * gain


def segment_tables(lengths_row, group_tok):
    offsets = jnp.cumsum(lengths_row) - lengths_row
    total = jnp.sum(lengths_row)
    starts = jnp.concatenate([offsets, total[None]])
    block_first = jnp.arange(group_tok // SPAN, dtype=jnp.int32) * SPAN
    reset = jnp.any(block_first[:, None] == starts[None, :], axis=1).astype(f32)
    live = (jnp.arange(group_tok, dtype=jnp.int32) < total).astype(f32)
    return reset, live


def swap(values, axis, mask):
    size = lax.axis_size(axis)
    return lax.ppermute(values, axis, [(i, i ^ mask) for i in range(size)])


def dot(left, right, dims, kind=f32):
    return lax.dot_general(left, right, dims, preferred_element_type=f32).astype(kind)


def after(values, *others):
    return lax.optimization_barrier((values, *others))[0]


def added(first, second):
    return (first.astype(f32) + second.astype(f32)).astype(bf16)


def seq_pieces(values):
    return [values] + [swap(values, "seq", k) for k in range(1, lax.axis_size("seq"))]


def seq_relayed(values, upward):
    pieces = [values]
    for k in range(1, lax.axis_size("seq")):
        hop = 1 << (k.bit_length() - 1) if upward else k & -k
        pieces.append(swap(pieces[k ^ hop], "seq", hop))
    return pieces


def twin_rows(values):
    return swap(values, "dp", 2)


def returned(chunks):
    return [chunks[0]] + [swap(chunks[j], "seq", j) for j in range(1, len(chunks))]


def summed(pieces):
    total = pieces[0].astype(f32)
    for piece in pieces[1:]:
        total = total + piece.astype(f32)
    return total


def halves_of(arrays, half):
    picked = []
    for array in arrays:
        rows = array.shape[0] // 2
        picked.append(array[half * rows : (half + 1) * rows])
    return jnp.concatenate(picked, axis=0)


def line_exchange(values):
    dp_parts = lax.axis_size("dp")
    groups = [list(range(c, dp_parts, 2)) for c in (0, 1)]
    return lax.all_to_all(values, "dp", 0, 0, tiled=True, axis_index_groups=groups)


def line_pack(arrays, lines, *others):
    both = jnp.concatenate([halves_of(arrays, 0), halves_of(arrays, 1)], axis=0)
    return line_exchange(after(jnp.concatenate([both] * (lines // 2), axis=0), *others))


def line_total(pieces, lines, spans):
    rows = pieces.shape[0] // lines
    split = [pieces[k * rows : (k + 1) * rows] for k in range(lines)]
    low = summed(split[0::2])
    high = summed(split[1::2])
    return [
        jnp.concatenate([low[first : first + n], high[first : first + n]], axis=0) for first, n in spans
    ]


def doubled(values, axis):
    size = lax.axis_size(axis)
    mask = 1
    while mask < size:
        values = values + swap(values, axis, mask)
        mask *= 2
    return values


def chip_line_sum(values):
    values = summed([values] + [swap(values, "dp", k) for k in range(2, lax.axis_size("dp"), 2)])
    return values + swap(values, "dp", 1)


def group_sum(values):
    return summed([values] + [swap(values, "seq", k) for k in range(1, lax.axis_size("seq"))])


def shards(
    tokens,
    lengths,
    cotangent,
    attn_norm_gain,
    w_query,
    w_key,
    w_value,
    w_strength,
    conv_weight,
    head_gain,
    w_output,
    ffn_norm_gain,
    w_gate,
    w_up,
    w_down,
):
    local, model = tokens.shape
    seq_parts = lax.axis_size("seq")
    seq_place = lax.axis_index("seq")
    dp_parts = lax.axis_size("dp")
    dp_place = lax.axis_index("dp")
    lines = dp_parts // 2
    group_tok = local * seq_parts
    full_width = w_query.shape[1]
    full_heads = w_strength.shape[1]
    width = full_width // 2
    heads = full_heads // 2
    extra = 16
    units = w_gate.shape[1] // 2
    side = model // 2
    per = local // SPAN
    odd = dp_place >> 1 & 1

    def scalar(value):
        return jnp.full((1,), value, jnp.int32)

    def twin(values):
        return swap(values, "dp", 1)

    core = scalar(dp_place & 1)
    place = scalar(seq_place)
    rows_f32 = jax.ShapeDtypeStruct((local, model), f32)
    rows_b16 = jax.ShapeDtypeStruct((local, model), bf16)
    gain_f32 = jax.ShapeDtypeStruct((1, model), f32)

    reset_own, live = segment_tables(lengths[0], group_tok)
    live_col = lax.dynamic_slice_in_dim(live, seq_place * local, local)[:, None]
    taps = lax.dynamic_slice_in_dim(conv_weight.astype(f32).reshape(3 * CONV, full_width), odd * width, width, 1)
    gain_h = head_gain.astype(f32)[None]
    gain_one = attn_norm_gain.astype(f32)[None]
    gain_two = ffn_norm_gain.astype(f32)[None]

    tokens_twin = twin_rows(tokens)
    reset_twin = twin_rows(jnp.concatenate([reset_own, live]))
    reset_twin, live_twin = reset_twin[: reset_own.shape[0]], reset_twin[reset_own.shape[0] :]
    live_twin_col = lax.dynamic_slice_in_dim(live_twin, seq_place * local, local)[:, None]
    hidden_own, hidden_twin = on_core(
        functools.partial(first_kernel, dp_parts), "first_norm", (rows_b16,) * 2, core, gain_one, tokens, tokens_twin
    )
    pad = jnp.zeros((extra - heads, w_strength.shape[0]), bf16)
    strength_t = w_strength.T
    strength_rows = jnp.concatenate([strength_t[:heads], pad, strength_t[heads:], pad], axis=0)
    mix_in = line_pack(
        (w_query.T, w_key.T, w_value.T, strength_rows, w_output), lines, tokens_twin, reset_twin
    )
    near_hidden = seq_relayed(hidden_own, True)
    far_hidden = seq_relayed(hidden_twin, False)
    reset = jnp.concatenate([reset_own, reset_twin])
    cot_twin = twin_rows(after(cotangent, tuple(far_hidden[:2])))
    late_cot = on_core(
        functools.partial(cot_kernel, dp_parts),
        "live_rows",
        (jax.ShapeDtypeStruct((2 * local, model), bf16),),
        core,
        cotangent,
        live_col,
        cot_twin,
        live_twin_col,
    )[0]
    mix_near = after(mix_in, tuple(near_hidden), tuple(far_hidden))
    mix_packs = (mix_near, twin(after(mix_near, late_cot)))
    o_first = 3 * width + extra

    ffn_in = line_pack((w_gate.T, w_up.T, w_down), lines, mix_packs[1])
    cots_all = lax.all_gather(after(late_cot, mix_near), "seq", axis=0, tiled=True)
    (hidden_0, hidden_1), (x_0, x_1), (logit_0, logit_1) = mix_product(
        lines, (near_hidden, far_hidden), mix_packs, 3 * width, extra
    )
    normed, mixed, kept = delta_forward(per, reset, place, (x_0, x_1), (logit_0, logit_1), taps, gain_h)
    o_span = ((o_first, width),)
    far_chunks, near_chunks = team_product(lines, ((normed[1],), (normed[0],)), o_span, mix_packs, seq_parts)
    far_sum = summed(returned(far_chunks)).astype(bf16)
    near_got = returned(near_chunks)
    resid, second_own = on_core(
        functools.partial(middle_kernel, dp_parts),
        "middle_norm",
        (rows_f32, rows_b16),
        core,
        tokens,
        gain_two,
        *near_got,
        twin_rows(far_sum),
    )
    second_twin = twin_rows(second_own)
    near_second = seq_pieces(second_own)
    far_second = seq_pieces(second_twin)
    ffn_near = after(ffn_in, second_own)
    ffn_packs = (ffn_near, twin(ffn_near))
    s_0, f_0, act_0, d_gate_0, d_up_0, *near_chunks = ffn_part(lines, 0, place, near_second, cots_all, ffn_packs)
    near_got = returned(near_chunks)
    far_second = after(tuple(far_second), near_chunks[0])
    s_1, f_1, act_1, d_gate_1, d_up_1, *far_chunks = ffn_part(lines, 1, place, far_second, cots_all, ffn_packs)
    acts, d_gates, d_ups, far_chunks = lax.optimization_barrier(
        ((act_0, act_1), (d_gate_0, d_gate_1), (d_up_0, d_up_1), tuple(far_chunks), tuple(near_got))
    )[:4]
    far_got = returned(far_chunks)

    def kept_sum(lefts, rights):
        def product(first, kind):
            return (
                dot(lefts[0], rights[0][:, first : first + side], TN)
                + dot(lefts[1], rights[1][:, first : first + side], TN)
            ).astype(kind)

        return product(0, bf16), product(side, bf16)

    seconds, cots = (s_0, s_1), (f_0, f_1)
    gate_kept, gate_sent = kept_sum(d_gates, seconds)
    up_kept, up_sent = kept_sum(d_ups, seconds)
    down_kept, down_sent = kept_sum(acts, cots)
    far_got = after(tuple(far_got), gate_sent, up_sent, down_sent)
    far_sum = summed(far_got).astype(bf16)
    back = twin_rows(far_sum)
    ffn_cut = line_cut(
        lines, (gate_kept, up_kept, down_kept), after((twin(gate_sent), twin(up_sent), twin(down_sent)), far_sum)
    )
    back = after(back, ffn_cut)
    d_resid, d_branch_own, grad_gain_two = on_core(
        functools.partial(back_kernel, dp_parts),
        "middle_back",
        (rows_f32, rows_b16, gain_f32),
        core,
        resid,
        gain_two,
        cotangent,
        live_col,
        *near_got,
        back,
    )
    d_branch_twin = twin_rows(d_branch_own)
    near_branch = seq_pieces(d_branch_own)
    far_branch = seq_pieces(d_branch_twin)
    ffn_back = line_exchange(after(ffn_cut, d_branch_twin))
    final = finish_product(
        lines, place, after((act_0, act_1), tuple(near_branch)), (2 * units, units), ffn_packs, seq_parts
    )
    far_pieces = tuple(far_branch)
    far_branch = after(far_pieces, final)
    b_0, d_normed_0 = branch_back(lines, after(tuple(near_branch), final), mix_packs, o_first, width)
    b_1, d_normed_1 = branch_back(lines, far_branch, mix_packs, o_first, width)
    final_sums = lax.psum_scatter(after(final, far_pieces, tuple(near_branch)), "seq", scatter_dimension=0, tiled=True)
    (d_x_0, d_x_1), d_taps, grad_head = delta_backward(
        per,
        reset,
        place,
        (x_0, x_1),
        (logit_0, logit_1),
        taps,
        gain_h,
        mixed,
        (d_normed_0, d_normed_1),
        kept,
    )
    x_span = ((0, 3 * width + extra),)
    far_chunks, near_chunks, gain_sum = team_product(
        lines, ((d_x_1,), (d_x_0,)), x_span, mix_packs, seq_parts, (hidden_1, hidden_0)
    )
    far_got = returned(far_chunks)
    near_got = returned(near_chunks)
    d_x_0, d_x_1 = after((d_x_0, d_x_1), gain_sum)
    x_kept, x_sent = kept_sum((d_x_0, d_x_1), (hidden_0, hidden_1))
    x_got = twin(x_sent)
    o_kept, o_sent = kept_sum(normed, after((b_0, b_1), x_sent))
    o_got = twin(o_sent)
    grad_gate, grad_up, grad_down = line_total(
        ffn_back, lines, ((0, units), (units, units), (2 * units, units))
    )
    by_core = gain_sum.reshape(2, lines, -1)
    by_core = jnp.where((dp_place & 1) == 1, by_core[::-1], by_core)
    grad_gain_one = by_core.transpose(1, 0, 2).reshape(1, model) / gain_one
    early = jnp.zeros((3 * CONV, model), f32)
    early = lax.dynamic_update_slice_in_dim(early, d_taps, seq_place * full_width + odd * width, 1)
    gains = jnp.concatenate([grad_gain_one, grad_gain_two, early], axis=0).reshape(-1, DH)
    gains = chip_line_sum(jnp.concatenate([gains, grad_head], axis=0))
    mix_cut = line_cut(lines, (x_kept, o_kept), after((x_got, o_got), gains, tuple(far_got[:3]), grad_gate, grad_up, grad_down))
    mix_back = line_exchange(mix_cut)
    mix_spans = (
        (0, width),
        (width, width),
        (2 * width, width),
        (3 * width, heads),
        (o_first, width),
    )
    grad_query, grad_key, grad_value, grad_strength, grad_out = line_total(mix_back, lines, mix_spans)
    far_sum = summed(after(tuple(far_got), mix_cut, tuple(near_got))).astype(bf16)
    back = twin_rows(far_sum)
    final_twin = twin_rows(after(final_sums, far_sum)[local:])
    output = on_core(
        functools.partial(finish_kernel, dp_parts),
        "finish_rows",
        (rows_b16,),
        core,
        resid,
        live_col,
        final_sums[:local],
        final_twin,
    )[0]
    back = after(back, grad_query)
    input_grad = on_core(
        functools.partial(last_kernel, dp_parts),
        "last_norm",
        (rows_f32,),
        core,
        tokens,
        gain_one,
        d_resid,
        *near_got,
        back,
    )[0]
    gains = group_sum(after(gains, far_sum))
    wide = gains[:-1].reshape(-1, model)
    conv_grad = lax.dynamic_slice_in_dim(wide[2:], seq_place * full_width, full_width, 1)
    conv_grad = conv_grad.reshape(3, CONV, full_width)
    return (
        output,
        input_grad,
        wide[0],
        grad_query.T,
        grad_key.T,
        grad_value.T,
        grad_strength.T,
        conv_grad,
        gains[-1],
        grad_out,
        wide[1],
        grad_gate.T,
        grad_up.T,
        grad_down,
    )


def solution(mesh):
    placed = (
        P(("dp", "seq"), None),
        P("dp", None),
        P(("dp", "seq"), None),
        P(),
        P("dp", "seq"),
        P("dp", "seq"),
        P("dp", "seq"),
        P("dp", "seq"),
        P(None, None, "seq"),
        P(),
        P("seq", "dp"),
        P(),
        P("dp", "seq"),
        P("dp", "seq"),
        P("seq", "dp"),
    )
    return jax.shard_map(
        shards,
        mesh=mesh,
        in_specs=placed,
        out_specs=(
            P(("dp", "seq"), None),
            P(("dp", "seq"), None),
            P(),
            P("dp", "seq"),
            P("dp", "seq"),
            P("dp", "seq"),
            P("dp", "seq"),
            P(None, None, "seq"),
            P(),
            P("seq", "dp"),
            P(),
            P("dp", "seq"),
            P("dp", "seq"),
            P("seq", "dp"),
        ),
        check_vma=False,
    )
```
